32 devices in a mesh: dp: 4 (over z), heads: 4 (over x, core), tensor: 2 (over y).
Axes of the slice: x: 2, y: 2, z: 4, core: 2. Of those that a mesh axis runs over, the one named last changes fastest.
Arguments:
- inputs: bfloat16 [6304, 768], P(('dp', 'heads', 'tensor')), may hold values from -6 to 6
- first_gain: bfloat16 [768], replicated, may hold values from 0.099609375 to 1.8984375
- first_bias: bfloat16 [768], replicated, may hold values from -2.5 to 2.5
- head_weight: bfloat16 [3, 768, 768], P(None, ('dp', 'tensor'), 'heads'), may hold values from -0.21875 to 0.21875
- head_bias: bfloat16 [2, 768], P(None, ('heads', 'dp', 'tensor')), may hold values from -2.5 to 2.5
- merge_weight: bfloat16 [768, 768], P('heads', ('dp', 'tensor')), may hold values from -0.625 to 0.625
- merge_bias: bfloat16 [768], replicated, may hold values from -2.5 to 2.5
- second_gain: bfloat16 [768], replicated, may hold values from 0.099609375 to 1.8984375
- second_bias: bfloat16 [768], replicated, may hold values from -2.5 to 2.5
- router: bfloat16 [768, 4], replicated, may hold values from -0.15625 to 0.15625
- router_noise: float32 [6304, 4], P(('dp', 'heads', 'tensor')), may hold values from -4 to 4
- expert_ids: int32 [6304, 2], P(('dp', 'heads', 'tensor')), may hold values from 0 to 3, all different within a row; in each aligned block of 197 rows (0 to 196, 197 to 393, ...) at most 128 rows name the same one
- expert_in: bfloat16 [4, 768, 3072], P(None, ('dp', 'heads'), 'tensor'), may hold values from -0.21875 to 0.21875
- expert_in_bias: bfloat16 [4, 3072], P(None, ('tensor', 'dp', 'heads')), may hold values from -2.5 to 2.5
- expert_out: bfloat16 [4, 3072, 768], P(None, 'tensor', ('dp', 'heads')), may hold values from -0.3125 to 0.3125
- expert_out_bias: bfloat16 [4, 768], replicated, may hold values from -2.5 to 2.5
- cotangent: bfloat16 [6304, 768], P(('dp', 'heads', 'tensor')), may hold values from -6 to 6
Outputs:
- output: float32 [6304, 768], P(('dp', 'heads', 'tensor'))
- balance_loss: float32 [], replicated
- input_grad: float32 [6304, 768], P(('dp', 'heads', 'tensor'))
- first_gain_grad: float32 [768], replicated
- first_bias_grad: float32 [768], replicated
- head_weight_grad: float32 [3, 768, 768], P(None, ('dp', 'tensor'), 'heads')
- head_bias_grad: float32 [2, 768], P(None, ('heads', 'dp', 'tensor'))
- merge_weight_grad: float32 [768, 768], P('heads', ('dp', 'tensor'))
- merge_bias_grad: float32 [768], replicated
- second_gain_grad: float32 [768], replicated
- second_bias_grad: float32 [768], replicated
- router_grad: float32 [768, 4], replicated
- expert_in_grad: float32 [4, 768, 3072], P(None, ('dp', 'heads'), 'tensor')
- expert_in_bias_grad: float32 [4, 3072], P(None, ('tensor', 'dp', 'heads'))
- expert_out_grad: float32 [4, 3072, 768], P(None, 'tensor', ('dp', 'heads'))
- expert_out_bias_grad: float32 [4, 768], replicated
The draws below stay inside these ranges and needn't reach their ends.
Inputs may be any that keep to these rules, and one draw needn't show every extreme that they name: `expert_ids`: each row names two different experts; in the rows of one device no expert is named by more than 128 rows, and in some device's rows an expert is named by exactly 128 rows.
All inputs are finite; a program needn't handle non-finite values.
Results may differ from the reference program's by a relative error of at most 0.025.
Values may be sent and summed in bfloat16 or wider, within the bound.
A program may use at most 192 MiB of HBM per device.

```python
import math
import jax
import jax.numpy as jnp
import numpy as np
from jax import lax

D = 768
HEADS = 12
HEAD_DIM = 64
FF = 3072
E = 4
SEQ = 197
IMG_DEV = 1
TOK_DEV = 197
CAP = 128
TOKENS = 6304
N_HEADS = 4


def draw_router_noise(key, part):
    jitter_key = jax.random.fold_in(key, 11)
    tilt_key = jax.random.fold_in(key, 12)
    jitter = jnp.clip(jax.random.normal(jitter_key, (TOKENS, E), jnp.float32), -4.0, 4.0)
    tilt_rate = jnp.clip(jax.random.normal(tilt_key, (E,), jnp.float32), -2.0, 2.0)
    position = jnp.arange(TOKENS, dtype=jnp.float32) / TOKENS
    return 0.5 * jitter + position[:, None] * tilt_rate[None, :]


def raised(entries, own_key, source, target, shards_of, factor):
    owner, partner = [(jnp.arange(entries.shape[dim]) // (entries.shape[dim] // shards_of)).reshape([-1 if axis == dim else 1 for axis in range(entries.ndim)]) for dim in (source, target)]
    chosen = jax.random.permutation(own_key, shards_of)[partner]
    strong = (owner == chosen) | (owner == (partner + shards_of // 2) % shards_of)
    return jnp.where(strong, factor * entries, entries)


def steps_of(own_key, dims, pieces, smallest, high):
    gain, own = 1.0, jax.random.fold_in(own_key, 6)
    for dim, shards_of in pieces:
        draws = jnp.exp(jax.random.uniform(jax.random.fold_in(own, dim), (shards_of,), jnp.float32, smallest / len(pieces), high / len(pieces)))
        gain = gain * jnp.repeat(draws, dims[dim] // shards_of).reshape([-1 if axis == dim else 1 for axis in range(len(dims))])
    return gain


def routed_block(rng, own, number, rows, number_of, top, reach, slope):
    sequence = jax.random.permutation(rng, number_of)
    crowded, common = portions_of(number_of, rows * top, reach, slope, True), portions_of(number_of, rows * top, reach, slope, False)
    places = jnp.arange(number_of)

    def named(lengths, turn):
        used = int((lengths > 0).sum())
        fixed = max(1, used // 4)
        passed = fixed + (places - fixed + turn * (used - fixed)) % max(1, number_of - fixed)
        return jnp.zeros((number_of,), jnp.int32).at[sequence[jnp.where(places < fixed, places, passed)]].set(jnp.asarray(lengths, jnp.int32))

    lengths = jnp.where(number % 4 == 0, named(crowded, number // 4), named(common, number - number // 4 - 1))
    mixed = jax.random.permutation(jax.random.fold_in(own, 3), number_of)
    donor, receiver = mixed[0:number_of // 2 * 2:2], mixed[1:number_of // 2 * 2:2]
    margin = jnp.minimum(lengths[donor] - 1, reach - lengths[receiver]) // 2
    margin = jnp.where((donor == sequence[0]) | (receiver == sequence[0]) | (lengths[receiver] == 0), 0, jnp.maximum(margin, 0))
    passed = jax.random.randint(jax.random.fold_in(own, 4), (number_of // 2,), 0, 1 << 20) % (margin + 1)
    lengths = lengths.at[donor].add(-passed).at[receiver].add(passed)
    members = jnp.searchsorted(jnp.cumsum(lengths), jnp.arange(rows * top), side="right").astype(jnp.int32)
    table = members.reshape(top, rows).T
    table = table[jax.random.permutation(jax.random.fold_in(own, 1), rows)]
    turn = jax.random.randint(jax.random.fold_in(own, 2), (rows, 1), 0, top)
    return jnp.take_along_axis(table, (jnp.arange(top)[None, :] + turn) % top, axis=1)


def portions_of(count, total, bound, skew, full):
    loads = [(1 << 20) // math.isqrt(rank ** skew) + 1 for rank in range(1, count + 1)]
    largest = bound if full else min(bound, max(-(-total // count), total * loads[0] // sum(loads)))
    least = 1 if total - largest >= count - 1 else 0
    holding, rest = [largest] + [least] * (count - 1), total - largest - least * (count - 1)
    while rest > 0:
        candidates = [i for i in range(1, count) if holding[i] < largest] or [i for i in range(1, count) if holding[i] < bound]
        whole, remaining = sum([loads[i] for i in candidates]), rest
        for i in candidates:
            more = min(bound - holding[i], max(1, remaining * loads[i] // whole), rest)
            holding[i] = holding[i] + more
            rest = rest - more
    return np.array(holding)


def gaussian(key, dims, scale, limit, pieces=(), held_as=jnp.bfloat16):
    drawn = scale * jax.random.normal(key, dims, jnp.float32)
    if pieces:
        drawn = drawn * steps_of(key, dims, pieces, -0.22, 0.18)
    return jnp.clip(drawn, -limit, limit).astype(held_as)


def bell_draw_with(rng, dims, deviation, limit, pieces, heavy, held_as=jnp.bfloat16):
    result = deviation * jax.random.normal(rng, dims, jnp.float32)
    if pieces:
        result = result * steps_of(rng, dims, pieces, -0.22, 0.18)
    return jnp.clip(raised(result, jax.random.fold_in(rng, 3), *heavy), -limit, limit).astype(held_as)


def setup_inputs(seed: int = 0) -> dict:
    streams_of = jax.random.split(jax.random.key(seed), 18)
    inputs = gaussian(streams_of[0], (TOKENS, D), 1.0, 6.0, ((0, 32),))
    first_gain = jnp.clip(1.0 + 0.18 * jax.random.normal(streams_of[1], (D,), jnp.float32), 0.099609375, 1.8984375).astype(jnp.bfloat16)
    first_bias = gaussian(streams_of[2], (D,), 0.2, 2.5)
    head_weight = gaussian(streams_of[3], (3, D, D), D ** -0.5, 0.21875, ((1, 8), (2, 4)))
    head_bias = gaussian(streams_of[4], (2, D), 0.2, 2.5, ((1, 32),))
    merge_weight = gaussian(streams_of[5], (D, D), (D // 8) ** -0.5, 0.625, ((0, 4), (1, 8)))
    merge_bias = gaussian(streams_of[6], (D,), 0.2, 2.5)
    second_gain = jnp.clip(1.0 + 0.18 * jax.random.normal(streams_of[7], (D,), jnp.float32), 0.099609375, 1.8984375).astype(jnp.bfloat16)
    second_bias = gaussian(streams_of[8], (D,), 0.2, 2.5)
    router = gaussian(streams_of[9], (D, E), (2 * D) ** -0.5, 0.15625)
    router_noise = draw_router_noise(jax.random.fold_in(streams_of[17], 71), 0)
    expert_ids_keys = jax.random.split(jax.random.fold_in(streams_of[11], 1), TOKENS // TOK_DEV)
    expert_ids_turns = jax.random.permutation(jax.random.fold_in(streams_of[11], 3), TOKENS // TOK_DEV)
    expert_ids = jax.vmap(lambda own, number: routed_block(jax.random.fold_in(streams_of[11], 2), own, number, TOK_DEV, E, 2, CAP, 0))(expert_ids_keys, expert_ids_turns).reshape((TOKENS, 2))
    expert_in = gaussian(streams_of[12], (E, D, FF), D ** -0.5, 0.21875, ((1, 16), (2, 2)))
    expert_in_bias = gaussian(streams_of[13], (E, FF), 0.2, 2.5, ((1, 32),))
    expert_out = gaussian(streams_of[14], (E, FF, D), (FF // 8) ** -0.5, 0.3125, ((1, 2), (2, 16)))
    expert_out_bias = gaussian(streams_of[15], (E, D), 0.2, 2.5)
    cotangent = bell_draw_with(streams_of[16], (TOKENS, D), 1.0, 6.0, ((0, 32),), (0, 1, 32, 2.75))
    return dict(inputs=inputs, first_gain=first_gain, first_bias=first_bias, head_weight=head_weight, head_bias=head_bias, merge_weight=merge_weight, merge_bias=merge_bias, second_gain=second_gain, second_bias=second_bias, router=router, router_noise=router_noise, expert_ids=expert_ids, expert_in=expert_in, expert_in_bias=expert_in_bias, expert_out=expert_out, expert_out_bias=expert_out_bias, cotangent=cotangent)


HIGHEST = lax.Precision.HIGHEST

@jax.custom_vjp
def low(v):
    return lax.optimization_barrier(v.astype(jnp.bfloat16)).astype(jnp.float32)

@jax.custom_vjp
def low_back(v):
    return v

def low_keep(v):
    return (low(v), None)

def low_pass(kept, grad):
    return (grad,)

def back_keep(v):
    return (v, None)

def back_low(kept, grad):
    return (low(grad),)
low.defvjp(low_keep, low_pass)
low_back.defvjp(back_keep, back_low)

def layer_norm(values, factor, offset):
    average = lax.optimization_barrier(jnp.mean(values, axis=-1, keepdims=True))
    centred = values - average
    spread = lax.optimization_barrier(jnp.mean(centred * centred, axis=-1, keepdims=True))
    return centred * lax.rsqrt(spread + 1e-06) * factor + offset

def expert_rows(expert_ids):
    blocks = TOKENS // TOK_DEV
    grouped = expert_ids.reshape(blocks, TOK_DEV, 2)
    chosen = lax.optimization_barrier(jnp.sum((grouped[..., None] == jnp.arange(E, dtype=jnp.int32)).astype(jnp.int32), axis=2))
    before = jnp.cumsum(chosen, axis=1) - chosen
    slot_ids = jnp.take_along_axis(before, grouped, axis=2)
    block_start = (jnp.arange(blocks, dtype=jnp.int32) * (E * CAP))[:, None, None]
    return (block_start + grouped * CAP + slot_ids).reshape(TOKENS, 2).astype(jnp.int32)

def attend_block(triple):
    queries, key_rows, value_rows = triple
    scores = low_back(HEAD_DIM ** (-0.5) * jnp.einsum('ishd,ithd->ihst', queries, key_rows, precision=HIGHEST))
    weights = low(jax.nn.softmax(scores, axis=-1))
    return low(low_back(jnp.einsum('ihst,ithd->ishd', weights, value_rows, precision=HIGHEST)))

def run_expert(packed):
    slot_rows, weight_in, bias_in, weight_out, bias_out = packed
    hidden = low(jax.nn.gelu(low_back(jnp.dot(slot_rows, weight_in, precision=HIGHEST) + bias_in)))
    return low_back(jnp.dot(hidden, weight_out, precision=HIGHEST) + bias_out)

def forward(inputs, first_gain, first_bias, head_weight, head_bias, merge_weight, merge_bias, second_gain, second_bias, router, expert_in, expert_in_bias, expert_out, expert_out_bias, router_noise, expert_ids, flat_rows, counts):
    normed = low(layer_norm(inputs, first_gain, first_bias))
    projected = jnp.einsum('td,jdc->jtc', normed, head_weight, precision=HIGHEST)
    queries = low(low_back(projected[0] + head_bias[0]))
    key_rows = low(low_back(projected[1]))
    value_rows = low(low_back(projected[2] + head_bias[1]))
    per_step = IMG_DEV * N_HEADS
    steps_count = TOKENS // (SEQ * per_step)

    def shaped(array):
        return array.reshape(steps_count, per_step, SEQ, HEADS, HEAD_DIM)
    attended = lax.map(jax.checkpoint(attend_block), (shaped(queries), shaped(key_rows), shaped(value_rows)))
    branch = low_back(jnp.dot(attended.reshape(TOKENS, D), merge_weight, precision=HIGHEST) + merge_bias)
    residual = inputs + branch
    normed_two = low(layer_norm(residual, second_gain, second_bias))
    logits = low_back(jnp.dot(normed_two, router, precision=HIGHEST)) + router_noise
    chances = jax.nn.softmax(logits, axis=-1)
    blocks = TOKENS // TOK_DEV
    buffers = jnp.zeros((blocks * E * CAP, D), jnp.float32).at[flat_rows.reshape(-1)].set(jnp.repeat(normed_two, 2, axis=0))
    by_expert = buffers.reshape(blocks, E, CAP, D).transpose(1, 0, 2, 3).reshape(E, blocks * CAP, D)
    results = lax.map(jax.checkpoint(run_expert), (by_expert, expert_in, expert_in_bias, expert_out, expert_out_bias))
    results = results.reshape(E, blocks, CAP, D).transpose(1, 0, 2, 3).reshape(blocks * E * CAP, D)
    picked = results[flat_rows]
    gate_values = jnp.take_along_axis(chances, expert_ids, axis=1)
    output = residual + lax.optimization_barrier(jnp.sum(gate_values[:, :, None] * picked, axis=1))
    balance = E * jnp.sum(counts / (2 * TOKENS) * lax.optimization_barrier(jnp.mean(chances, axis=0)))
    return (output, balance)

def reference(inputs, first_gain, first_bias, head_weight, head_bias, merge_weight, merge_bias, second_gain, second_bias, router, router_noise, expert_ids, expert_in, expert_in_bias, expert_out, expert_out_bias, cotangent):
    flat_rows = expert_rows(expert_ids)
    counts = lax.optimization_barrier(jnp.sum((expert_ids[:, :, None] == jnp.arange(E, dtype=jnp.int32)).astype(jnp.float32), axis=(0, 1)))
    params = tuple((argument.astype(jnp.float32) for argument in (inputs, first_gain, first_bias, head_weight, head_bias, merge_weight, merge_bias, second_gain, second_bias, router, expert_in, expert_in_bias, expert_out, expert_out_bias)))
    noise_values = router_noise.astype(jnp.float32)

    def wrapped(*floats):
        return forward(*floats, noise_values, expert_ids, flat_rows, counts)
    results, pullback = jax.vjp(wrapped, *params)
    gradients = pullback((cotangent.astype(jnp.float32), jnp.ones((), jnp.float32)))
    return (results[0], results[1], gradients[0], gradients[1], gradients[2], gradients[3], gradients[4], gradients[5], gradients[6], gradients[7], gradients[8], gradients[9], gradients[10], gradients[11], gradients[12], gradients[13])
```

```python
import functools

import jax
import jax.numpy as jnp
from jax import lax
from jax.experimental import pallas as pl
from jax.experimental.pallas import tpu as pltpu
from jax.sharding import PartitionSpec as P

HEAD_DIM = 64
SEQ = 197
CAP = 128
ROWS = 208
MIB = 1 << 20
F32 = jnp.float32
BF16 = jnp.bfloat16
VM = pl.BlockSpec(memory_space=pltpu.VMEM)
ANY = pl.BlockSpec(memory_space=pl.ANY)
CHUNKS = (0, 1, 3, 4, 2, 8, 5, 11, 6, 7, 9, 10)


def nn(a, b):
    return lax.dot_general(a, b, (((1,), (0,)), ((), ())), preferred_element_type=F32)


def nt(a, b):
    return lax.dot_general(a, b, (((1,), (1,)), ((), ())), preferred_element_type=F32)


def tn(a, b):
    return lax.dot_general(a, b, (((0,), (0,)), ((), ())), preferred_element_type=F32)


def place():
    d, h, t = lax.axis_index("dp"), lax.axis_index("heads"), lax.axis_index("tensor")
    return d, h // 2, h % 2, t


def device(d, x, c, t):
    return (d, 2 * x + c, t)


def meet(peers):
    barrier = pltpu.get_barrier_semaphore()
    for peer in peers:
        pl.semaphore_signal(barrier, inc=1, device_id=peer, device_id_type=pl.DeviceIdType.MESH)
    pl.semaphore_wait(barrier, len(peers))


def send(src, dst, send_sem, recv_sem, peer):
    copy = pltpu.make_async_remote_copy(
        src_ref=src,
        dst_ref=dst,
        send_sem=send_sem,
        recv_sem=recv_sem,
        device_id=peer,
        device_id_type=pl.DeviceIdType.MESH,
    )
    copy.start()
    return copy


def planar(x, t):
    return ((1 - x, t), (x, 1 - t), (1 - x, 1 - t))


def gather_kernel(a_ref, w_ref, g_ref, e_ref, own_sem, zs, zr, ps, pr, cs, cr, ezs, ezr, exs, exr, ecs, ecr):
    d, x, c, t = place()
    plane = planar(x, t)
    mate = device(d, x, 1 - c, t)
    peers = [device((d + k) % 4, x, c, t) for k in (1, 2, 3)]
    peers += [device(d, px, c, pt) for px, pt in plane] + [mate]
    me = 2 * x + c
    own = pltpu.make_async_copy(a_ref, g_ref.at[me, 2 * d + t], own_sem.at[0])
    own.start()
    own_w = pltpu.make_async_copy(w_ref.at[d], e_ref.at[:, 4 * d + me], own_sem.at[1])
    own_w.start()
    meet(peers)
    sent = []

    def slot(k, px, pt, pc):
        return g_ref.at[2 * px + pc, 2 * ((d + 4 - k) % 4) + pt]

    def piece(k, px, pc):
        return e_ref.at[:, 4 * ((d + 4 - k) % 4) + 2 * px + pc]

    for k in (1, 2, 3):
        sent.append(send(a_ref, slot(0, x, t, c), zs.at[k - 1], zr.at[k - 1], device((d + k) % 4, x, c, t)))
    for j, (px, pt) in enumerate(plane):
        sent.append(send(a_ref, slot(0, x, t, c), ps.at[j, 0], pr.at[j, 0], device(d, px, c, pt)))
    sent.append(send(a_ref, slot(0, x, t, c), cs.at[3, 0], cr.at[3, 0], mate))
    for k in (1, 2, 3):
        target = (d + k) % 4
        sent.append(
            send(w_ref.at[target], piece(0, x, c), ezs.at[k - 1], ezr.at[k - 1], device(target, x, c, t))
        )
    other = device(d, 1 - x, c, t)
    sent.append(send(w_ref.at[d], piece(0, x, c), exs.at[0], exr.at[0], other))
    sent.append(send(w_ref.at[d], piece(0, x, c), ecs.at[0, 0], ecr.at[0, 0], mate))
    waits = []
    for k in (1, 2, 3):
        here = slot(k, x, t, c)
        pltpu.make_async_copy(here, here, zr.at[k - 1]).wait()
        for j, (px, pt) in enumerate(plane):
            sent.append(send(here, here, ps.at[j, k], pr.at[j, k], device(d, px, c, pt)))
        sent.append(send(here, here, cs.at[3, k], cr.at[3, k], mate))
    for k in (1, 2, 3):
        here = piece(k, x, c)
        pltpu.make_async_copy(here, here, ezr.at[k - 1]).wait()
        sent.append(send(here, here, exs.at[k], exr.at[k], other))
        sent.append(send(here, here, ecs.at[0, k], ecr.at[0, k], mate))
    for k in range(4):
        for j, (px, pt) in enumerate(plane):
            here = slot(k, px, pt, c)
            pltpu.make_async_copy(here, here, pr.at[j, k]).wait()
            sent.append(send(here, here, cs.at[j, k], cr.at[j, k], mate))
    for k in range(4):
        here = piece(k, 1 - x, c)
        pltpu.make_async_copy(here, here, exr.at[k]).wait()
        sent.append(send(here, here, ecs.at[1, k], ecr.at[1, k], mate))
    for k in range(4):
        for j, (px, pt) in enumerate(plane + ((x, t),)):
            here = slot(k, px, pt, 1 - c)
            pltpu.make_async_copy(here, here, cr.at[j, k]).wait()
        for j, px in enumerate((x, 1 - x)):
            here = piece(k, px, 1 - c)
            pltpu.make_async_copy(here, here, ecr.at[j, k]).wait()
    for copy in sent:
        copy.wait_send()
    own.wait()
    own_w.wait()


def gather_weights(shard, experts):
    dma = pltpu.SemaphoreType.DMA
    return pl.pallas_call(
        gather_kernel,
        out_shape=(
            jax.ShapeDtypeStruct((4, 8) + shard.shape, BF16),
            jax.ShapeDtypeStruct((2, 16) + experts.shape[2:], BF16),
        ),
        in_specs=[VM, VM],
        out_specs=(ANY, ANY),
        scratch_shapes=[
            dma((2,)),
            dma((3,)),
            dma((3,)),
            dma((3, 4)),
            dma((3, 4)),
            dma((4, 4)),
            dma((4, 4)),
            dma((3,)),
            dma((3,)),
            dma((4,)),
            dma((4,)),
            dma((2, 4)),
            dma((2, 4)),
        ],
        compiler_params=pltpu.CompilerParams(collective_id=0, has_side_effects=True),
        name="gather_weights",
    )(shard, experts)


def dispatch_kernel(s_ref, r_ref, own_sem, zs, zr, ys, yr):
    d, x, c, t = place()
    beside = device(d, x, c, 1 - t)
    own = pltpu.make_async_copy(s_ref.at[d], r_ref.at[2 * d + t], own_sem)
    own.start()
    meet([device((d + k) % 4, x, c, t) for k in (1, 2, 3)] + [beside])
    sent = []
    for k in (1, 2, 3):
        target = (d + k) % 4
        sent.append(
            send(s_ref.at[target], r_ref.at[2 * d + t], zs.at[k - 1], zr.at[k - 1], device(target, x, c, t))
        )
    sent.append(send(s_ref.at[d], r_ref.at[2 * d + t], ys.at[0], yr.at[0], beside))
    for k in (1, 2, 3):
        here = r_ref.at[2 * ((d + 4 - k) % 4) + t]
        pltpu.make_async_copy(here, here, zr.at[k - 1]).wait()
        sent.append(send(here, here, ys.at[k], yr.at[k], beside))
    for k in range(4):
        here = r_ref.at[2 * ((d + 4 - k) % 4) + 1 - t]
        pltpu.make_async_copy(here, here, yr.at[k]).wait()
    for copy in sent:
        copy.wait_send()
    own.wait()


def dispatch(slots):
    dma = pltpu.SemaphoreType.DMA
    return pl.pallas_call(
        dispatch_kernel,
        out_shape=jax.ShapeDtypeStruct((8,) + slots.shape[1:], BF16),
        in_specs=[VM],
        out_specs=ANY,
        scratch_shapes=[dma, dma((3,)), dma((3,)), dma((4,)), dma((4,))],
        compiler_params=pltpu.CompilerParams(collective_id=1, has_side_effects=True),
        name="dispatch_slots",
    )(slots)


def collect_kernel(p_ref, b_ref, got, acc, ys, yr, zs, zr):
    d, x, c, t = place()
    beside = device(d, x, c, 1 - t)
    meet([device((d + k) % 4, x, c, t) for k in (1, 2, 3)] + [beside])
    sent = []
    order = [(d + k) % 4 for k in (1, 2, 3, 0)]
    for k, z in enumerate(order):
        sent.append(send(p_ref.at[2 * z + 1 - t], got.at[k], ys.at[k], yr.at[k], beside))
    for k, z in enumerate(order):
        pltpu.make_async_copy(got.at[k], got.at[k], yr.at[k]).wait()
        total = (p_ref[2 * z + t].astype(F32) + got[k].astype(F32)).astype(BF16)
        if k == 3:
            b_ref[d] = total
        else:
            acc[k] = total
            sent.append(send(acc.at[k], b_ref.at[d], zs.at[k], zr.at[k], device(z, x, c, t)))
    for k in (1, 2, 3):
        here = b_ref.at[(d + 4 - k) % 4]
        pltpu.make_async_copy(here, here, zr.at[k - 1]).wait()
    for copy in sent:
        copy.wait_send()


def collect(partial):
    dma = pltpu.SemaphoreType.DMA
    block = partial.shape[1:]
    return pl.pallas_call(
        collect_kernel,
        out_shape=jax.ShapeDtypeStruct((4,) + block, BF16),
        in_specs=[VM],
        out_specs=VM,
        scratch_shapes=[
            pltpu.VMEM((4,) + block, BF16),
            pltpu.VMEM((3,) + block, BF16),
            dma((4,)),
            dma((4,)),
            dma((3,)),
            dma((3,)),
        ],
        compiler_params=pltpu.CompilerParams(
            collective_id=2, has_side_effects=True, vmem_limit_bytes=32 * MIB
        ),
        name="collect_rows",
    )(partial)


def reduce_experts_kernel(p_ref, o_ref, got1, acc1, got2, acc2, cs, cr, xs, xr, zs, zr):
    d, x, c, t = place()
    mate, other = device(d, x, 1 - c, t), device(d, 1 - x, c, t)
    meet([device((d + k) % 4, x, c, t) for k in (1, 2, 3)] + [other, mate])
    sent = []
    order = [(d + k) % 4 for k in (1, 2, 3, 0)]
    for i, px in enumerate((1 - x, x)):
        for k, z in enumerate(order):
            sent.append(
                send(p_ref.at[:, 4 * z + 2 * px + 1 - c], got1.at[i, k], cs.at[i, k], cr.at[i, k], mate)
            )
    for i, px in enumerate((1 - x, x)):
        for k, z in enumerate(order):
            pltpu.make_async_copy(got1.at[i, k], got1.at[i, k], cr.at[i, k]).wait()
            acc1[i, k] = (p_ref[:, 4 * z + 2 * px + c].astype(F32) + got1[i, k].astype(F32)).astype(BF16)
            if i == 0:
                sent.append(send(acc1.at[0, k], got2.at[k], xs.at[k], xr.at[k], other))
    for k, z in enumerate(order):
        pltpu.make_async_copy(got2.at[k], got2.at[k], xr.at[k]).wait()
        total = (acc1[1, k].astype(F32) + got2[k].astype(F32)).astype(BF16)
        if k == 3:
            o_ref[d] = total
        else:
            acc2[k] = total
            sent.append(send(acc2.at[k], o_ref.at[d], zs.at[k], zr.at[k], device(z, x, c, t)))
    for k in (1, 2, 3):
        here = o_ref.at[(d + 4 - k) % 4]
        pltpu.make_async_copy(here, here, zr.at[k - 1]).wait()
    for copy in sent:
        copy.wait_send()


def reduce_experts(partial):
    dma = pltpu.SemaphoreType.DMA
    two, _, rows, wide = partial.shape
    piece = (two, rows, wide)
    return pl.pallas_call(
        reduce_experts_kernel,
        out_shape=jax.ShapeDtypeStruct((4,) + piece, BF16),
        in_specs=[VM],
        out_specs=VM,
        scratch_shapes=[
            pltpu.VMEM((2, 4) + piece, BF16),
            pltpu.VMEM((2, 4) + piece, BF16),
            pltpu.VMEM((4,) + piece, BF16),
            pltpu.VMEM((3,) + piece, BF16),
            dma((2, 4)),
            dma((2, 4)),
            dma((4,)),
            dma((4,)),
            dma((3,)),
            dma((3,)),
        ],
        compiler_params=pltpu.CompilerParams(
            collective_id=3, has_side_effects=True, vmem_limit_bytes=48 * MIB
        ),
        name="reduce_experts",
    )(partial)


def reduce_shards_kernel(
    p_ref, s_ref, o_ref, q_ref, got1, acc1, got2, acc2, got3, sgot, sacc, cs, cr, ps, pr, zs, zr, ss, sr
):
    d, x, c, t = place()
    plane = planar(x, t)
    mate = device(d, x, 1 - c, t)
    along = [device((d + k) % 4, x, c, t) for k in (1, 2, 3)]
    across = [device(d, px, c, pt) for px, pt in plane]
    meet(along + across + [mate])
    order = [(d + k) % 4 for k in (1, 2, 3, 0)]
    columns = plane + ((x, t),)
    sent = []
    for j, (px, pt) in enumerate(columns):
        for k, z in enumerate(order):
            sent.append(
                send(p_ref.at[2 * px + 1 - c, 2 * z + pt], got1.at[j, k], cs.at[j, k], cr.at[j, k], mate)
            )
    for k, peer in enumerate(along):
        sent.append(send(s_ref, sgot.at[k], ss.at[k], sr.at[k], peer))
    for j, (px, pt) in enumerate(columns):
        for k, z in enumerate(order):
            pltpu.make_async_copy(got1.at[j, k], got1.at[j, k], cr.at[j, k]).wait()
            acc1[j, k] = (p_ref[2 * px + c, 2 * z + pt].astype(F32) + got1[j, k].astype(F32)).astype(BF16)
            if j < 3:
                sent.append(send(acc1.at[j, k], got2.at[j, k], ps.at[j, k], pr.at[j, k], across[j]))
    for k in range(3):
        pltpu.make_async_copy(sgot.at[k], sgot.at[k], sr.at[k]).wait()
    sacc[0] = (s_ref[...] + sgot[1]) + (sgot[0] + sgot[2])
    for k, peer in enumerate(across):
        sent.append(send(sacc.at[0], sgot.at[3 + k], ss.at[3 + k], sr.at[3 + k], peer))
    for k in range(4):
        for j in range(3):
            pltpu.make_async_copy(got2.at[j, k], got2.at[j, k], pr.at[j, k]).wait()
        total = (acc1[3, k].astype(F32) + got2[0, k].astype(F32)) + (
            got2[1, k].astype(F32) + got2[2, k].astype(F32)
        )
        acc2[k] = total.astype(BF16)
        if k < 3:
            sent.append(send(acc2.at[k], got3.at[k], zs.at[k], zr.at[k], along[k]))
    for k in range(3):
        pltpu.make_async_copy(sgot.at[3 + k], sgot.at[3 + k], sr.at[3 + k]).wait()
    sacc[1] = (sacc[0] + sgot[5]) + (sgot[3] + sgot[4])
    sent.append(send(sacc.at[1], sgot.at[6], ss.at[6], sr.at[6], mate))
    for k in range(3):
        pltpu.make_async_copy(got3.at[k], got3.at[k], zr.at[k]).wait()
    o_ref[...] = (acc2[3].astype(F32) + got3[1].astype(F32)) + (got3[0].astype(F32) + got3[2].astype(F32))
    pltpu.make_async_copy(sgot.at[6], sgot.at[6], sr.at[6]).wait()
    q_ref[...] = sacc[1] + sgot[6]
    for copy in sent:
        copy.wait_send()


def reduce_shards(partial, small):
    dma = pltpu.SemaphoreType.DMA
    block = partial.shape[2:]
    return pl.pallas_call(
        reduce_shards_kernel,
        out_shape=(jax.ShapeDtypeStruct(block, F32), jax.ShapeDtypeStruct(small.shape, F32)),
        in_specs=[VM, VM],
        out_specs=(VM, VM),
        scratch_shapes=[
            pltpu.VMEM((4, 4) + block, BF16),
            pltpu.VMEM((4, 4) + block, BF16),
            pltpu.VMEM((3, 4) + block, BF16),
            pltpu.VMEM((4,) + block, BF16),
            pltpu.VMEM((3,) + block, BF16),
            pltpu.VMEM((7,) + small.shape, F32),
            pltpu.VMEM((2,) + small.shape, F32),
            dma((4, 4)),
            dma((4, 4)),
            dma((3, 4)),
            dma((3, 4)),
            dma((3,)),
            dma((3,)),
            dma((7,)),
            dma((7,)),
        ],
        compiler_params=pltpu.CompilerParams(
            collective_id=4, has_side_effects=True, vmem_limit_bytes=48 * MIB
        ),
        name="reduce_shards",
    )(partial, small)


def normalise(values):
    average = jnp.mean(values, axis=-1, keepdims=True)
    centred = values - average
    spread = jnp.mean(centred * centred, axis=-1, keepdims=True)
    inverse = lax.rsqrt(spread + 1e-06)
    return centred * inverse, inverse


def lanes(shape):
    return lax.broadcasted_iota(jnp.int32, shape, len(shape) - 1)


def halves():
    low = (lanes((1, 128)) < HEAD_DIM).astype(BF16)
    return low, (1 - low.astype(F32)).astype(BF16)


def selectors(spread_ref):
    chosen = spread_ref[...]
    rows = chosen.shape[1]
    earlier = lax.broadcasted_iota(jnp.int32, (rows, rows), 0) < lanes((rows, rows))
    before = nn(chosen.astype(BF16), earlier.astype(F32).astype(BF16)).astype(jnp.int32)
    slot = lax.broadcasted_iota(jnp.int32, (CAP, rows), 0)
    return [
        jnp.where((before[e : e + 1] == slot) & (chosen[e : e + 1] > 0.5), 1.0, 0.0).astype(BF16)
        for e in range(4)
    ]


HEADS_AT = ((0, 1, 4, 0, 0), (0, 1, 4, 1, 1), (2, 3, 2, 0, 1))


def forward_kernel(
    x_ref,
    g_ref,
    hb_ref,
    vec_ref,
    router_ref,
    noise_ref,
    spread_ref,
    cot_ref,
    n1_ref,
    qkv_ref,
    att_ref,
    lse_ref,
    res_ref,
    ch_ref,
    ds_ref,
    ob_ref,
):
    rows, wide = x_ref.shape
    values = x_ref[...].astype(F32)
    normal, _ = normalise(values)
    n1_ref[...] = (normal * vec_ref[0:1] + vec_ref[1:2]).astype(BF16)
    res_ref[...] = values + vec_ref[4:5]
    low, high = halves()
    alive = lanes((1, rows)) < SEQ

    def one(h, carry):
        weight = g_ref[h, :, 0:96, :].reshape(wide, wide)
        qkv_ref[h] = (nn(n1_ref[...], weight[:, 0:640]) + hb_ref[h]).astype(BF16)
        parts = []
        ends = jnp.zeros((rows, 128), F32)
        for i, (sq, sk, sv, uq, uv) in enumerate(HEADS_AT):
            query = qkv_ref[h, :, 128 * sq : 128 * sq + 128] * (high if uq else low)
            key = qkv_ref[h, :, 128 * sk : 128 * sk + 128]
            value = qkv_ref[h, :, 128 * sv : 128 * sv + 128] * (high if uv else low)
            scores = jnp.where(alive, HEAD_DIM ** (-0.5) * nt(query, key), -1e30)
            top = jnp.max(scores, axis=-1, keepdims=True)
            raised = jnp.exp(scores - top)
            total = jnp.sum(raised, axis=-1, keepdims=True)
            parts.append(nn((raised / total).astype(BF16), value))
            ends = jnp.where(lanes((1, 128)) == i, top + jnp.log(total), ends)
        lse_ref[h] = ends
        first, second = (parts[0] + parts[1]).astype(BF16), parts[2].astype(BF16)
        att_ref[h, :, 0:128] = first
        att_ref[h, :, 128:256] = second
        res_ref[...] += nt(first, weight[:, 640:768]) + nt(second, weight[:, 384:512])
        return carry

    lax.fori_loop(0, 4, one, 0)
    normal, _ = normalise(res_ref[...])
    second = (normal * vec_ref[2:3] + vec_ref[3:4]).astype(BF16)
    logits = nn(second, router_ref[...]) + noise_ref[...]
    raised = jnp.exp(logits - jnp.max(logits, axis=-1, keepdims=True))
    chances = raised / jnp.sum(raised, axis=-1, keepdims=True)
    ch_ref[...] = chances
    incoming = cot_ref[...].astype(F32)
    for e, select in enumerate(selectors(spread_ref)):
        ds_ref[e, 0] = nn(select, second).astype(BF16)
        taken = nn(select, (chances[:, e : e + 1] * incoming).astype(BF16))
        ds_ref[e, 1] = taken.astype(BF16)
        ob_ref[e : e + 1] = jnp.sum(taken, axis=0, keepdims=True)
    ob_ref[4:8] = jnp.zeros((4, wide), F32)


def forward_block(x, gathered, bias, vectors, router, noise, spread, cot):
    rows, wide = x.shape
    return pl.pallas_call(
        forward_kernel,
        out_shape=(
            jax.ShapeDtypeStruct((rows, wide), BF16),
            jax.ShapeDtypeStruct((4, rows, 640), BF16),
            jax.ShapeDtypeStruct((4, rows, 256), BF16),
            jax.ShapeDtypeStruct((4, rows, 128), F32),
            jax.ShapeDtypeStruct((rows, wide), F32),
            jax.ShapeDtypeStruct((rows, 128), F32),
            jax.ShapeDtypeStruct((4, 2, CAP, wide), BF16),
            jax.ShapeDtypeStruct((8, wide), F32),
        ),
        in_specs=[VM] * 8,
        out_specs=(VM,) * 8,
        compiler_params=pltpu.CompilerParams(vmem_limit_bytes=48 * MIB),
        cost_estimate=pl.CostEstimate(flops=2 * 10**9, bytes_accessed=12 * 10**6, transcendentals=10**6),
        name="attention_forward",
    )(x, gathered, bias, vectors, router, noise, spread, cot)


def expert_kernel(r_ref, w_ref, b_ref, o_ref, dw_ref, db_ref, hid, pre, xt, rt):
    blocks, _, cap, wide = r_ref.shape
    units = w_ref.shape[3]
    step, tile = 2 * cap, 512
    db_ref[...] = jnp.zeros_like(db_ref)

    def rows_of(i, carry):
        x = r_ref[pl.ds(2 * i, 2), 0].reshape(step, wide)
        r = r_ref[pl.ds(2 * i, 2), 1].reshape(step, wide)
        at = pl.ds(pl.multiple_of(i * step, step), step)
        xt[:, at] = x.T
        rt[:, at] = r.T
        out = jnp.zeros((step, wide), F32)
        back = jnp.zeros((step, wide), F32)
        for f in range(units // tile):
            cols = slice(f * tile, f * tile + tile)
            w_in = w_ref[0, :, :, cols].reshape(wide, tile)
            w_out = w_ref[1, :, :, cols].reshape(wide, tile)
            v = nn(x, w_in) + b_ref[0:1, cols]
            square = v * v
            bend = jnp.tanh(0.7978845608028654 * v * (1.0 + 0.044715 * square))
            hidden = (0.5 * v * (1.0 + bend)).astype(BF16)
            slope = 0.5 * (1.0 + bend) + 0.5 * v * (1.0 - bend * bend) * (
                0.7978845608028654 * (1.0 + 3 * 0.044715 * square)
            )
            grad = nn(r, w_out) * slope
            low = grad.astype(BF16)
            hid[at, cols] = hidden
            pre[at, cols] = low
            db_ref[0:1, cols] += jnp.sum(low.astype(F32), axis=0, keepdims=True)
            out += nt(hidden, w_out)
            back += nt(low, w_in)
        o_ref[pl.ds(2 * i, 2), 0] = out.astype(BF16).reshape(2, cap, wide)
        o_ref[pl.ds(2 * i, 2), 1] = back.astype(BF16).reshape(2, cap, wide)
        return carry

    lax.fori_loop(0, blocks // 2, rows_of, 0)

    def columns_of(f, carry):
        cols = pl.ds(pl.multiple_of(f * 256, 256), 256)
        shape = w_ref.shape[1:3] + (256,)
        dw_ref[0, :, :, cols] = nn(xt[...], pre[:, cols]).astype(BF16).reshape(shape)
        dw_ref[1, :, :, cols] = nn(rt[...], hid[:, cols]).astype(BF16).reshape(shape)
        return carry

    lax.fori_loop(0, units // 256, columns_of, 0)


def expert_block(received, weights, bias):
    blocks, _, cap, wide = received.shape
    units = weights.shape[3]
    return pl.pallas_call(
        expert_kernel,
        out_shape=(
            jax.ShapeDtypeStruct(received.shape, BF16),
            jax.ShapeDtypeStruct(weights.shape, BF16),
            jax.ShapeDtypeStruct((8, units), F32),
        ),
        in_specs=[VM] * 3,
        out_specs=(VM,) * 3,
        scratch_shapes=[
            pltpu.VMEM((blocks * cap, units), BF16),
            pltpu.VMEM((blocks * cap, units), BF16),
            pltpu.VMEM((wide, blocks * cap), BF16),
            pltpu.VMEM((wide, blocks * cap), BF16),
        ],
        compiler_params=pltpu.CompilerParams(vmem_limit_bytes=56 * MIB),
        cost_estimate=pl.CostEstimate(flops=15 * 10**9, bytes_accessed=16 * 10**6, transcendentals=2 * 10**6),
        name="expert_block",
    )(received, weights, bias)


def backward_kernel(
    x_ref,
    g_ref,
    vec_ref,
    router_ref,
    chosen_ref,
    spread_ref,
    cot_ref,
    load_ref,
    eb_ref,
    n1_ref,
    qkv_ref,
    att_ref,
    lse_ref,
    res_ref,
    ch_ref,
    ob_ref,
    bk_ref,
    out_ref,
    ig_ref,
    dg_ref,
    hb_ref,
    sm_ref,
    n1t,
    brt,
    dqkv,
    dn1,
):
    rows, wide = x_ref.shape
    incoming = cot_ref[...].astype(F32)
    chances, chosen = ch_ref[...], chosen_ref[...]
    normal, inverse = normalise(res_ref[...])
    second = (normal * vec_ref[2:3] + vec_ref[3:4]).astype(BF16)
    output = res_ref[...]
    dn2 = jnp.zeros((rows, wide), F32)
    gate_grads = jnp.zeros((rows, 128), F32)
    for e, select in enumerate(selectors(spread_ref)):
        used = chosen[:, e : e + 1]
        picked = tn(select, bk_ref[e, 0]) + used * eb_ref[e : e + 1]
        output += chances[:, e : e + 1] * picked
        gate_grads = jnp.where(
            lanes((1, 128)) == e, jnp.sum(incoming * picked, axis=-1, keepdims=True), gate_grads
        )
        dn2 += tn(select, bk_ref[e, 1])
    out_ref[...] = output
    chance_grad = gate_grads + load_ref[0:1]
    logit_grad = chances * (chance_grad - jnp.sum(chances * chance_grad, axis=-1, keepdims=True))
    living = lax.broadcasted_iota(jnp.int32, (rows, 1), 0) < SEQ
    logit_low = jnp.where(living, logit_grad, 0.0).astype(BF16)
    router_grad = tn(logit_low, second)
    dn2 += nt(logit_low, router_ref[...])
    scaled = dn2 * vec_ref[2:3]
    resid = incoming + inverse * (
        scaled
        - jnp.mean(scaled, axis=-1, keepdims=True)
        - normal * jnp.mean(scaled * normal, axis=-1, keepdims=True)
    )
    ig_ref[...] = resid
    branch = resid.astype(BF16)
    sm_ref[...] = jnp.zeros_like(sm_ref)
    sm_ref[2:3] = jnp.sum(dn2 * normal, axis=0, keepdims=True)
    sm_ref[3:4] = jnp.sum(dn2, axis=0, keepdims=True)
    sm_ref[4:5] = jnp.sum(branch.astype(F32), axis=0, keepdims=True)
    sm_ref[8:12] = router_grad[0:4]
    sm_ref[12:16] = ob_ref[0:4]
    sm_ref[5:6, 0:128] = jnp.sum(jnp.where(living, chances, 0.0), axis=0, keepdims=True)
    n1t[...] = n1_ref[...].T
    brt[...] = branch.T
    dn1[...] = jnp.zeros_like(dn1)
    low, high = halves()
    alive = lanes((1, rows)) < SEQ

    def one(h, carry):
        weight = g_ref[h, :, 0:96, :].reshape(wide, wide)
        from_first = nn(branch, weight[:, 640:768]).astype(BF16)
        from_second = nn(branch, weight[:, 384:512]).astype(BF16)
        ends = lse_ref[h]
        slabs = [None] * 5
        for i, (sq, sk, sv, uq, uv) in enumerate(HEADS_AT):
            mask_q, mask_v = (high if uq else low), (high if uv else low)
            query = qkv_ref[h, :, 128 * sq : 128 * sq + 128] * mask_q
            key = qkv_ref[h, :, 128 * sk : 128 * sk + 128]
            value = qkv_ref[h, :, 128 * sv : 128 * sv + 128]
            grad = (from_first if i < 2 else from_second) * mask_v
            scores = HEAD_DIM ** (-0.5) * nt(query, key)
            weights = jnp.where(alive, jnp.exp(jnp.where(alive, scores - ends[:, i : i + 1], 0.0)), 0.0)
            value_grad = tn(weights.astype(BF16), grad)
            weight_grad = nt(grad, value)
            inner = jnp.sum(weight_grad * weights, axis=-1, keepdims=True)
            score = (weights * (weight_grad - inner)).astype(BF16)
            query_grad = HEAD_DIM ** (-0.5) * nn(score, key * mask_q)
            key_grad = HEAD_DIM ** (-0.5) * tn(score, query)
            for at, part in ((sq, query_grad), (sk, key_grad), (sv, value_grad)):
                slabs[at] = part if slabs[at] is None else slabs[at] + part
        for at, slab in enumerate(slabs):
            low_slab = slab.astype(BF16)
            dqkv[:, 128 * at : 128 * at + 128] = low_slab
            hb_ref[h, 0:1, 128 * at : 128 * at + 128] = jnp.sum(low_slab.astype(F32), axis=0, keepdims=True)
        dn1[...] += nt(dqkv[...], weight[:, 0:640])
        shape = (8, 96, 128)
        for at in range(6):
            if at < 5:
                part = nn(n1t[...], dqkv[:, 128 * at : 128 * at + 128])
                if at == 3:
                    part += nn(brt[...], att_ref[h, :, 128:256])
            else:
                part = nn(brt[...], att_ref[h, :, 0:128])
            dg_ref[h, :, :, 128 * at : 128 * at + 128] = part.astype(BF16).reshape(shape)
        return carry

    lax.fori_loop(0, 4, one, 0)
    first_grad = dn1[...]
    normal, inverse = normalise(x_ref[...].astype(F32))
    scaled = first_grad * vec_ref[0:1]
    ig_ref[...] += inverse * (
        scaled
        - jnp.mean(scaled, axis=-1, keepdims=True)
        - normal * jnp.mean(scaled * normal, axis=-1, keepdims=True)
    )
    sm_ref[0:1] = jnp.sum(first_grad * normal, axis=0, keepdims=True)
    sm_ref[1:2] = jnp.sum(first_grad, axis=0, keepdims=True)


def backward_block(*operands):
    rows, wide = operands[0].shape
    return pl.pallas_call(
        backward_kernel,
        out_shape=(
            jax.ShapeDtypeStruct((rows, wide), F32),
            jax.ShapeDtypeStruct((rows, wide), F32),
            jax.ShapeDtypeStruct((4, 8, 96, wide), BF16),
            jax.ShapeDtypeStruct((4, 1, 640), F32),
            jax.ShapeDtypeStruct((16, wide), F32),
        ),
        in_specs=[VM] * len(operands),
        out_specs=(VM,) * 5,
        scratch_shapes=[
            pltpu.VMEM((wide, rows), BF16),
            pltpu.VMEM((wide, rows), BF16),
            pltpu.VMEM((rows, 640), BF16),
            pltpu.VMEM((rows, wide), F32),
        ],
        compiler_params=pltpu.CompilerParams(vmem_limit_bytes=56 * MIB),
        cost_estimate=pl.CostEstimate(flops=4 * 10**9, bytes_accessed=18 * 10**6, transcendentals=10**6),
        name="attention_backward",
    )(*operands)


def staged_body(
    inputs,
    first_gain,
    first_bias,
    head_weight,
    head_bias,
    merge_weight,
    merge_bias,
    second_gain,
    second_bias,
    router,
    router_noise,
    expert_ids,
    expert_in,
    expert_in_bias,
    expert_out,
    expert_out_bias,
    cotangent,
):
    tok_rows, wide = inputs.shape
    experts = expert_in.shape[0]
    d, h, t = lax.axis_index("dp"), lax.axis_index("heads"), lax.axis_index("tensor")
    total_tokens = tok_rows * lax.axis_size(("dp", "heads", "tensor"))
    extra = ROWS - tok_rows
    chosen = jnp.sum(
        (expert_ids[:, :, None] == jnp.arange(experts, dtype=jnp.int32)).astype(F32), axis=1
    )
    counts = jnp.sum(chosen, axis=0)
    kinds = jnp.concatenate([head_weight, merge_weight.T[None]], axis=0)
    kinds = jnp.transpose(kinds, (1, 0, 2)).reshape(96, 12, HEAD_DIM)
    packed = jnp.concatenate([kinds[:, k] for k in CHUNKS], axis=1)
    tiny = jnp.concatenate([head_bias.reshape(-1), expert_in_bias.reshape(-1), counts.astype(BF16)])
    tiny = jnp.pad(tiny[None], ((0, 15), (0, wide - tiny.shape[0])))
    shard = jnp.concatenate([packed, tiny], axis=0)
    pieces = jnp.stack([expert_in, jnp.transpose(expert_out, (0, 2, 1))], axis=1)
    gathered, weights = gather_weights(shard, pieces)
    tinies = gathered[:, :, 96, :]
    bias = tinies[:, :, 0:48].reshape(4, 8, 2, 24).transpose(2, 0, 1, 3).reshape(2, 4, 3, HEAD_DIM).astype(F32)
    none = jnp.zeros((4, 2 * HEAD_DIM), F32)
    head_row = jnp.concatenate(
        [bias[0, :, 0], bias[0, :, 1], none, bias[0, :, 2], bias[1, :, 2], none, bias[1, :, 0], bias[1, :, 1]],
        axis=1,
    )[:, None]
    in_bias = tinies[:, :, 48 : 48 + 96 * experts].reshape(4, 4, 2, experts, 96).transpose(3, 2, 1, 0, 4)
    in_bias = lax.dynamic_slice(in_bias.reshape(experts, 2, 1536), (d, t, 0), (1, 1, 1536))
    in_bias = jnp.broadcast_to(in_bias.reshape(1, 1536).astype(F32), (8, 1536))
    count_all = jnp.sum(tinies[:, :, 48 + 96 * experts : 52 + 96 * experts].astype(F32), axis=(0, 1))
    load_share = count_all / (2 * total_tokens)
    vectors = jnp.stack(
        [first_gain, first_bias, second_gain, second_bias, merge_bias] + [jnp.zeros_like(merge_bias)] * 3
    ).astype(F32)
    router_wide = jnp.pad(router, ((0, 0), (0, 128 - experts)))
    noise = jnp.pad(
        jnp.pad(router_noise, ((0, extra), (0, 0))), ((0, 0), (0, 128 - experts)), constant_values=-1e30
    )
    chosen_wide = jnp.pad(chosen, ((0, extra), (0, 128 - experts)))
    spread = jnp.pad(chosen.T, ((0, 8 - experts), (0, extra)))
    x = jnp.pad(inputs, ((0, extra), (0, 0)))
    cot = jnp.pad(cotangent, ((0, extra), (0, 0)))
    n1, qkv, attended, lse, residual, chances, slots, out_bias = forward_block(
        x, gathered, head_row, vectors, router_wide, noise, spread, cot
    )
    received = dispatch(slots)
    partial, weight_grads, in_bias_rows = expert_block(received, weights, in_bias)
    own_grads = reduce_experts(weight_grads)
    back = collect(partial)
    load = jnp.pad((experts * load_share / total_tokens)[None], ((0, 7), (0, 128 - experts)))
    eb = jnp.pad(expert_out_bias.astype(F32), ((0, 8 - experts), (0, 0)))
    output, input_grad, shard_grads, head_rows, small = backward_block(
        x,
        gathered,
        vectors,
        router_wide,
        chosen_wide,
        spread,
        cot,
        load,
        eb,
        n1,
        qkv,
        attended,
        lse,
        residual,
        chances,
        out_bias,
        back,
    )
    mine = (jnp.arange(experts)[:, None] == d) & (jnp.arange(2)[None, :] == t)
    in_rows = jnp.where(mine[:, :, None], in_bias_rows[0][None, None], 0.0).reshape(16, wide)
    head_rows = jnp.pad(head_rows.reshape(4, 640), ((0, 4), (0, wide - 640)))
    shard_grad, sums = reduce_shards(shard_grads, jnp.concatenate([small, head_rows, in_rows], axis=0))
    order = [CHUNKS.index(k) for k in range(12)]
    parts = [shard_grad[:, HEAD_DIM * k : HEAD_DIM * k + HEAD_DIM] for k in order]
    head_weight_grad = jnp.stack([jnp.concatenate(parts[3 * j : 3 * j + 3], axis=1) for j in range(3)])
    merge_grad = jnp.concatenate(parts[9:12], axis=1).T
    heads = lax.dynamic_slice(sums[16:20], (h, 0), (1, 640))[0]
    biases = jnp.stack(
        [
            jnp.concatenate([heads[0:128], heads[256:320]]),
            jnp.concatenate([heads[512:640], heads[320:384]]),
        ]
    )
    head_bias_grad = lax.dynamic_slice(biases, (0, 24 * (2 * d + t)), (2, 24))
    in_bias_grad = lax.dynamic_slice(
        sums[24:40].reshape(experts, 3072), (0, 1536 * t + 96 * (4 * d + h)), (experts, 96)
    )
    balance_loss = experts * jnp.sum(load_share * sums[5, 0:experts] / total_tokens)
    return (
        output[:tok_rows],
        balance_loss,
        input_grad[:tok_rows],
        sums[0],
        sums[1],
        head_weight_grad,
        head_bias_grad,
        merge_grad,
        sums[4],
        sums[2],
        sums[3],
        sums[8:12].T,
        own_grads[:, 0].astype(F32),
        in_bias_grad,
        jnp.transpose(own_grads[:, 1], (0, 2, 1)).astype(F32),
        sums[12:16],
    )


def layer_norm(values, factor, offset):
    average = jnp.mean(values, axis=-1, keepdims=True)
    centred = values - average
    spread = jnp.mean(centred * centred, axis=-1, keepdims=True)
    return centred * lax.rsqrt(spread + 1e-06) * factor + offset


def expert_weights(expert_in, expert_out, expert_in_bias):
    return (
        lax.all_gather(expert_in, ("dp", "heads"), axis=1, tiled=True),
        lax.all_gather(expert_out, ("dp", "heads"), axis=2, tiled=True),
        lax.all_gather(expert_in_bias, ("dp", "heads"), axis=1, tiled=True),
    )


def plain_body(
    inputs,
    first_gain,
    first_bias,
    head_weight,
    head_bias,
    merge_weight,
    merge_bias,
    second_gain,
    second_bias,
    router,
    router_noise,
    expert_ids,
    expert_in,
    expert_in_bias,
    expert_out,
    expert_out_bias,
    cotangent,
):
    tok_rows = inputs.shape[0]
    features = inputs.shape[1]
    experts = expert_in.shape[0]
    head_cols = head_weight.shape[2]
    heads_local = head_cols // HEAD_DIM
    total_tokens = tok_rows * lax.axis_size(("dp", "heads", "tensor"))
    scale = HEAD_DIM ** (-0.5)
    whole_head, whole_merge, whole_bias = (
        lax.all_gather(head_weight, ("dp", "tensor"), axis=1, tiled=True),
        lax.all_gather(merge_weight, ("dp", "tensor"), axis=1, tiled=True),
        lax.all_gather(head_bias, ("dp", "tensor"), axis=1, tiled=True),
    )
    residual_in = inputs.astype(jnp.float32)
    normed, norm_back = jax.vjp(
        layer_norm, residual_in, first_gain.astype(jnp.float32), first_bias.astype(jnp.float32)
    )
    group_rows = lax.all_gather(normed.astype(jnp.bfloat16), "heads", axis=0, tiled=True)
    group_count = group_rows.shape[0]
    group_images = group_count // SEQ
    projected = jnp.einsum(
        "gd,jdc->jgc", group_rows, whole_head, preferred_element_type=jnp.float32
    )
    bias_values = whole_bias.astype(jnp.float32)
    query_low = (projected[0] + bias_values[0]).astype(jnp.bfloat16)
    key_low = projected[1].astype(jnp.bfloat16)
    value_low = (projected[2] + bias_values[1]).astype(jnp.bfloat16)

    def shaped(array):
        return array.reshape(group_images, SEQ, heads_local, HEAD_DIM)

    query_img, key_img, value_img = (shaped(query_low), shaped(key_low), shaped(value_low))
    scores = scale * jnp.einsum(
        "ishd,ithd->ihst", query_img, key_img, preferred_element_type=jnp.float32
    )
    top_score = jnp.max(scores, axis=-1, keepdims=True)
    raised = jnp.exp(scores - top_score)
    row_total = jnp.sum(raised, axis=-1, keepdims=True)
    weights = raised / row_total
    log_total = top_score + jnp.log(row_total)
    attended = jnp.einsum(
        "ihst,ithd->ishd",
        weights.astype(jnp.bfloat16),
        value_img,
        preferred_element_type=jnp.float32,
    )
    attended_low = attended.reshape(group_count, head_cols).astype(jnp.bfloat16)
    segment = attended_low
    branch = lax.psum_scatter(
        jnp.dot(segment, whole_merge, preferred_element_type=jnp.float32).astype(jnp.bfloat16),
        "heads",
        scatter_dimension=0,
        tiled=True,
    ).astype(jnp.float32) + merge_bias.astype(jnp.float32)
    residual = residual_in + branch
    normed_two, norm_two_back = jax.vjp(
        layer_norm, residual, second_gain.astype(jnp.float32), second_bias.astype(jnp.float32)
    )
    second_low = normed_two.astype(jnp.bfloat16)
    router_logits = jnp.dot(second_low, router, preferred_element_type=jnp.float32) + router_noise
    chances = jax.nn.softmax(router_logits, axis=-1)
    expert_range = jnp.arange(experts, dtype=jnp.int32)
    chosen_pair = (expert_ids[:, :, None] == expert_range).astype(jnp.int32)
    chosen = jnp.sum(chosen_pair, axis=1)
    order = jnp.arange(tok_rows, dtype=jnp.int32)
    earlier = (order[None, :] < order[:, None]).astype(jnp.bfloat16)
    before = jnp.dot(
        earlier, chosen.astype(jnp.bfloat16), preferred_element_type=jnp.float32
    ).astype(jnp.int32)
    slot_ids = jnp.take_along_axis(before, expert_ids, axis=1)
    flat_rows = (slot_ids * experts + expert_ids).reshape(-1)
    picks = chosen_pair.astype(jnp.float32)
    count_terms = jnp.sum(chosen.astype(jnp.float32), axis=0)
    chance_terms = jnp.sum(chances, axis=0)
    count_all, chance_all = lax.psum((count_terms, chance_terms), ("dp", "heads", "tensor"))
    load_share = count_all / (2 * total_tokens)
    balance_loss = experts * jnp.sum(load_share * chance_all / total_tokens)
    gate_values = jnp.sum(picks * chances[:, None, :], axis=2)
    doubled = jnp.repeat(second_low, 2, axis=0)
    own_buffer = jnp.zeros((CAP * experts, features), jnp.bfloat16).at[flat_rows].set(doubled)
    pair_buffer = lax.all_gather(
        own_buffer.reshape(CAP, experts, features), "tensor", axis=0, tiled=True
    )
    weight_in, weight_out, bias_in = expert_weights(expert_in, expert_out, expert_in_bias)
    before_act = (
        jnp.einsum("ced,edf->cef", pair_buffer, weight_in, preferred_element_type=jnp.float32)
        + bias_in.astype(jnp.float32)[None, :, :]
    )
    activated, gelu_back = jax.vjp(jax.nn.gelu, before_act)
    activated_low = activated.astype(jnp.bfloat16)
    partial_out = jnp.einsum(
        "cef,efd->ced", activated_low, weight_out, preferred_element_type=jnp.float32
    )
    own_out = (
        lax.psum_scatter(
            partial_out.astype(jnp.bfloat16), "tensor", scatter_dimension=0, tiled=True
        ).astype(jnp.float32)
        + expert_out_bias.astype(jnp.float32)[None, :, :]
    )
    picked = own_out.reshape(CAP * experts, features)[flat_rows].reshape(tok_rows, 2, features)
    output = residual + jnp.sum(gate_values[:, :, None] * picked, axis=1)
    incoming = cotangent.astype(jnp.float32)
    gate_grad = jnp.sum(incoming[:, None, :] * picked, axis=2)
    slot_grad = (
        (gate_values[:, :, None] * incoming[:, None, :])
        .astype(jnp.bfloat16)
        .reshape(tok_rows * 2, features)
    )
    own_slot_grad = (
        jnp.zeros((CAP * experts, features), jnp.bfloat16)
        .at[flat_rows]
        .set(slot_grad)
        .reshape(CAP, experts, features)
    )
    out_bias_grad = jnp.sum(own_slot_grad, axis=0, dtype=jnp.float32)
    pair_grad = lax.all_gather(own_slot_grad, "tensor", axis=0, tiled=True)
    back_in, back_out, unused_bias = expert_weights(expert_in, expert_out, expert_in_bias)
    hidden_grad = jnp.einsum(
        "ced,efd->cef", pair_grad, back_out, preferred_element_type=jnp.float32
    )
    pre_grad = gelu_back(hidden_grad)[0].astype(jnp.bfloat16)
    out_grad_rows = jnp.einsum(
        "cef,ced->def", activated_low, pair_grad, preferred_element_type=jnp.float32
    )
    in_grad_rows = jnp.einsum(
        "ced,cef->def", pair_buffer, pre_grad, preferred_element_type=jnp.float32
    )
    in_bias_rows = jnp.sum(pre_grad, axis=0, dtype=jnp.float32).T
    in_grad_rows, out_grad_rows, in_bias_rows = (
        lax.psum_scatter(in_grad_rows, ("dp", "heads"), scatter_dimension=0, tiled=True),
        lax.psum_scatter(out_grad_rows, ("dp", "heads"), scatter_dimension=0, tiled=True),
        lax.psum_scatter(in_bias_rows, ("dp", "heads"), scatter_dimension=0, tiled=True),
    )
    expert_in_grad = jnp.transpose(in_grad_rows, (1, 0, 2))
    expert_out_grad = jnp.transpose(out_grad_rows, (1, 2, 0))
    in_bias_grad = in_bias_rows.T
    buffer_grad = jnp.einsum("cef,edf->ced", pre_grad, back_in, preferred_element_type=jnp.float32)
    own_buffer_grad = (
        lax.psum_scatter(
            buffer_grad.astype(jnp.bfloat16), "tensor", scatter_dimension=0, tiled=True
        )
        .astype(jnp.float32)
        .reshape(CAP * experts, features)
    )
    second_grad = jnp.sum(own_buffer_grad[flat_rows].reshape(tok_rows, 2, features), axis=1)
    chance_grad = (
        jnp.sum(picks * gate_grad[:, :, None], axis=1) + experts * load_share / total_tokens
    )
    logit_grad = chances * (chance_grad - jnp.sum(chances * chance_grad, axis=-1, keepdims=True))
    logit_low = logit_grad.astype(jnp.bfloat16)
    router_grad = lax.dot_general(
        second_low, logit_low, (((0,), (0,)), ((), ())), preferred_element_type=jnp.float32
    )
    second_grad = second_grad + jnp.dot(logit_low, router.T, preferred_element_type=jnp.float32)
    resid_part, gain_two_grad, bias_two_grad = norm_two_back(second_grad)
    resid_grad = incoming + resid_part
    branch_low = resid_grad.astype(jnp.bfloat16)
    merge_bias_grad = jnp.sum(branch_low, axis=0, dtype=jnp.float32)
    group_grad = lax.all_gather(branch_low, "heads", axis=0, tiled=True)
    merge_rows_grad = lax.dot_general(
        group_grad, attended_low, (((0,), (0,)), ((), ())), preferred_element_type=jnp.float32
    )
    attended_grad = shaped(
        jnp.dot(group_grad, whole_merge.T, preferred_element_type=jnp.float32).astype(jnp.bfloat16)
    )
    weights_again = jnp.exp(
        scale
        * jnp.einsum("ishd,ithd->ihst", query_img, key_img, preferred_element_type=jnp.float32)
        - log_total
    )
    value_grad = jnp.einsum(
        "ihst,ishd->ithd",
        weights_again.astype(jnp.bfloat16),
        attended_grad,
        preferred_element_type=jnp.float32,
    )
    weight_grad = jnp.einsum(
        "ishd,ithd->ihst", attended_grad, value_img, preferred_element_type=jnp.float32
    )
    inner_sum = jnp.sum(weight_grad * weights_again, axis=-1, keepdims=True)
    score_low = (weights_again * (weight_grad - inner_sum)).astype(jnp.bfloat16)
    query_grad = scale * jnp.einsum(
        "ihst,ithd->ishd", score_low, key_img, preferred_element_type=jnp.float32
    )
    key_grad = scale * jnp.einsum(
        "ihst,ishd->ithd", score_low, query_img, preferred_element_type=jnp.float32
    )
    triple_low = jnp.stack(
        [
            query_grad.reshape(group_count, head_cols),
            key_grad.reshape(group_count, head_cols),
            value_grad.reshape(group_count, head_cols),
        ],
        axis=0,
    ).astype(jnp.bfloat16)
    head_rows_grad = jnp.einsum(
        "gd,jgc->djc", group_rows, triple_low, preferred_element_type=jnp.float32
    )
    head_bias_rows = jnp.sum(triple_low[0::2], axis=1, dtype=jnp.float32).T
    segment = triple_low
    first_grad = lax.psum_scatter(
        jnp.einsum("jgc,jdc->gd", segment, whole_head, preferred_element_type=jnp.float32).astype(
            jnp.bfloat16
        ),
        "heads",
        scatter_dimension=0,
        tiled=True,
    ).astype(jnp.float32)
    input_part, gain_one_grad, bias_one_grad = norm_back(first_grad)
    input_grad = resid_grad + input_part
    head_rows_grad, merge_rows_grad, head_bias_rows = (
        lax.psum_scatter(head_rows_grad, ("dp", "tensor"), scatter_dimension=0, tiled=True),
        lax.psum_scatter(merge_rows_grad, ("dp", "tensor"), scatter_dimension=0, tiled=True),
        lax.psum_scatter(head_bias_rows, ("dp", "tensor"), scatter_dimension=0, tiled=True),
    )
    head_weight_grad = jnp.transpose(head_rows_grad, (1, 0, 2))
    merge_grad = merge_rows_grad.T
    head_bias_grad = head_bias_rows.T
    small = lax.psum(
        (
            gain_one_grad,
            bias_one_grad,
            gain_two_grad,
            bias_two_grad,
            merge_bias_grad,
            router_grad,
            out_bias_grad,
        ),
        ("dp", "heads", "tensor"),
    )
    return (
        output,
        balance_loss,
        input_grad,
        small[0],
        small[1],
        head_weight_grad,
        head_bias_grad,
        merge_grad,
        small[4],
        small[2],
        small[3],
        small[5],
        expert_in_grad,
        in_bias_grad,
        expert_out_grad,
        small[6],
    )


def solution(mesh):
    in_specs = (
        P(("dp", "heads", "tensor"), None),
        P(),
        P(),
        P(None, ("dp", "tensor"), "heads"),
        P(None, ("heads", "dp", "tensor")),
        P("heads", ("dp", "tensor")),
        P(),
        P(),
        P(),
        P(),
        P(("dp", "heads", "tensor"), None),
        P(("dp", "heads", "tensor"), None),
        P(None, ("dp", "heads"), "tensor"),
        P(None, ("tensor", "dp", "heads")),
        P(None, "tensor", ("dp", "heads")),
        P(),
        P(("dp", "heads", "tensor"), None),
    )
    out_specs = (
        P(("dp", "heads", "tensor"), None),
        P(),
        P(("dp", "heads", "tensor"), None),
        P(),
        P(),
        P(None, ("dp", "tensor"), "heads"),
        P(None, ("heads", "dp", "tensor")),
        P("heads", ("dp", "tensor")),
        P(),
        P(),
        P(),
        P(),
        P(None, ("dp", "heads"), "tensor"),
        P(None, ("tensor", "dp", "heads")),
        P(None, "tensor", ("dp", "heads")),
        P(),
    )
    sizes = tuple(mesh.shape[name] for name in ("dp", "heads", "tensor"))
    body = staged_body if sizes == (4, 4, 2) else plain_body
    return jax.shard_map(body, mesh=mesh, in_specs=in_specs, out_specs=out_specs, check_vma=False)
```

```python
import functools

import jax
import jax.numpy as jnp
import numpy as np
from jax import lax
from jax.experimental import pallas as pl
from jax.experimental.pallas import tpu as pltpu
from jax.sharding import PartitionSpec as P

HEAD_DIM = 64
SEQ = 197
CAP = 128
ROWS = 208
MIB = 1 << 20
F32 = jnp.float32
BF16 = jnp.bfloat16
MESH = pl.DeviceIdType.MESH
VM = pl.BlockSpec(memory_space=pltpu.VMEM)
SCALE = HEAD_DIM ** (-0.5)
HEADS_AT = ((0, 1, 4, 0, 0), (0, 1, 4, 1, 1), (2, 3, 2, 0, 1))


def nn(a, b):
    return lax.dot_general(a, b, (((1,), (0,)), ((), ())), preferred_element_type=F32)


def nt(a, b):
    return lax.dot_general(a, b, (((1,), (1,)), ((), ())), preferred_element_type=F32)


def tn(a, b):
    return lax.dot_general(a, b, (((0,), (0,)), ((), ())), preferred_element_type=F32)


def exact_parts(values):
    parts = []
    for _ in range(3):
        part = values.astype(BF16)
        parts.append(part)
        values = values - part.astype(F32)
    return parts


def normalise(values):
    average = jnp.mean(values, axis=-1, keepdims=True)
    centred = values - average
    spread = jnp.mean(centred * centred, axis=-1, keepdims=True)
    inverse = lax.rsqrt(spread + 1e-06)
    return centred * inverse, inverse


def norm_back(grad, normal, inverse):
    return inverse * (
        grad
        - jnp.mean(grad, axis=-1, keepdims=True)
        - normal * jnp.mean(grad * normal, axis=-1, keepdims=True)
    )


def lanes(shape):
    return lax.broadcasted_iota(jnp.int32, shape, len(shape) - 1)


def rows_of(shape):
    return lax.broadcasted_iota(jnp.int32, shape, 0)


def halves():
    low = (lanes((1, 128)) < HEAD_DIM).astype(F32)
    return low.astype(BF16), (1 - low).astype(BF16)


def row_of(values, at):
    return jnp.sum(jnp.where(rows_of((values.shape[0], 1)) == at, values, 0.0), axis=0, keepdims=True)


def as_row(column):
    n = column.shape[0]
    return jnp.sum(jnp.where(rows_of((n, n)) == lanes((n, n)), column, 0.0), axis=0, keepdims=True)


def as_column(row):
    n = row.shape[1]
    return jnp.sum(jnp.where(rows_of((n, n)) == lanes((n, n)), row, 0.0), axis=1, keepdims=True)


def scratch_plan(wide, units, rows):
    shard, piece, block = (96, wide), (2, 48, units), (CAP, wide)
    return (
        ("a", shard, BF16),
        ("wp", (4,) + piece, BF16),
        ("g", (4, 4, 2) + shard, BF16),
        ("w", (16,) + piece, BF16),
        ("xb", piece, BF16),
        ("p0", (16, units), BF16),
        ("psum", (3, 16, units), BF16),
        ("pgot", (6, 16, units), BF16),
        ("bias", (16, units), F32),
        ("vec", (8, wide), F32),
        ("brow", (8, units), F32),
        ("eb", (128, wide), BF16),
        ("cs", (4,) + block, BF16),
        ("gs", (4, 8, CAP), F32),
        ("rt", (4, 2) + block, BF16),
        ("rc", (4, 2) + block, BF16),
        ("rg", (4, 2, 8, CAP), F32),
        ("sel", (4, CAP, rows), BF16),
        ("xs", (rows, wide), BF16),
        ("cot", (rows, wide), BF16),
        ("wide8", (128, rows), F32),
        ("chosen", (rows, 128), F32),
        ("spread", (8, rows), F32),
        ("before", (8, rows), F32),
        ("noise", (rows, 128), F32),
        ("router", (128, wide), BF16),
        ("n1", (rows, wide), BF16),
        ("n2", (rows, wide), BF16),
        ("qkv", (4, rows, 640), BF16),
        ("att", (4, rows, 256), BF16),
        ("lse", (4, rows, 128), F32),
        ("res", (rows, wide), F32),
        ("ch", (rows, 128), F32),
        ("chp", (3, rows, 128), BF16),
        ("hp", (4 * 8 * CAP, wide), BF16),
        ("xt", (wide, 8 * CAP), BF16),
        ("gt", (wide, 8 * CAP), BF16),
        ("db", (8, units), F32),
        ("so", (2 * CAP, wide), F32),
        ("sb", (2 * CAP, wide), F32),
        ("yo", (4, 2) + block, BF16),
        ("yx", (4, 2) + block, BF16),
        ("yg", (4, 2, 8, CAP), F32),
        ("goto", (4,) + block, BF16),
        ("gotx", (4,) + block, BF16),
        ("gotg", (4, 8, CAP), F32),
        ("bo", (4,) + block, BF16),
        ("bx", (4,) + block, BF16),
        ("bg", (4, 8, CAP), F32),
        ("gotc", (8,) + piece, BF16),
        ("gotz", (4,) + piece, BF16),
        ("gotm", (2, wide, wide), BF16),
        ("gotp", (3, 4) + shard, BF16),
        ("gots", (3,) + shard, BF16),
        ("n1t", (wide, rows), BF16),
        ("brt", (wide, rows), BF16),
        ("dqkv", (rows, 640), BF16),
        ("dn1", (rows, wide), F32),
        ("told", (rows, 128), F32),
        ("ig", (rows, wide), F32),
        ("e0", (16, wide), F32),
        ("esum", (3, 16, wide), F32),
        ("egot", (6, 16, wide), F32),
        ("l0", (8, wide), F32),
        ("lsum", (3, 8, wide), F32),
        ("lgot", (6, 8, wide), F32),
        ("d0", (3, 16, 128), F32),
        ("dgot", (6, 16, 128), F32),
    )


class Buffers:
    pass


class Exchange:
    def __init__(self, send_sems, recv_sems):
        self.send_sems, self.recv_sems = send_sems, recv_sems
        self.used = 0
        d, h, t = lax.axis_index("dp"), lax.axis_index("heads"), lax.axis_index("tensor")
        x, c = h // 2, h % 2
        self.d, self.x, self.c, self.t = d, x, c, t
        self.zh, self.zl = d // 2, d % 2
        self.zs = (d, (d + 2) % 4, 2 * self.zh + 1 - self.zl, 2 * (1 - self.zh) + 1 - self.zl)
        self.plane = ((1 - x, t), (x, 1 - t), (1 - x, 1 - t))
        self.along = [self.at(z, x, c, t) for z in self.zs[1:]]
        self.across = [self.at(d, px, c, pt) for px, pt in self.plane]
        self.mate = self.at(d, x, 1 - c, t)
        self.other_y = self.across[1]

    @staticmethod
    def at(d, x, c, t):
        return (d, 2 * x + c, t)

    def group(self, g):
        return 2 * self.zh + (self.zl + g // 2) % 2, (self.x + g) % 2

    def expert(self, g):
        z, x = self.group(g)
        return 2 * (z % 2) + x

    def holder(self, g):
        z, x = self.group(g)
        return self.at(z, x, self.c, self.t)

    def shard(self, j):
        return 2 * ((self.x + 1 + j) % 2) + (self.c + 1 + j // 2) % 2

    def slots(self, count):
        self.used += count
        return self.used - count

    def send(self, slot, src, dst, peer):
        pltpu.make_async_remote_copy(
            src_ref=src,
            dst_ref=dst,
            send_sem=self.send_sems.at[slot],
            recv_sem=self.recv_sems.at[slot],
            device_id=peer,
            device_id_type=MESH,
        ).start()

    def sent(self, slot, ref):
        pltpu.make_async_copy(ref, ref, self.send_sems.at[slot]).wait()

    def arrived(self, slot, ref):
        pltpu.make_async_copy(ref, ref, self.recv_sems.at[slot]).wait()

    def meet(self):
        barrier = pltpu.get_barrier_semaphore()
        peers = self.along + self.across + [self.mate, self.holder(3)]
        for peer in peers:
            pl.semaphore_signal(barrier, inc=1, device_id=peer, device_id_type=MESH)
        pl.semaphore_wait(barrier, len(peers))


class SumOverAll:
    def __init__(self, ex, own, sums, got):
        self.ex, self.own, self.sums, self.got = ex, own, sums, got
        self.slot = ex.slots(6)

    def start(self):
        self.ex.send(self.slot, self.own, self.got.at[0], self.ex.mate)

    def to_plane(self):
        self.ex.arrived(self.slot, self.got.at[0])
        self.sums[0] = self.own[...] + self.got[0]
        for j, peer in enumerate(self.ex.across):
            self.ex.send(self.slot + 1 + j, self.sums.at[0], self.got.at[1 + j], peer)

    def to_half(self):
        for j in range(3):
            self.ex.arrived(self.slot + 1 + j, self.got.at[1 + j])
        self.sums[1] = (self.sums[0] + self.got[3]) + (self.got[1] + self.got[2])
        self.ex.send(self.slot + 4, self.sums.at[1], self.got.at[4], self.ex.along[0])

    def to_pair(self):
        self.ex.arrived(self.slot + 4, self.got.at[4])
        self.sums[2] = self.sums[1] + self.got[4]
        self.ex.send(self.slot + 5, self.sums.at[2], self.got.at[5], self.ex.along[1])

    def result(self):
        self.ex.arrived(self.slot + 5, self.got.at[5])
        return self.sums[2].astype(F32) + self.got[5].astype(F32)

    def done(self):
        for k in range(6):
            self.ex.sent(self.slot + k, self.got.at[k])


def bias_lanes(ex):
    chunk, lane = lanes((1, 640)) // HEAD_DIM, lanes((1, 640)) % HEAD_DIM
    kind = jnp.where(
        (chunk < 2) | (chunk == 4), 0, jnp.where((chunk == 5) | (chunk == 8) | (chunk == 9), 1, 2)
    )
    head = jnp.where((chunk == 1) | (chunk == 9), 1, jnp.where((chunk == 4) | (chunk == 5), 2, 0))
    wanted = 24 * (2 * ex.d + ex.t) + rows_of((24, 640))
    heads = ((HEAD_DIM * head + lane == wanted) & (kind < 2)).astype(F32).astype(BF16)
    return heads, kind


def hidden_lanes(ex, units):
    wanted = 96 * (4 * ex.d + 2 * ex.x + ex.c) + rows_of((96, units))
    return (lanes((96, units)) == wanted).astype(F32).astype(BF16)


def pack(b, ex, inputs):
    heads, merge, w_in, w_out = inputs
    q, k, v = heads[0], heads[1], heads[2]
    m = merge[...].T
    b.a[:, 0:128] = q[:, 0:128]
    b.a[:, 128:256] = k[:, 0:128]
    b.a[:, 256:384] = jnp.concatenate([q[:, 128:192], v[:, 128:192]], axis=1)
    b.a[:, 384:512] = jnp.concatenate([k[:, 128:192], m[:, 128:192]], axis=1)
    b.a[:, 512:640] = v[:, 0:128]
    b.a[:, 640:768] = m[:, 0:128]
    b.wp[:, 0] = w_in[...]
    b.wp[:, 1] = w_out[...]
    me = 2 * ex.x + ex.c
    b.g[3, ex.d, ex.t] = b.a[...]
    b.w[4 * ex.d + me] = b.wp[ex.expert(0)]


def small_operands(b, ex, ids_ref, head_bias_ref, in_bias_ref):
    named = rows_of((4, SEQ))
    ids = ids_ref[...]
    b.wide8[...] = jnp.zeros_like(b.wide8)
    b.wide8[0:4, 0:SEQ] = ((ids[0:1] == named) | (ids[1:2] == named)).astype(F32)
    b.spread[...] = b.wide8[0:8]
    b.chosen[...] = b.wide8[...].T
    heads, kind = bias_lanes(ex)
    row = nn(head_bias_ref[...], heads)
    row = jnp.where(kind == 0, row[0:1], jnp.where(kind == 1, row[1:2], 0.0))
    me = 2 * ex.x + ex.c
    hidden = nn(in_bias_ref[...], hidden_lanes(ex, b.p0.shape[1]))
    b.p0[...] = jnp.zeros_like(b.p0)
    b.p0[0:4] = jnp.where(ex.t == 0, hidden, 0.0).astype(BF16)
    b.p0[4:8] = jnp.where(ex.t == 1, hidden, 0.0).astype(BF16)
    b.p0[8:12, 0:640] = jnp.where(rows_of((4, 1)) == me, row, 0.0).astype(BF16)
    counts = jnp.sum(b.chosen[...], axis=0, keepdims=True)
    high = jnp.floor(counts / 64)
    middle = jnp.floor((counts - 64 * high) / 8)
    digits = jnp.concatenate([counts - 64 * high - 8 * middle, middle, high], axis=0)
    b.p0[12:15, 0:128] = digits.astype(BF16)


def prepare(b, ex, x_ref, cot_ref, noise_ref, router_ref, eb_ref, vector_refs):
    rows = b.xs.shape[0]
    for ref, source in ((b.xs, x_ref), (b.cot, cot_ref)):
        ref[rows - 16 : rows] = jnp.zeros((16, ref.shape[1]), BF16)
        ref[0:SEQ] = source[...]
    for i, ref in enumerate(vector_refs):
        b.vec[i : i + 1] = ref[...].astype(F32).reshape(1, -1)
    b.wide8[...] = jnp.full(b.wide8.shape, -1e30, F32)
    b.wide8[0:4, 0:SEQ] = noise_ref[...]
    b.noise[...] = b.wide8[...].T
    for ref, source in ((b.router, router_ref), (b.eb, eb_ref)):
        ref[...] = jnp.zeros_like(ref)
        ref[0:4] = source[...]
    values = b.xs[...].astype(F32)
    normal, _ = normalise(values)
    b.n1[...] = (normal * b.vec[0:1] + b.vec[1:2]).astype(BF16)
    b.res[...] = values + b.vec[4:5]
    earlier = (rows_of((rows, rows)) < lanes((rows, rows))).astype(F32).astype(BF16)
    b.before[...] = nn(b.spread[...].astype(BF16), earlier)

    def one(g, carry):
        e = ex.expert(g)
        slot = rows_of((CAP, rows)).astype(F32)
        served = (row_of(b.before[...], e) == slot) & (row_of(b.spread[...], e) > 0.5)
        b.sel[g] = jnp.where(served, 1.0, 0.0).astype(BF16)
        b.cs[g] = nn(b.sel[g], b.cot[...]).astype(BF16)
        return carry

    lax.fori_loop(0, 4, one, 0)


def attend(b, ex, h):
    rows, wide = b.n1.shape
    low, high = halves()
    alive = lanes((1, rows)) < SEQ
    weight = b.g[h].reshape(wide, wide)
    b.qkv[h] = (nn(b.n1[...], weight[:, 0:640]) + row_of(b.bias[:, 0:640], 8 + ex.shard(h))).astype(BF16)
    parts = []
    ends = jnp.zeros((rows, 128), F32)
    for i, (sq, sk, sv, uq, uv) in enumerate(HEADS_AT):
        query = b.qkv[h, :, 128 * sq : 128 * sq + 128] * (high if uq else low)
        key = b.qkv[h, :, 128 * sk : 128 * sk + 128]
        value = b.qkv[h, :, 128 * sv : 128 * sv + 128] * (high if uv else low)
        scores = jnp.where(alive, SCALE * nt(query, key), -1e30)
        top = jnp.max(scores, axis=-1, keepdims=True)
        raised = jnp.exp(scores - top)
        total = jnp.sum(raised, axis=-1, keepdims=True)
        parts.append(nn((raised / total).astype(BF16), value))
        ends = jnp.where(lanes((1, 128)) == i, top + jnp.log(total), ends)
    b.lse[h] = ends
    first, second = (parts[0] + parts[1]).astype(BF16), parts[2].astype(BF16)
    b.att[h, :, 0:128] = first
    b.att[h, :, 128:256] = second
    b.res[...] += nt(first, weight[:, 640:768]) + nt(second, weight[:, 384:512])


def attend_back(b, ex, h):
    rows, wide = b.n1.shape
    low, high = halves()
    alive = lanes((1, rows)) < SEQ
    weight = b.g[h].reshape(wide, wide)
    branch = b.ig[...].astype(BF16)
    from_first = nn(branch, weight[:, 640:768]).astype(BF16)
    from_second = nn(branch, weight[:, 384:512]).astype(BF16)
    ends = b.lse[h]
    slabs = [None] * 5
    for i, (sq, sk, sv, uq, uv) in enumerate(HEADS_AT):
        mask_q, mask_v = (high if uq else low), (high if uv else low)
        query = b.qkv[h, :, 128 * sq : 128 * sq + 128] * mask_q
        key = b.qkv[h, :, 128 * sk : 128 * sk + 128]
        value = b.qkv[h, :, 128 * sv : 128 * sv + 128]
        grad = (from_first if i < 2 else from_second) * mask_v
        scores = SCALE * nt(query, key)
        weights = jnp.where(alive, jnp.exp(jnp.where(alive, scores - ends[:, i : i + 1], 0.0)), 0.0)
        value_grad = tn(weights.astype(BF16), grad)
        weight_grad = nt(grad, value)
        inner = jnp.sum(weight_grad * weights, axis=-1, keepdims=True)
        score = (weights * (weight_grad - inner)).astype(BF16)
        query_grad = SCALE * nn(score, key * mask_q)
        key_grad = SCALE * tn(score, query)
        for at, part in ((sq, query_grad), (sk, key_grad), (sv, value_grad)):
            slabs[at] = part if slabs[at] is None else slabs[at] + part
    for at, slab in enumerate(slabs):
        low_slab = slab.astype(BF16)
        b.dqkv[:, 128 * at : 128 * at + 128] = low_slab
        b.l0[:, 128 * at : 128 * at + 128] = jnp.where(
            rows_of((8, 1)) == 4 + ex.shard(h),
            jnp.sum(low_slab.astype(F32), axis=0, keepdims=True),
            b.l0[:, 128 * at : 128 * at + 128],
        )
    b.dn1[...] += nt(b.dqkv[...], weight[:, 0:640])
    put = pl.ds(pl.multiple_of(wide * h, wide), wide)
    for at in range(6):
        if at < 5:
            part = nn(b.n1t[...], b.dqkv[:, 128 * at : 128 * at + 128])
            if at == 3:
                part += nn(b.brt[...], b.att[h, :, 128:256])
        else:
            part = nn(b.brt[...], b.att[h, :, 0:128])
        b.hp[put, 128 * at : 128 * at + 128] = part.astype(BF16)


def route(b, ex):
    normal, _ = normalise(b.res[...])
    b.n2[...] = (normal * b.vec[2:3] + b.vec[3:4]).astype(BF16)
    logits = nt(b.n2[...], b.router[...]) + b.noise[...]
    raised = jnp.exp(logits - jnp.max(logits, axis=-1, keepdims=True))
    chances = raised / jnp.sum(raised, axis=-1, keepdims=True)
    b.ch[...] = chances
    for i, part in enumerate(exact_parts(chances)):
        b.chp[i] = part

    def one(g, carry):
        b.cs[g] = nn(b.sel[g], b.n2[...]).astype(BF16)
        gates = nn(b.sel[g], b.chp[0]) + nn(b.sel[g], b.chp[1]) + nn(b.sel[g], b.chp[2])
        gates = jnp.sum(jnp.where(lanes((1, 128)) == ex.expert(g), gates, 0.0), axis=-1, keepdims=True)
        b.gs[g] = jnp.broadcast_to(as_row(gates), (8, CAP))
        return carry

    lax.fori_loop(0, 4, one, 0)


def serve(b, ex, g):
    cap, wide = b.rt.shape[2:]
    units = b.w.shape[3]
    step, tile = 2 * cap, wide // 2
    x = b.rt[g].reshape(step, wide)
    raw = b.rc[g].reshape(step, wide).astype(F32)
    gate = jnp.concatenate([as_column(b.rg[g, 0, 0:1]), as_column(b.rg[g, 1, 0:1])], axis=0)
    at = pl.ds(pl.multiple_of(g * step, step), step)
    b.xt[:, at] = x.T
    b.gt[:, at] = (gate * raw).astype(BF16).T
    b.so[...] = jnp.zeros_like(b.so)
    b.sb[...] = jnp.zeros_like(b.sb)

    def columns(f, carry):
        x = b.rt[g].reshape(step, wide)
        raw = b.rc[g].reshape(step, wide).astype(F32)
        r = (gate * raw).astype(BF16)
        cols = pl.ds(pl.multiple_of(f * tile, tile), tile)
        w_in = b.w[:, 0, :, cols].reshape(wide, tile)
        w_out = b.w[:, 1, :, cols].reshape(wide, tile)
        v = nn(x, w_in) + b.brow[0:1, cols]
        square = v * v
        bend = jnp.tanh(0.7978845608028654 * v * (1.0 + 0.044715 * square))
        hidden = (0.5 * v * (1.0 + bend)).astype(BF16)
        slope = 0.5 * (1.0 + bend) + 0.5 * v * (1.0 - bend * bend) * (
            0.7978845608028654 * (1.0 + 3 * 0.044715 * square)
        )
        low = (nn(r, w_out) * slope).astype(BF16)
        here = pl.ds(pl.multiple_of((f // 2) * 8 * cap + g * step, step), step)
        there = pl.ds(pl.multiple_of((2 + f // 2) * 8 * cap + g * step, step), step)
        within = pl.ds(pl.multiple_of((f % 2) * tile, tile), tile)
        b.hp[here, within] = hidden
        b.hp[there, within] = low
        b.db[0:1, cols] += jnp.sum(low.astype(F32), axis=0, keepdims=True)
        b.so[...] += nt(hidden, w_out)
        b.sb[...] += nt(low, w_in)
        return carry

    lax.fori_loop(0, units // tile, columns, 0)
    b.yo[g] = b.so[...].astype(BF16).reshape(2, cap, wide)
    b.yx[g] = b.sb[...].astype(BF16).reshape(2, cap, wide)
    told = jnp.sum(raw * b.so[...], axis=-1, keepdims=True)
    b.yg[g, 0] = jnp.broadcast_to(as_row(told[0:cap]), (8, cap))
    b.yg[g, 1] = jnp.broadcast_to(as_row(told[cap:step]), (8, cap))


def weight_grads(b, half):
    rows, slots = b.xt.shape[0] // 2, b.xt.shape[1]

    def one(f, carry):
        cols = pl.ds(pl.multiple_of(f * 256, 256), 256)
        shape = (8, b.w.shape[2], 256)
        take = pl.ds(pl.multiple_of(half * rows, rows), rows)
        put = pl.ds(8 * half, 8)
        within = pl.ds(pl.multiple_of((f % 3) * 256, 256), 256)
        hidden = b.hp[pl.ds(pl.multiple_of((f // 3) * slots, slots), slots), within]
        before = b.hp[pl.ds(pl.multiple_of((2 + f // 3) * slots, slots), slots), within]
        b.w[put, 0, :, cols] = nn(b.xt[take], before).astype(BF16).reshape(shape)
        b.w[put, 1, :, cols] = nn(b.gt[take], hidden).astype(BF16).reshape(shape)
        return carry

    lax.fori_loop(0, b.w.shape[3] // 256, one, 0)


def back_to_branch(b, ex, total_tokens):
    chances, chosen = b.ch[...], b.chosen[...]
    b.told[...] = chosen * nt(b.cot[...], b.eb[...])
    b.dn1[...] = jnp.zeros_like(b.dn1)

    def one(g, carry):
        select = b.sel[g]
        b.dn1[...] += tn(select, b.bx[g])
        gate = jnp.where(lanes((1, 128)) == ex.expert(g), as_column(b.bg[g, 0:1]), 0.0)
        first, second, third = exact_parts(gate)
        b.told[...] += tn(select, first) + tn(select, second) + tn(select, third)
        return carry

    lax.fori_loop(0, 4, one, 0)
    chance_grad = b.told[...] + b.bias[15:16, 0:128] * (4.0 / (2.0 * total_tokens * total_tokens))
    logit_grad = chances * (chance_grad - jnp.sum(chances * chance_grad, axis=-1, keepdims=True))
    living = rows_of((b.n1.shape[0], 1)) < SEQ
    logit_low = jnp.where(living, logit_grad, 0.0).astype(BF16)
    b.e0[...] = jnp.zeros_like(b.e0)
    b.e0[3:4, 0:128] = jnp.sum(jnp.where(living, chances, 0.0), axis=0, keepdims=True)
    b.e0[4:8] = tn(logit_low, b.n2[...])[0:4]
    normal, inverse = normalise(b.res[...])
    dn2 = b.dn1[...] + nn(logit_low, b.router[...])
    b.e0[0:1] = jnp.sum(dn2 * normal, axis=0, keepdims=True)
    b.e0[1:2] = jnp.sum(dn2, axis=0, keepdims=True)
    b.ig[...] = b.cot[...].astype(F32) + norm_back(dn2 * b.vec[2:3], normal, inverse)
    branch = b.ig[...].astype(BF16)
    b.e0[2:3] = jnp.sum(branch.astype(F32), axis=0, keepdims=True)
    for e in range(4):
        gate = (chances * chosen)[:, e : e + 1]
        b.e0[8 + e : 9 + e] = jnp.sum(
            (gate * b.cot[...].astype(F32)).astype(BF16).astype(F32), axis=0, keepdims=True
        )
    b.n1t[...] = b.n1[...].T
    b.brt[...] = branch.T
    b.dn1[...] = jnp.zeros_like(b.dn1)
    b.l0[...] = jnp.zeros_like(b.l0)


def combine(b, ex, out_ref):
    gates = b.ch[...] * b.chosen[...]
    first, second, third = exact_parts(gates)
    b.res[...] += nn(first, b.eb[...]) + nn(second, b.eb[...]) + nn(third, b.eb[...])

    def one(g, carry):
        gates = b.ch[...] * b.chosen[...]
        gate = jnp.sum(jnp.where(lanes((1, 128)) == ex.expert(g), gates, 0.0), axis=-1, keepdims=True)
        b.res[...] += gate * tn(b.sel[g], b.bo[g])
        return carry

    lax.fori_loop(0, 4, one, 0)
    out_ref[...] = b.res[0:SEQ]


def shard_rows(h, z=0, y=0, rows=768):
    return pl.ds(pl.multiple_of(768 * h + 192 * z + 96 * y, 96), rows)


def add_into(ref, *others):
    total = ref[...].astype(F32)
    for other in others:
        total += other[...].astype(F32)
    ref[...] = total.astype(ref.dtype)


def block_kernel(total_tokens, plan, *refs):
    inputs, outputs, (send_sems, recv_sems) = refs[:17], refs[17:26], refs[26:28]
    x_ref, cot_ref, ids_ref, noise_ref, router_ref, eb_ref = inputs[:6]
    out_ref, ig_ref, og_ref, hw_ref, mg_ref, early_ref, late_ref, hb_ref, ib_ref = outputs
    b = Buffers()
    for (name, _, _), ref in zip(plan, refs[28:], strict=True):
        setattr(b, name, ref)
    ex = Exchange(send_sems, recv_sems)
    d, x, c, t = ex.d, ex.x, ex.c, ex.t
    zh, zl = ex.zh, ex.zl
    pack(b, ex, inputs[11:15])
    small_operands(b, ex, ids_ref, inputs[15], inputs[16])
    tiny = SumOverAll(ex, b.p0, b.psum, b.pgot)
    ex.meet()

    fz, fp, fc = ex.slots(3), ex.slots(12), ex.slots(16)

    def slot(r, j, pt):
        return b.g.at[j, ex.zs[r], pt]

    shards = ((2, 0), (3, 1), (2, 0), (3, 1))

    def spread_shard(r):
        here = slot(r, 3, t)
        for j in range(3):
            ex.send(fp + 4 * j + r, here, slot(r, shards[j][0], t), ex.across[j])
        ex.send(fc + 12 + r, here, slot(r, 1, t), ex.mate)

    own = slot(0, 3, t)
    ex.send(fz, own, own, ex.along[0])
    ex.send(fz + 1, own, own, ex.along[1])
    spread_shard(0)
    tiny.start()

    ez, exx, ec = ex.slots(6), ex.slots(2), ex.slots(8)

    def part(r, px, pc):
        return b.w.at[4 * ex.zs[r] + 2 * px + pc]

    for r in (1, 3, 2):
        ex.send(ez + 2 * (r - 1), b.wp.at[2 * (ex.zs[r] % 2) + x], part(0, x, c), ex.along[r - 1])
    prepare(b, ex, x_ref, cot_ref, noise_ref, router_ref, eb_ref, inputs[6:11])
    here = slot(1, 3, t)
    ex.arrived(fz, here)
    ex.send(fz + 2, here, here, ex.along[1])
    spread_shard(1)
    for r in (2, 3):
        ex.arrived(fz + r - 1, slot(r, 3, t))
        spread_shard(r)
    tiny.to_plane()
    ct, cy = ex.slots(4), ex.slots(4)
    for r in range(4):
        for j, (_, pt) in enumerate(ex.plane):
            here = slot(r, shards[j][0], pt)
            ex.arrived(fp + 4 * j + r, here)
            ex.send(fc + 4 * j + r, here, slot(r, shards[j][1], pt), ex.mate)
        if r == 1:
            tiny.to_half()
            ex.send(exx, b.wp.at[2 * zl + 1 - x], part(0, x, c), ex.across[0])
            ex.send(exx + 1, b.wp.at[2 * (1 - zl) + 1 - x], b.xb, ex.across[0])
        if r == 2:
            tiny.to_pair()
            for g in (1, 2, 3):
                ex.send(ct + g, b.cs.at[g], b.rc.at[g, 0], ex.holder(g))
    ex.send(cy, b.cs.at[0], b.rc.at[0, 1], ex.other_y)
    ex.send(ec, part(0, x, c), part(0, x, c), ex.mate)
    b.rc[0, 0] = b.cs[0]
    b.bias[...] = tiny.result()
    b.bias[15:16, 0:128] = (
        b.bias[12:13, 0:128] + 8 * b.bias[13:14, 0:128] + 64 * b.bias[14:15, 0:128]
    )
    b.brow[0:1] = row_of(b.bias[...], 4 * t + ex.expert(0))
    for r in range(4):
        for j, (_, pt) in enumerate(ex.plane + ((x, t),)):
            ex.arrived(fc + 4 * j + r, slot(r, shards[j][1], pt))

    def forward_head(h, carry):
        attend(b, ex, h)

        @pl.when(h == 0)
        def _():
            ex.arrived(exx, part(0, 1 - x, c))
            ex.arrived(exx + 1, b.xb)
            for r in (1, 3, 2):
                source = part(0, 1 - x, c) if r == 1 else b.xb
                ex.send(ez + 2 * (r - 1) + 1, source, part(0, 1 - x, c), ex.along[r - 1])
            ex.send(ec + 1, part(0, 1 - x, c), part(0, 1 - x, c), ex.mate)

        @pl.when(h == 1)
        def _():
            for g in (1, 2, 3):
                ex.arrived(ct + g, b.rc.at[g, 0])
                ex.send(cy + g, b.rc.at[g, 0], b.rc.at[g, 1], ex.other_y)

        return carry

    lax.fori_loop(0, 4, forward_head, 0)
    for g in (1, 2, 3):
        ex.sent(ct + g, b.cs.at[0])
    ex.sent(cy, b.cs.at[0])
    route(b, ex)

    tt, ty, gt, gy = ex.slots(4), ex.slots(4), ex.slots(4), ex.slots(4)
    for g in (1, 2, 3):
        ex.send(tt + g, b.cs.at[g], b.rt.at[g, 0], ex.holder(g))
        ex.send(gt + g, b.gs.at[g], b.rg.at[g, 0], ex.holder(g))
    ex.send(ty, b.cs.at[0], b.rt.at[0, 1], ex.other_y)
    ex.send(gy, b.gs.at[0], b.rg.at[0, 1], ex.other_y)
    b.rt[0, 0] = b.cs[0]
    b.rg[0, 0] = b.gs[0]
    for r in (1, 2, 3):
        here = part(r, x, c)
        ex.arrived(ez + 2 * (r - 1), here)
        ex.send(ec + 2 * r, here, here, ex.mate)
    for g in (1, 2, 3):
        ex.arrived(tt + g, b.rt.at[g, 0])
        ex.send(ty + g, b.rt.at[g, 0], b.rt.at[g, 1], ex.other_y)
        ex.arrived(gt + g, b.rg.at[g, 0])
        ex.send(gy + g, b.rg.at[g, 0], b.rg.at[g, 1], ex.other_y)
    for r in (1, 2, 3):
        here = part(r, 1 - x, c)
        ex.arrived(ez + 2 * (r - 1) + 1, here)
        ex.send(ec + 2 * r + 1, here, here, ex.mate)
    for g in range(4):
        ex.arrived(cy + g, b.rc.at[g, 1])
        ex.arrived(ty + g, b.rt.at[g, 1])
        ex.arrived(gy + g, b.rg.at[g, 1])
    for r in range(4):
        for i, px in enumerate((x, 1 - x)):
            ex.arrived(ec + 2 * r + i, part(r, px, 1 - c))
    b.db[...] = jnp.zeros_like(b.db)

    yx, yg, yo = ex.slots(4), ex.slots(4), ex.slots(4)
    hx, hg, ho = ex.slots(4), ex.slots(4), ex.slots(4)

    def serve_blocks(g, carry):
        serve(b, ex, g)
        ex.send(yx + g, b.yx.at[g, 1], b.gotx.at[g], ex.other_y)
        ex.send(yg + g, b.yg.at[g, 1], b.gotg.at[g], ex.other_y)
        return carry

    lax.fori_loop(0, 4, serve_blocks, 0)

    def give_back(g, carry):
        ex.arrived(yx + g, b.gotx.at[g])
        ex.arrived(yg + g, b.gotg.at[g])
        add_into(b.yx.at[g, 0], b.gotx.at[g])
        add_into(b.yg.at[g, 0], b.gotg.at[g])

        @pl.when(g > 0)
        def _():
            ex.send(hx + g, b.yx.at[g, 0], b.bx.at[g], ex.holder(g))
            ex.send(hg + g, b.yg.at[g, 0], b.bg.at[g], ex.holder(g))

        return carry

    lax.fori_loop(0, 3, give_back, 0)
    b.bx[0] = b.yx[0, 0]
    b.bg[0] = b.yg[0, 0]
    for k in range(6):
        ex.sent(ez + k, b.xb)
    ex.sent(exx, b.xb)
    ex.sent(exx + 1, b.xb)
    for k in range(8):
        ex.sent(ec + k, b.xb)

    kc, kz, ko = ex.slots(8), ex.slots(4), ex.slots(4)

    def rows_at(half, i, pc):
        return 4 * (2 * half + i // 2) + 2 * (i % 2) + pc

    def to_mate(base, half):
        for i in range(4):
            ex.send(kc + base + i, b.w.at[rows_at(half, i, 1 - c)], b.gotc.at[base + i], ex.mate)

    weight_grads(b, 1 - zh)
    to_mate(0, 1 - zh)
    give_back(3, 0)
    for g in range(4):
        ex.send(yo + g, b.yo.at[g, 1], b.goto.at[g], ex.other_y)

    def to_other_half(i, carry):
        ex.arrived(kc + i, b.gotc.at[i])
        at = rows_at(1 - zh, i, c)
        add_into(b.w.at[at], b.gotc.at[i])
        ex.send(kz + i, b.w.at[at], b.gotz.at[i], ex.along[0])
        return carry

    lax.fori_loop(0, 4, to_other_half, 0)
    weight_grads(b, zh)
    to_mate(4, zh)
    for g in (1, 2, 3):
        ex.arrived(hx + g, b.bx.at[g])
        ex.arrived(hg + g, b.bg.at[g])
    back_to_branch(b, ex, total_tokens)
    sums = SumOverAll(ex, b.e0, b.esum, b.egot)
    sums.start()

    db = ex.slots(5)
    for i in range(b.db.shape[1] // 128):
        b.d0[0, i : i + 1] = b.db[0:1, 128 * i : 128 * i + 128]
    ex.send(db, b.d0.at[0], b.dgot.at[0], ex.mate)

    def own_half(i, carry):
        ex.arrived(kc + 4 + i, b.gotc.at[4 + i])
        add_into(b.w.at[rows_at(zh, i, c)], b.gotc.at[4 + i])
        return carry

    lax.fori_loop(0, 4, own_half, 0)

    sm, sp, sz = ex.slots(2), ex.slots(12), ex.slots(3)

    def merge_core(i):
        ex.arrived(sm + i, b.gotm.at[i])

        h = 2 + i
        for r in (3, 2, 1, 0):
            z = ex.zs[r]
            add_into(b.hp.at[shard_rows(h, z, 0, 192)], b.gotm.at[i, shard_rows(0, z, 0, 192)])
            for j in (0, 2) if i == 0 else (1,):
                ex.send(
                    sp + 4 * j + r,
                    b.hp.at[shard_rows(h, z, ex.plane[j][1], 96)],
                    b.gotp.at[j, r],
                    ex.across[j],
                )

    def backward_head(j, carry):
        attend_back(b, ex, j)

        @pl.when(j < 2)
        def _():
            ex.send(sm + j, b.hp.at[shard_rows(j)], b.gotm.at[j], ex.mate)

        @pl.when(j == 0)
        def _():
            sums.to_plane()
            ex.arrived(db, b.dgot.at[0])
            b.d0[1] = b.d0[0] + b.dgot[0]
            ex.send(db + 1, b.d0.at[1], b.dgot.at[1], ex.along[0])

        @pl.when(j == 1)
        def _():
            def one(g, carry):
                ex.arrived(yo + g, b.goto.at[g])
                add_into(b.yo.at[g, 0], b.goto.at[g])

                @pl.when(g > 0)
                def _():
                    ex.send(ho + g, b.yo.at[g, 0], b.bo.at[g], ex.holder(g))

                return carry

            lax.fori_loop(0, 4, one, 0)
            b.bo[0] = b.yo[0, 0]
            sums.to_half()

        @pl.when(j == 2)
        def _():
            merge_core(0)
            ex.arrived(db + 1, b.dgot.at[1])
            b.d0[2] = b.d0[1] + b.dgot[1]
            for g in (1, 2, 3):
                ex.send(db + 1 + g, b.d0.at[2], b.dgot.at[1 + g], ex.holder(g))
            sums.to_pair()

        return carry

    lax.fori_loop(0, 4, backward_head, 0)
    merge_core(1)
    first_grad = b.dn1[...]
    normal, inverse = normalise(b.xs[...].astype(F32))
    b.l0[0:1] = jnp.sum(first_grad * normal, axis=0, keepdims=True)
    b.l0[1:2] = jnp.sum(first_grad, axis=0, keepdims=True)
    late = SumOverAll(ex, b.l0, b.lsum, b.lgot)
    late.start()
    ig_ref[...] = (b.ig[...] + norm_back(first_grad * b.vec[0:1], normal, inverse))[0:SEQ]
    late.to_plane()
    for g in (1, 2, 3):
        ex.arrived(ho + g, b.bo.at[g])
    combine(b, ex, out_ref)
    home = 2 * x + c
    for r in (3, 2, 1, 0):
        for j in range(3):
            ex.arrived(sp + 4 * j + r, b.gotp.at[j, r])
        mine = b.hp.at[shard_rows(3, ex.zs[r], t, 96)]
        add_into(mine, b.gotp.at[0, r], b.gotp.at[1, r], b.gotp.at[2, r])
        if r >= 2:
            ex.send(sz + r - 2, mine, b.gots.at[r - 2], ex.along[1])
    late.to_half()
    ex.arrived(sz + 1, b.gots.at[1])
    mine = b.hp.at[shard_rows(3, ex.zs[1], t, 96)]
    add_into(mine, b.gots.at[1])
    ex.send(sz + 2, mine, b.gots.at[2], ex.along[0])
    late.to_pair()

    def to_owner(i, carry):
        g = 3 - i
        z, px = ex.group(g)
        got = 2 * (z % 2) + px
        ex.arrived(kz + got, b.gotz.at[got])
        at = 4 * z + 2 * px + c
        add_into(b.w.at[at], b.gotz.at[got])

        @pl.when(g > 0)
        def _():
            ex.send(ko + g, b.w.at[at], og_ref.at[ex.expert(0)], ex.holder(g))

        return carry

    lax.fori_loop(0, 4, to_owner, 0)
    og_ref[ex.expert(0)] = b.w[4 * d + home]
    totals = sums.result()
    early_ref[...] = totals
    share = b.bias[15:16, 0:128] / (2.0 * total_tokens)
    balance = 4.0 * jnp.sum(share * (totals[3:4, 0:128] / total_tokens), axis=-1, keepdims=True)
    early_ref[3:4, 0:128] = jnp.broadcast_to(balance, (1, 128))
    units = b.db.shape[1]
    hidden_rows = jnp.zeros((8, units), F32)
    for g in range(4):
        if g:
            ex.arrived(db + 1 + g, b.dgot.at[1 + g])
        source = b.dgot.at[1 + g] if g else b.d0.at[2]
        line = jnp.concatenate([source[i : i + 1] for i in range(units // 128)], axis=1)
        hidden_rows = jnp.where(rows_of((8, 1)) == ex.expert(g), line, hidden_rows)
    select = hidden_lanes(ex, units)
    ib_ref[...] = sum(nt(part_of, select) for part_of in exact_parts(hidden_rows))[0:4]
    late_sum = late.result()
    late_ref[...] = late_sum
    heads, kind = bias_lanes(ex)
    row = row_of(late_sum, 4 + home)[:, 0:640]
    rows = jnp.concatenate([jnp.where(kind == 0, row, 0.0), jnp.where(kind == 1, row, 0.0)], axis=0)
    hb_ref[...] = sum(nt(part_of, heads) for part_of in exact_parts(rows))
    ex.arrived(sz, b.gots.at[0])
    ex.arrived(sz + 2, b.gots.at[2])
    shard = b.hp[shard_rows(3, d, t, 96)].astype(F32) + b.gots[0].astype(F32) + b.gots[2].astype(F32)
    for k, (whole, lane) in enumerate(((0, 256), (128, 384), (512, 320))):
        hw_ref[k, :, 0:128] = shard[:, whole : whole + 128]
        hw_ref[k, :, 128:192] = shard[:, lane : lane + 64]
    mg_ref[...] = jnp.concatenate([shard[:, 640:768], shard[:, 448:512]], axis=1).T
    for g in (1, 2, 3):
        ex.arrived(ko + g, og_ref.at[ex.expert(g)])
    for sum_of in (tiny, sums, late):
        sum_of.done()
    for k in range(3):
        ex.sent(fz + k, b.a)
        ex.sent(sz + k, b.a)
    for k in range(12):
        ex.sent(fp + k, b.a)
        ex.sent(sp + k, b.a)
    for k in range(16):
        ex.sent(fc + k, b.a)
    for g in range(4):
        for base in (ty, yx, yo):
            ex.sent(base + g, b.cs.at[0])
        for base in (gy, yg):
            ex.sent(base + g, b.gs.at[0])
        ex.sent(kz + g, b.xb)
    for g in (1, 2, 3):
        for base in (cy, tt, hx, ho):
            ex.sent(base + g, b.cs.at[0])
        for base in (gt, hg):
            ex.sent(base + g, b.gs.at[0])
        ex.sent(ko + g, b.xb)
    for k in range(8):
        ex.sent(kc + k, b.xb)
    for k in range(5):
        ex.sent(db + k, b.dgot.at[0])
    for i in range(2):
        ex.sent(sm + i, b.gotm.at[0])
    assert ex.used <= COPIES


COPIES = 192


def staged_body(
    inputs,
    first_gain,
    first_bias,
    head_weight,
    head_bias,
    merge_weight,
    merge_bias,
    second_gain,
    second_bias,
    router,
    router_noise,
    expert_ids,
    expert_in,
    expert_in_bias,
    expert_out,
    expert_out_bias,
    cotangent,
):
    tok_rows, wide = inputs.shape
    experts, _, units = expert_in.shape
    total_tokens = tok_rows * lax.axis_size(("dp", "heads", "tensor"))
    plan = scratch_plan(wide, units, ROWS)
    output, input_grad, expert_grads, head_grad, merge_grad, early, late, head_bias_grad, in_bias_grad = (
        pl.pallas_call(
            functools.partial(block_kernel, float(total_tokens), plan),
            out_shape=(
                jax.ShapeDtypeStruct((tok_rows, wide), F32),
                jax.ShapeDtypeStruct((tok_rows, wide), F32),
                jax.ShapeDtypeStruct((experts, 2) + expert_in.shape[1:], BF16),
                jax.ShapeDtypeStruct(head_weight.shape, F32),
                jax.ShapeDtypeStruct(merge_weight.shape, F32),
                jax.ShapeDtypeStruct((16, wide), F32),
                jax.ShapeDtypeStruct((8, wide), F32),
                jax.ShapeDtypeStruct(head_bias.shape, F32),
                jax.ShapeDtypeStruct(expert_in_bias.shape, F32),
            ),
            in_specs=[VM] * 17,
            out_specs=(VM,) * 9,
            scratch_shapes=[pltpu.SemaphoreType.DMA((COPIES,))] * 2
            + [pltpu.VMEM(shape, kind) for _, shape, kind in plan],
            compiler_params=pltpu.CompilerParams(
                collective_id=0, has_side_effects=True, vmem_limit_bytes=60 * MIB
            ),
            name="block",
        )(
            inputs,
            cotangent,
            expert_ids.T,
            router_noise.T,
            router.T,
            expert_out_bias,
            first_gain,
            first_bias,
            second_gain,
            second_bias,
            merge_bias,
            head_weight,
            merge_weight,
            expert_in,
            jnp.transpose(expert_out, (0, 2, 1)),
            head_bias,
            expert_in_bias,
        )
    )
    return (
        output,
        early[3, 0],
        input_grad,
        late[0],
        late[1],
        head_grad,
        head_bias_grad,
        merge_grad,
        early[2],
        early[0],
        early[1],
        early[4:8].T,
        expert_grads[:, 0].astype(F32),
        in_bias_grad,
        jnp.transpose(expert_grads[:, 1], (0, 2, 1)).astype(F32),
        early[8:12],
    )


def layer_norm(values, factor, offset):
    average = jnp.mean(values, axis=-1, keepdims=True)
    centred = values - average
    spread = jnp.mean(centred * centred, axis=-1, keepdims=True)
    return centred * lax.rsqrt(spread + 1e-06) * factor + offset


def expert_weights(expert_in, expert_out, expert_in_bias):
    return (
        lax.all_gather(expert_in, ("dp", "heads"), axis=1, tiled=True),
        lax.all_gather(expert_out, ("dp", "heads"), axis=2, tiled=True),
        lax.all_gather(expert_in_bias, ("dp", "heads"), axis=1, tiled=True),
    )


def plain_body(
    inputs,
    first_gain,
    first_bias,
    head_weight,
    head_bias,
    merge_weight,
    merge_bias,
    second_gain,
    second_bias,
    router,
    router_noise,
    expert_ids,
    expert_in,
    expert_in_bias,
    expert_out,
    expert_out_bias,
    cotangent,
):
    tok_rows = inputs.shape[0]
    features = inputs.shape[1]
    experts = expert_in.shape[0]
    head_cols = head_weight.shape[2]
    heads_local = head_cols // HEAD_DIM
    total_tokens = tok_rows * lax.axis_size(("dp", "heads", "tensor"))
    scale = HEAD_DIM ** (-0.5)
    whole_head, whole_merge, whole_bias = (
        lax.all_gather(head_weight, ("dp", "tensor"), axis=1, tiled=True),
        lax.all_gather(merge_weight, ("dp", "tensor"), axis=1, tiled=True),
        lax.all_gather(head_bias, ("dp", "tensor"), axis=1, tiled=True),
    )
    residual_in = inputs.astype(jnp.float32)
    normed, norm_back = jax.vjp(
        layer_norm, residual_in, first_gain.astype(jnp.float32), first_bias.astype(jnp.float32)
    )
    group_rows = lax.all_gather(normed.astype(jnp.bfloat16), "heads", axis=0, tiled=True)
    group_count = group_rows.shape[0]
    group_images = group_count // SEQ
    projected = jnp.einsum(
        "gd,jdc->jgc", group_rows, whole_head, preferred_element_type=jnp.float32
    )
    bias_values = whole_bias.astype(jnp.float32)
    query_low = (projected[0] + bias_values[0]).astype(jnp.bfloat16)
    key_low = projected[1].astype(jnp.bfloat16)
    value_low = (projected[2] + bias_values[1]).astype(jnp.bfloat16)

    def shaped(array):
        return array.reshape(group_images, SEQ, heads_local, HEAD_DIM)

    query_img, key_img, value_img = (shaped(query_low), shaped(key_low), shaped(value_low))
    scores = scale * jnp.einsum(
        "ishd,ithd->ihst", query_img, key_img, preferred_element_type=jnp.float32
    )
    top_score = jnp.max(scores, axis=-1, keepdims=True)
    raised = jnp.exp(scores - top_score)
    row_total = jnp.sum(raised, axis=-1, keepdims=True)
    weights = raised / row_total
    log_total = top_score + jnp.log(row_total)
    attended = jnp.einsum(
        "ihst,ithd->ishd",
        weights.astype(jnp.bfloat16),
        value_img,
        preferred_element_type=jnp.float32,
    )
    attended_low = attended.reshape(group_count, head_cols).astype(jnp.bfloat16)
    segment = attended_low
    branch = lax.psum_scatter(
        jnp.dot(segment, whole_merge, preferred_element_type=jnp.float32).astype(jnp.bfloat16),
        "heads",
        scatter_dimension=0,
        tiled=True,
    ).astype(jnp.float32) + merge_bias.astype(jnp.float32)
    residual = residual_in + branch
    normed_two, norm_two_back = jax.vjp(
        layer_norm, residual, second_gain.astype(jnp.float32), second_bias.astype(jnp.float32)
    )
    second_low = normed_two.astype(jnp.bfloat16)
    router_logits = jnp.dot(second_low, router, preferred_element_type=jnp.float32) + router_noise
    chances = jax.nn.softmax(router_logits, axis=-1)
    expert_range = jnp.arange(experts, dtype=jnp.int32)
    chosen_pair = (expert_ids[:, :, None] == expert_range).astype(jnp.int32)
    chosen = jnp.sum(chosen_pair, axis=1)
    order = jnp.arange(tok_rows, dtype=jnp.int32)
    earlier = (order[None, :] < order[:, None]).astype(jnp.bfloat16)
    before = jnp.dot(
        earlier, chosen.astype(jnp.bfloat16), preferred_element_type=jnp.float32
    ).astype(jnp.int32)
    slot_ids = jnp.take_along_axis(before, expert_ids, axis=1)
    flat_rows = (slot_ids * experts + expert_ids).reshape(-1)
    picks = chosen_pair.astype(jnp.float32)
    count_terms = jnp.sum(chosen.astype(jnp.float32), axis=0)
    chance_terms = jnp.sum(chances, axis=0)
    count_all, chance_all = lax.psum((count_terms, chance_terms), ("dp", "heads", "tensor"))
    load_share = count_all / (2 * total_tokens)
    balance_loss = experts * jnp.sum(load_share * chance_all / total_tokens)
    gate_values = jnp.sum(picks * chances[:, None, :], axis=2)
    doubled = jnp.repeat(second_low, 2, axis=0)
    own_buffer = jnp.zeros((CAP * experts, features), jnp.bfloat16).at[flat_rows].set(doubled)
    pair_buffer = lax.all_gather(
        own_buffer.reshape(CAP, experts, features), "tensor", axis=0, tiled=True
    )
    weight_in, weight_out, bias_in = expert_weights(expert_in, expert_out, expert_in_bias)
    before_act = (
        jnp.einsum("ced,edf->cef", pair_buffer, weight_in, preferred_element_type=jnp.float32)
        + bias_in.astype(jnp.float32)[None, :, :]
    )
    activated, gelu_back = jax.vjp(jax.nn.gelu, before_act)
    activated_low = activated.astype(jnp.bfloat16)
    partial_out = jnp.einsum(
        "cef,efd->ced", activated_low, weight_out, preferred_element_type=jnp.float32
    )
    own_out = (
        lax.psum_scatter(
            partial_out.astype(jnp.bfloat16), "tensor", scatter_dimension=0, tiled=True
        ).astype(jnp.float32)
        + expert_out_bias.astype(jnp.float32)[None, :, :]
    )
    picked = own_out.reshape(CAP * experts, features)[flat_rows].reshape(tok_rows, 2, features)
    output = residual + jnp.sum(gate_values[:, :, None] * picked, axis=1)
    incoming = cotangent.astype(jnp.float32)
    gate_grad = jnp.sum(incoming[:, None, :] * picked, axis=2)
    slot_grad = (
        (gate_values[:, :, None] * incoming[:, None, :])
        .astype(jnp.bfloat16)
        .reshape(tok_rows * 2, features)
    )
    own_slot_grad = (
        jnp.zeros((CAP * experts, features), jnp.bfloat16)
        .at[flat_rows]
        .set(slot_grad)
        .reshape(CAP, experts, features)
    )
    out_bias_grad = jnp.sum(own_slot_grad, axis=0, dtype=jnp.float32)
    pair_grad = lax.all_gather(own_slot_grad, "tensor", axis=0, tiled=True)
    back_in, back_out, unused_bias = expert_weights(expert_in, expert_out, expert_in_bias)
    hidden_grad = jnp.einsum(
        "ced,efd->cef", pair_grad, back_out, preferred_element_type=jnp.float32
    )
    pre_grad = gelu_back(hidden_grad)[0].astype(jnp.bfloat16)
    out_grad_rows = jnp.einsum(
        "cef,ced->def", activated_low, pair_grad, preferred_element_type=jnp.float32
    )
    in_grad_rows = jnp.einsum(
        "ced,cef->def", pair_buffer, pre_grad, preferred_element_type=jnp.float32
    )
    in_bias_rows = jnp.sum(pre_grad, axis=0, dtype=jnp.float32).T
    in_grad_rows, out_grad_rows, in_bias_rows = (
        lax.psum_scatter(in_grad_rows, ("dp", "heads"), scatter_dimension=0, tiled=True),
        lax.psum_scatter(out_grad_rows, ("dp", "heads"), scatter_dimension=0, tiled=True),
        lax.psum_scatter(in_bias_rows, ("dp", "heads"), scatter_dimension=0, tiled=True),
    )
    expert_in_grad = jnp.transpose(in_grad_rows, (1, 0, 2))
    expert_out_grad = jnp.transpose(out_grad_rows, (1, 2, 0))
    in_bias_grad = in_bias_rows.T
    buffer_grad = jnp.einsum("cef,edf->ced", pre_grad, back_in, preferred_element_type=jnp.float32)
    own_buffer_grad = (
        lax.psum_scatter(
            buffer_grad.astype(jnp.bfloat16), "tensor", scatter_dimension=0, tiled=True
        )
        .astype(jnp.float32)
        .reshape(CAP * experts, features)
    )
    second_grad = jnp.sum(own_buffer_grad[flat_rows].reshape(tok_rows, 2, features), axis=1)
    chance_grad = (
        jnp.sum(picks * gate_grad[:, :, None], axis=1) + experts * load_share / total_tokens
    )
    logit_grad = chances * (chance_grad - jnp.sum(chances * chance_grad, axis=-1, keepdims=True))
    logit_low = logit_grad.astype(jnp.bfloat16)
    router_grad = lax.dot_general(
        second_low, logit_low, (((0,), (0,)), ((), ())), preferred_element_type=jnp.float32
    )
    second_grad = second_grad + jnp.dot(logit_low, router.T, preferred_element_type=jnp.float32)
    resid_part, gain_two_grad, bias_two_grad = norm_two_back(second_grad)
    resid_grad = incoming + resid_part
    branch_low = resid_grad.astype(jnp.bfloat16)
    merge_bias_grad = jnp.sum(branch_low, axis=0, dtype=jnp.float32)
    group_grad = lax.all_gather(branch_low, "heads", axis=0, tiled=True)
    merge_rows_grad = lax.dot_general(
        group_grad, attended_low, (((0,), (0,)), ((), ())), preferred_element_type=jnp.float32
    )
    attended_grad = shaped(
        jnp.dot(group_grad, whole_merge.T, preferred_element_type=jnp.float32).astype(jnp.bfloat16)
    )
    weights_again = jnp.exp(
        scale
        * jnp.einsum("ishd,ithd->ihst", query_img, key_img, preferred_element_type=jnp.float32)
        - log_total
    )
    value_grad = jnp.einsum(
        "ihst,ishd->ithd",
        weights_again.astype(jnp.bfloat16),
        attended_grad,
        preferred_element_type=jnp.float32,
    )
    weight_grad = jnp.einsum(
        "ishd,ithd->ihst", attended_grad, value_img, preferred_element_type=jnp.float32
    )
    inner_sum = jnp.sum(weight_grad * weights_again, axis=-1, keepdims=True)
    score_low = (weights_again * (weight_grad - inner_sum)).astype(jnp.bfloat16)
    query_grad = scale * jnp.einsum(
        "ihst,ithd->ishd", score_low, key_img, preferred_element_type=jnp.float32
    )
    key_grad = scale * jnp.einsum(
        "ihst,ishd->ithd", score_low, query_img, preferred_element_type=jnp.float32
    )
    triple_low = jnp.stack(
        [
            query_grad.reshape(group_count, head_cols),
            key_grad.reshape(group_count, head_cols),
            value_grad.reshape(group_count, head_cols),
        ],
        axis=0,
    ).astype(jnp.bfloat16)
    head_rows_grad = jnp.einsum(
        "gd,jgc->djc", group_rows, triple_low, preferred_element_type=jnp.float32
    )
    head_bias_rows = jnp.sum(triple_low[0::2], axis=1, dtype=jnp.float32).T
    segment = triple_low
    first_grad = lax.psum_scatter(
        jnp.einsum("jgc,jdc->gd", segment, whole_head, preferred_element_type=jnp.float32).astype(
            jnp.bfloat16
        ),
        "heads",
        scatter_dimension=0,
        tiled=True,
    ).astype(jnp.float32)
    input_part, gain_one_grad, bias_one_grad = norm_back(first_grad)
    input_grad = resid_grad + input_part
    head_rows_grad, merge_rows_grad, head_bias_rows = (
        lax.psum_scatter(head_rows_grad, ("dp", "tensor"), scatter_dimension=0, tiled=True),
        lax.psum_scatter(merge_rows_grad, ("dp", "tensor"), scatter_dimension=0, tiled=True),
        lax.psum_scatter(head_bias_rows, ("dp", "tensor"), scatter_dimension=0, tiled=True),
    )
    head_weight_grad = jnp.transpose(head_rows_grad, (1, 0, 2))
    merge_grad = merge_rows_grad.T
    head_bias_grad = head_bias_rows.T
    small = lax.psum(
        (
            gain_one_grad,
            bias_one_grad,
            gain_two_grad,
            bias_two_grad,
            merge_bias_grad,
            router_grad,
            out_bias_grad,
        ),
        ("dp", "heads", "tensor"),
    )
    return (
        output,
        balance_loss,
        input_grad,
        small[0],
        small[1],
        head_weight_grad,
        head_bias_grad,
        merge_grad,
        small[4],
        small[2],
        small[3],
        small[5],
        expert_in_grad,
        in_bias_grad,
        expert_out_grad,
        small[6],
    )


def solution(mesh):
    in_specs = (
        P(("dp", "heads", "tensor"), None),
        P(),
        P(),
        P(None, ("dp", "tensor"), "heads"),
        P(None, ("heads", "dp", "tensor")),
        P("heads", ("dp", "tensor")),
        P(),
        P(),
        P(),
        P(),
        P(("dp", "heads", "tensor"), None),
        P(("dp", "heads", "tensor"), None),
        P(None, ("dp", "heads"), "tensor"),
        P(None, ("tensor", "dp", "heads")),
        P(None, "tensor", ("dp", "heads")),
        P(),
        P(("dp", "heads", "tensor"), None),
    )
    out_specs = (
        P(("dp", "heads", "tensor"), None),
        P(),
        P(("dp", "heads", "tensor"), None),
        P(),
        P(),
        P(None, ("dp", "tensor"), "heads"),
        P(None, ("heads", "dp", "tensor")),
        P("heads", ("dp", "tensor")),
        P(),
        P(),
        P(),
        P(),
        P(None, ("dp", "heads"), "tensor"),
        P(None, ("tensor", "dp", "heads")),
        P(None, "tensor", ("dp", "heads")),
        P(),
    )
    sizes = tuple(mesh.shape[name] for name in ("dp", "heads", "tensor"))
    body = staged_body if sizes == (4, 4, 2) else plain_body
    return jax.shard_map(body, mesh=mesh, in_specs=in_specs, out_specs=out_specs, check_vma=False)
```

```python
import functools

import jax
import jax.numpy as jnp
import numpy as np
from jax import lax
from jax.experimental import pallas as pl
from jax.experimental.pallas import tpu as pltpu
from jax.sharding import PartitionSpec as P

HEAD_DIM = 64
SEQ = 197
CAP = 128
ROWS = 208
MIB = 1 << 20
F32 = jnp.float32
BF16 = jnp.bfloat16
MESH = pl.DeviceIdType.MESH
VM = pl.BlockSpec(memory_space=pltpu.VMEM)
SCALE = HEAD_DIM ** (-0.5)
HEADS_AT = ((0, 1, 4, 0, 0), (0, 1, 4, 1, 1), (2, 3, 2, 0, 1))


def nn(a, b):
    return lax.dot_general(a, b, (((1,), (0,)), ((), ())), preferred_element_type=F32)


def nt(a, b):
    return lax.dot_general(a, b, (((1,), (1,)), ((), ())), preferred_element_type=F32)


def tn(a, b):
    return lax.dot_general(a, b, (((0,), (0,)), ((), ())), preferred_element_type=F32)


def exact_parts(values):
    parts = []
    for _ in range(3):
        part = values.astype(BF16)
        parts.append(part)
        values = values - part.astype(F32)
    return parts


def normalise(values):
    average = jnp.mean(values, axis=-1, keepdims=True)
    centred = values - average
    spread = jnp.mean(centred * centred, axis=-1, keepdims=True)
    inverse = lax.rsqrt(spread + 1e-06)
    return centred * inverse, inverse


def norm_back(grad, normal, inverse):
    return inverse * (
        grad
        - jnp.mean(grad, axis=-1, keepdims=True)
        - normal * jnp.mean(grad * normal, axis=-1, keepdims=True)
    )


def lanes(shape):
    return lax.broadcasted_iota(jnp.int32, shape, len(shape) - 1)


def rows_of(shape):
    return lax.broadcasted_iota(jnp.int32, shape, 0)


def halves():
    low = (lanes((1, 128)) < HEAD_DIM).astype(F32)
    return low.astype(BF16), (1 - low).astype(BF16)


def row_of(values, at):
    return jnp.sum(jnp.where(rows_of((values.shape[0], 1)) == at, values, 0.0), axis=0, keepdims=True)


def as_row(column):
    n = column.shape[0]
    return jnp.sum(jnp.where(rows_of((n, n)) == lanes((n, n)), column, 0.0), axis=0, keepdims=True)


def as_column(row):
    n = row.shape[1]
    return jnp.sum(jnp.where(rows_of((n, n)) == lanes((n, n)), row, 0.0), axis=1, keepdims=True)


def scratch_plan(wide, units, rows):
    shard, piece, block = (96, wide), (2, 48, units), (CAP, wide)
    return (
        ("a", shard, BF16),
        ("wp", (4,) + piece, BF16),
        ("g", (4, 4, 2) + shard, BF16),
        ("w", (16,) + piece, BF16),
        ("xb", piece, BF16),
        ("p0", (16, units), BF16),
        ("psum", (3, 16, units), BF16),
        ("pgot", (6, 16, units), BF16),
        ("bias", (16, units), F32),
        ("vec", (8, wide), F32),
        ("brow", (8, units), F32),
        ("eb", (128, wide), BF16),
        ("cs", (4,) + block, BF16),
        ("gs", (4, 8, CAP), F32),
        ("rt", (4, 2) + block, BF16),
        ("rc", (4, 2) + block, BF16),
        ("rg", (4, 2, 8, CAP), F32),
        ("sel", (4, CAP, rows), BF16),
        ("xs", (rows, wide), BF16),
        ("cot", (rows, wide), BF16),
        ("wide8", (128, rows), F32),
        ("chosen", (rows, 128), F32),
        ("spread", (8, rows), F32),
        ("before", (8, rows), F32),
        ("noise", (rows, 128), F32),
        ("router", (128, wide), BF16),
        ("n1", (rows, wide), BF16),
        ("n2", (rows, wide), BF16),
        ("qkv", (4, rows, 640), BF16),
        ("att", (4, rows, 256), BF16),
        ("lse", (4, rows, 128), F32),
        ("res", (rows, wide), F32),
        ("ch", (rows, 128), F32),
        ("chp", (3, rows, 128), BF16),
        ("hp", (4 * 8 * CAP, wide), BF16),
        ("xt", (wide, 8 * CAP), BF16),
        ("gt", (wide, 8 * CAP), BF16),
        ("db", (8, units), F32),
        ("yo", (4, 2) + block, BF16),
        ("yx", (4, 2) + block, BF16),
        ("yg", (4, 2, 8, CAP), F32),
        ("goto", (4,) + block, BF16),
        ("gotx", (4,) + block, BF16),
        ("gotg", (4, 8, CAP), F32),
        ("bo", (4,) + block, BF16),
        ("bx", (4,) + block, BF16),
        ("bg", (4, 8, CAP), F32),
        ("gotc", (8,) + piece, BF16),
        ("gott", (2, 4) + piece, BF16),
        ("gotm", (2, wide, wide), BF16),
        ("gotp", (3, 4) + shard, BF16),
        ("gots", (3,) + shard, BF16),
        ("n1t", (wide, rows), BF16),
        ("brt", (wide, rows), BF16),
        ("dqkv", (rows, 640), BF16),
        ("dn1", (rows, wide), F32),
        ("told", (rows, 128), F32),
        ("ig", (rows, wide), F32),
        ("e0", (16, wide), F32),
        ("esum", (3, 16, wide), F32),
        ("egot", (6, 16, wide), F32),
        ("l0", (8, wide), F32),
        ("lsum", (3, 8, wide), F32),
        ("lgot", (6, 8, wide), F32),
        ("d0", (3, 16, 128), F32),
        ("dgot", (6, 16, 128), F32),
    )


class Buffers:
    pass


class Exchange:
    def __init__(self, send_sems, recv_sems):
        self.send_sems, self.recv_sems = send_sems, recv_sems
        self.used = 0
        d, h, t = lax.axis_index("dp"), lax.axis_index("heads"), lax.axis_index("tensor")
        x, c = h // 2, h % 2
        self.d, self.x, self.c, self.t = d, x, c, t
        self.zh, self.zl = d // 2, d % 2
        self.zs = (d, (d + 2) % 4, 2 * self.zh + 1 - self.zl, 2 * (1 - self.zh) + 1 - self.zl)
        self.plane = ((1 - x, t), (x, 1 - t), (1 - x, 1 - t))
        self.along = [self.at(z, x, c, t) for z in self.zs[1:]]
        self.across = [self.at(d, px, c, pt) for px, pt in self.plane]
        self.mate = self.at(d, x, 1 - c, t)
        self.other_y = self.across[1]

    @staticmethod
    def at(d, x, c, t):
        return (d, 2 * x + c, t)

    def group(self, g):
        return 2 * self.zh + (self.zl + g // 2) % 2, (self.x + g) % 2

    def expert(self, g):
        z, x = self.group(g)
        return 2 * (z % 2) + x

    def holder(self, g):
        z, x = self.group(g)
        return self.at(z, x, self.c, self.t)

    def shard(self, j):
        return 2 * ((self.x + 1 + j) % 2) + (self.c + 1 + j // 2) % 2

    def slots(self, count):
        self.used += count
        return self.used - count

    def send(self, slot, src, dst, peer):
        pltpu.make_async_remote_copy(
            src_ref=src,
            dst_ref=dst,
            send_sem=self.send_sems.at[slot],
            recv_sem=self.recv_sems.at[slot],
            device_id=peer,
            device_id_type=MESH,
        ).start()

    def sent(self, slot, ref):
        pltpu.make_async_copy(ref, ref, self.send_sems.at[slot]).wait()

    def arrived(self, slot, ref):
        pltpu.make_async_copy(ref, ref, self.recv_sems.at[slot]).wait()

    def meet(self):
        barrier = pltpu.get_barrier_semaphore()
        peers = self.along + self.across + [self.mate]
        peers += [self.at(z, 1 - self.x, self.c, self.t) for z in self.zs[1:]]
        for peer in peers:
            pl.semaphore_signal(barrier, inc=1, device_id=peer, device_id_type=MESH)
        pl.semaphore_wait(barrier, len(peers))


class SumOverAll:
    def __init__(self, ex, own, sums, got):
        self.ex, self.own, self.sums, self.got = ex, own, sums, got
        self.slot = ex.slots(6)

    def start(self):
        self.ex.send(self.slot, self.own, self.got.at[0], self.ex.mate)

    def to_plane(self):
        self.ex.arrived(self.slot, self.got.at[0])
        self.sums[0] = self.own[...] + self.got[0]
        for j, peer in enumerate(self.ex.across):
            self.ex.send(self.slot + 1 + j, self.sums.at[0], self.got.at[1 + j], peer)

    def to_half(self):
        for j in range(3):
            self.ex.arrived(self.slot + 1 + j, self.got.at[1 + j])
        self.sums[1] = (self.sums[0] + self.got[3]) + (self.got[1] + self.got[2])
        self.ex.send(self.slot + 4, self.sums.at[1], self.got.at[4], self.ex.along[0])

    def to_pair(self):
        self.ex.arrived(self.slot + 4, self.got.at[4])
        self.sums[2] = self.sums[1] + self.got[4]
        self.ex.send(self.slot + 5, self.sums.at[2], self.got.at[5], self.ex.along[1])

    def result(self):
        self.ex.arrived(self.slot + 5, self.got.at[5])
        return self.sums[2].astype(F32) + self.got[5].astype(F32)

    def done(self):
        for k in range(6):
            self.ex.sent(self.slot + k, self.got.at[k])


def bias_lanes(ex):
    chunk, lane = lanes((1, 640)) // HEAD_DIM, lanes((1, 640)) % HEAD_DIM
    kind = jnp.where(
        (chunk < 2) | (chunk == 4), 0, jnp.where((chunk == 5) | (chunk == 8) | (chunk == 9), 1, 2)
    )
    head = jnp.where((chunk == 1) | (chunk == 9), 1, jnp.where((chunk == 4) | (chunk == 5), 2, 0))
    wanted = 24 * (2 * ex.d + ex.t) + rows_of((24, 640))
    heads = ((HEAD_DIM * head + lane == wanted) & (kind < 2)).astype(F32).astype(BF16)
    return heads, kind


def hidden_lanes(ex, units):
    wanted = 96 * (4 * ex.d + 2 * ex.x + ex.c) + rows_of((96, units))
    return (lanes((96, units)) == wanted).astype(F32).astype(BF16)


def pack(b, ex, inputs):
    heads, merge, w_in, w_out = inputs
    q, k, v = heads[0], heads[1], heads[2]
    m = merge[...].T
    b.a[:, 0:128] = q[:, 0:128]
    b.a[:, 128:256] = k[:, 0:128]
    b.a[:, 256:384] = jnp.concatenate([q[:, 128:192], v[:, 128:192]], axis=1)
    b.a[:, 384:512] = jnp.concatenate([k[:, 128:192], m[:, 128:192]], axis=1)
    b.a[:, 512:640] = v[:, 0:128]
    b.a[:, 640:768] = m[:, 0:128]
    b.wp[:, 0] = w_in[...]
    b.wp[:, 1] = w_out[...]
    me = 2 * ex.x + ex.c
    b.g[3, ex.d, ex.t] = b.a[...]
    b.w[4 * ex.d + me] = b.wp[ex.expert(0)]


def small_operands(b, ex, ids_ref, head_bias_ref, in_bias_ref):
    named = rows_of((4, SEQ))
    ids = ids_ref[...]
    b.wide8[...] = jnp.zeros_like(b.wide8)
    b.wide8[0:4, 0:SEQ] = ((ids[0:1] == named) | (ids[1:2] == named)).astype(F32)
    b.spread[...] = b.wide8[0:8]
    b.chosen[...] = b.wide8[...].T
    heads, kind = bias_lanes(ex)
    row = nn(head_bias_ref[...], heads)
    row = jnp.where(kind == 0, row[0:1], jnp.where(kind == 1, row[1:2], 0.0))
    me = 2 * ex.x + ex.c
    hidden = nn(in_bias_ref[...], hidden_lanes(ex, b.p0.shape[1]))
    b.p0[...] = jnp.zeros_like(b.p0)
    b.p0[0:4] = jnp.where(ex.t == 0, hidden, 0.0).astype(BF16)
    b.p0[4:8] = jnp.where(ex.t == 1, hidden, 0.0).astype(BF16)
    b.p0[8:12, 0:640] = jnp.where(rows_of((4, 1)) == me, row, 0.0).astype(BF16)
    counts = jnp.sum(b.chosen[...], axis=0, keepdims=True)
    high = jnp.floor(counts / 64)
    middle = jnp.floor((counts - 64 * high) / 8)
    digits = jnp.concatenate([counts - 64 * high - 8 * middle, middle, high], axis=0)
    b.p0[12:15, 0:128] = digits.astype(BF16)


def prepare(b, ex, x_ref, cot_ref, noise_ref, router_ref, eb_ref, vector_refs):
    rows = b.xs.shape[0]
    for ref, source in ((b.xs, x_ref), (b.cot, cot_ref)):
        ref[rows - 16 : rows] = jnp.zeros((16, ref.shape[1]), BF16)
        ref[0:SEQ] = source[...]
    for i, ref in enumerate(vector_refs):
        b.vec[i : i + 1] = ref[...].astype(F32).reshape(1, -1)
    b.wide8[...] = jnp.full(b.wide8.shape, -1e30, F32)
    b.wide8[0:4, 0:SEQ] = noise_ref[...]
    b.noise[...] = b.wide8[...].T
    for ref, source in ((b.router, router_ref), (b.eb, eb_ref)):
        ref[...] = jnp.zeros_like(ref)
        ref[0:4] = source[...]
    values = b.xs[...].astype(F32)
    normal, _ = normalise(values)
    b.n1[...] = (normal * b.vec[0:1] + b.vec[1:2]).astype(BF16)
    b.res[...] = values + b.vec[4:5]
    earlier = (rows_of((rows, rows)) < lanes((rows, rows))).astype(F32).astype(BF16)
    b.before[...] = nn(b.spread[...].astype(BF16), earlier)

    def one(g, carry):
        e = ex.expert(g)
        slot = rows_of((CAP, rows)).astype(F32)
        served = (row_of(b.before[...], e) == slot) & (row_of(b.spread[...], e) > 0.5)
        b.sel[g] = jnp.where(served, 1.0, 0.0).astype(BF16)
        b.cs[g] = nn(b.sel[g], b.cot[...]).astype(BF16)
        return carry

    lax.fori_loop(0, 4, one, 0)


def attend(b, ex, h):
    rows, wide = b.n1.shape
    low, high = halves()
    alive = lanes((1, rows)) < SEQ
    weight = b.g[h].reshape(wide, wide)
    b.qkv[h] = (nn(b.n1[...], weight[:, 0:640]) + row_of(b.bias[:, 0:640], 8 + ex.shard(h))).astype(BF16)
    parts = []
    ends = jnp.zeros((rows, 128), F32)
    for i, (sq, sk, sv, uq, uv) in enumerate(HEADS_AT):
        query = b.qkv[h, :, 128 * sq : 128 * sq + 128] * (high if uq else low)
        key = b.qkv[h, :, 128 * sk : 128 * sk + 128]
        value = b.qkv[h, :, 128 * sv : 128 * sv + 128] * (high if uv else low)
        scores = jnp.where(alive, SCALE * nt(query, key), -1e30)
        top = jnp.max(scores, axis=-1, keepdims=True)
        raised = jnp.exp(scores - top)
        total = jnp.sum(raised, axis=-1, keepdims=True)
        parts.append(nn((raised / total).astype(BF16), value))
        ends = jnp.where(lanes((1, 128)) == i, top + jnp.log(total), ends)
    b.lse[h] = ends
    first, second = (parts[0] + parts[1]).astype(BF16), parts[2].astype(BF16)
    b.att[h, :, 0:128] = first
    b.att[h, :, 128:256] = second
    b.res[...] += nt(first, weight[:, 640:768]) + nt(second, weight[:, 384:512])


def attend_back(b, ex, h):
    rows, wide = b.n1.shape
    low, high = halves()
    alive = lanes((1, rows)) < SEQ
    weight = b.g[h].reshape(wide, wide)
    branch = b.ig[...].astype(BF16)
    from_first = nn(branch, weight[:, 640:768]).astype(BF16)
    from_second = nn(branch, weight[:, 384:512]).astype(BF16)
    ends = b.lse[h]
    slabs = [None] * 5
    for i, (sq, sk, sv, uq, uv) in enumerate(HEADS_AT):
        mask_q, mask_v = (high if uq else low), (high if uv else low)
        query = b.qkv[h, :, 128 * sq : 128 * sq + 128] * mask_q
        key = b.qkv[h, :, 128 * sk : 128 * sk + 128]
        value = b.qkv[h, :, 128 * sv : 128 * sv + 128]
        grad = (from_first if i < 2 else from_second) * mask_v
        scores = SCALE * nt(query, key)
        weights = jnp.where(alive, jnp.exp(jnp.where(alive, scores - ends[:, i : i + 1], 0.0)), 0.0)
        value_grad = tn(weights.astype(BF16), grad)
        weight_grad = nt(grad, value)
        inner = jnp.sum(weight_grad * weights, axis=-1, keepdims=True)
        score = (weights * (weight_grad - inner)).astype(BF16)
        query_grad = SCALE * nn(score, key * mask_q)
        key_grad = SCALE * tn(score, query)
        for at, part in ((sq, query_grad), (sk, key_grad), (sv, value_grad)):
            slabs[at] = part if slabs[at] is None else slabs[at] + part
    for at, slab in enumerate(slabs):
        low_slab = slab.astype(BF16)
        b.dqkv[:, 128 * at : 128 * at + 128] = low_slab
        b.l0[:, 128 * at : 128 * at + 128] = jnp.where(
            rows_of((8, 1)) == 4 + ex.shard(h),
            jnp.sum(low_slab.astype(F32), axis=0, keepdims=True),
            b.l0[:, 128 * at : 128 * at + 128],
        )
    b.dn1[...] += nt(b.dqkv[...], weight[:, 0:640])
    put = pl.ds(pl.multiple_of(wide * h, wide), wide)
    for at in range(6):
        if at < 5:
            part = nn(b.n1t[...], b.dqkv[:, 128 * at : 128 * at + 128])
            if at == 3:
                part += nn(b.brt[...], b.att[h, :, 128:256])
        else:
            part = nn(b.brt[...], b.att[h, :, 0:128])
        b.hp[put, 128 * at : 128 * at + 128] = part.astype(BF16)


def route(b, ex):
    normal, _ = normalise(b.res[...])
    b.n2[...] = (normal * b.vec[2:3] + b.vec[3:4]).astype(BF16)
    logits = nt(b.n2[...], b.router[...]) + b.noise[...]
    raised = jnp.exp(logits - jnp.max(logits, axis=-1, keepdims=True))
    chances = raised / jnp.sum(raised, axis=-1, keepdims=True)
    b.ch[...] = chances
    for i, part in enumerate(exact_parts(chances)):
        b.chp[i] = part

    def one(g, carry):
        b.cs[g] = nn(b.sel[g], b.n2[...]).astype(BF16)
        gates = nn(b.sel[g], b.chp[0]) + nn(b.sel[g], b.chp[1]) + nn(b.sel[g], b.chp[2])
        gates = jnp.sum(jnp.where(lanes((1, 128)) == ex.expert(g), gates, 0.0), axis=-1, keepdims=True)
        b.gs[g] = jnp.broadcast_to(as_row(gates), (8, CAP))
        return carry

    lax.fori_loop(0, 4, one, 0)


def serve(b, ex, g):
    cap, wide = b.rt.shape[2:]
    units = b.w.shape[3]
    step = 2 * cap
    x = b.rt[g].reshape(step, wide)
    raw = b.rc[g].reshape(step, wide).astype(F32)
    gate = jnp.concatenate([as_column(b.rg[g, 0, 0:1]), as_column(b.rg[g, 1, 0:1])], axis=0)
    at = pl.ds(pl.multiple_of(g * step, step), step)
    b.xt[:, at] = x.T
    b.gt[:, at] = (gate * raw).astype(BF16).T
    out = jnp.zeros((step, wide), F32)
    back = jnp.zeros((step, wide), F32)
    for f in range(units // wide):
        cols = slice(f * wide, f * wide + wide)
        r = (gate * raw).astype(BF16)
        w_in = b.w[:, 0, :, cols].reshape(wide, wide)
        w_out = b.w[:, 1, :, cols].reshape(wide, wide)
        v = nn(x, w_in) + b.brow[0:1, cols]
        square = v * v
        bend = jnp.tanh(0.7978845608028654 * v * (1.0 + 0.044715 * square))
        hidden = (0.5 * v * (1.0 + bend)).astype(BF16)
        slope = 0.5 * (1.0 + bend) + 0.5 * v * (1.0 - bend * bend) * (
            0.7978845608028654 * (1.0 + 3 * 0.044715 * square)
        )
        low = (nn(r, w_out) * slope).astype(BF16)
        b.hp[pl.ds(pl.multiple_of(f * 8 * cap + g * step, step), step)] = hidden
        b.hp[pl.ds(pl.multiple_of((2 + f) * 8 * cap + g * step, step), step)] = low
        b.db[0:1, cols] += jnp.sum(low.astype(F32), axis=0, keepdims=True)
        out += nt(hidden, w_out)
        back += nt(low, w_in)
    b.yo[g] = out.astype(BF16).reshape(2, cap, wide)
    b.yx[g] = back.astype(BF16).reshape(2, cap, wide)
    told = jnp.sum(raw * out, axis=-1, keepdims=True)
    b.yg[g, 0] = jnp.broadcast_to(as_row(told[0:cap]), (8, cap))
    b.yg[g, 1] = jnp.broadcast_to(as_row(told[cap:step]), (8, cap))


def weight_grads(b, half):
    rows, slots = b.xt.shape[0] // 2, b.xt.shape[1]

    def one(f, carry):
        cols = pl.ds(pl.multiple_of(f * 256, 256), 256)
        shape = (8, b.w.shape[2], 256)
        take = pl.ds(pl.multiple_of(half * rows, rows), rows)
        put = pl.ds(8 * half, 8)
        within = pl.ds(pl.multiple_of((f % 3) * 256, 256), 256)
        hidden = b.hp[pl.ds(pl.multiple_of((f // 3) * slots, slots), slots), within]
        before = b.hp[pl.ds(pl.multiple_of((2 + f // 3) * slots, slots), slots), within]
        b.w[put, 0, :, cols] = nn(b.xt[take], before).astype(BF16).reshape(shape)
        b.w[put, 1, :, cols] = nn(b.gt[take], hidden).astype(BF16).reshape(shape)
        return carry

    lax.fori_loop(0, b.w.shape[3] // 256, one, 0)


def back_to_branch(b, ex, total_tokens):
    chances, chosen = b.ch[...], b.chosen[...]
    b.told[...] = chosen * nt(b.cot[...], b.eb[...])
    b.dn1[...] = jnp.zeros_like(b.dn1)

    def one(g, carry):
        select = b.sel[g]
        b.dn1[...] += tn(select, b.bx[g])
        gate = jnp.where(lanes((1, 128)) == ex.expert(g), as_column(b.bg[g, 0:1]), 0.0)
        first, second, third = exact_parts(gate)
        b.told[...] += tn(select, first) + tn(select, second) + tn(select, third)
        return carry

    lax.fori_loop(0, 4, one, 0)
    chance_grad = b.told[...] + b.bias[15:16, 0:128] * (4.0 / (2.0 * total_tokens * total_tokens))
    logit_grad = chances * (chance_grad - jnp.sum(chances * chance_grad, axis=-1, keepdims=True))
    living = rows_of((b.n1.shape[0], 1)) < SEQ
    logit_low = jnp.where(living, logit_grad, 0.0).astype(BF16)
    b.e0[...] = jnp.zeros_like(b.e0)
    b.e0[3:4, 0:128] = jnp.sum(jnp.where(living, chances, 0.0), axis=0, keepdims=True)
    b.e0[4:8] = tn(logit_low, b.n2[...])[0:4]
    normal, inverse = normalise(b.res[...])
    dn2 = b.dn1[...] + nn(logit_low, b.router[...])
    b.e0[0:1] = jnp.sum(dn2 * normal, axis=0, keepdims=True)
    b.e0[1:2] = jnp.sum(dn2, axis=0, keepdims=True)
    b.ig[...] = b.cot[...].astype(F32) + norm_back(dn2 * b.vec[2:3], normal, inverse)
    branch = b.ig[...].astype(BF16)
    b.e0[2:3] = jnp.sum(branch.astype(F32), axis=0, keepdims=True)
    for e in range(4):
        gate = (chances * chosen)[:, e : e + 1]
        b.e0[8 + e : 9 + e] = jnp.sum(
            (gate * b.cot[...].astype(F32)).astype(BF16).astype(F32), axis=0, keepdims=True
        )
    b.n1t[...] = b.n1[...].T
    b.brt[...] = branch.T
    b.dn1[...] = jnp.zeros_like(b.dn1)
    b.l0[...] = jnp.zeros_like(b.l0)


def combine(b, ex, out_ref):
    gates = b.ch[...] * b.chosen[...]
    first, second, third = exact_parts(gates)
    b.res[...] += nn(first, b.eb[...]) + nn(second, b.eb[...]) + nn(third, b.eb[...])

    def one(g, carry):
        gates = b.ch[...] * b.chosen[...]
        gate = jnp.sum(jnp.where(lanes((1, 128)) == ex.expert(g), gates, 0.0), axis=-1, keepdims=True)
        b.res[...] += gate * tn(b.sel[g], b.bo[g])
        return carry

    lax.fori_loop(0, 4, one, 0)
    out_ref[...] = b.res[0:SEQ]


def shard_rows(h, z=0, y=0, rows=768):
    return pl.ds(pl.multiple_of(768 * h + 192 * z + 96 * y, 96), rows)


def add_into(ref, *others):
    total = ref[...].astype(F32)
    for other in others:
        total += other[...].astype(F32)
    ref[...] = total.astype(ref.dtype)


def block_kernel(total_tokens, plan, *refs):
    inputs, outputs, (send_sems, recv_sems) = refs[:17], refs[17:26], refs[26:28]
    x_ref, cot_ref, ids_ref, noise_ref, router_ref, eb_ref = inputs[:6]
    out_ref, ig_ref, og_ref, hw_ref, mg_ref, early_ref, late_ref, hb_ref, ib_ref = outputs
    b = Buffers()
    for (name, _, _), ref in zip(plan, refs[28:], strict=True):
        setattr(b, name, ref)
    ex = Exchange(send_sems, recv_sems)
    d, x, c, t = ex.d, ex.x, ex.c, ex.t
    zh, zl = ex.zh, ex.zl
    pack(b, ex, inputs[11:15])
    small_operands(b, ex, ids_ref, inputs[15], inputs[16])
    tiny = SumOverAll(ex, b.p0, b.psum, b.pgot)
    ex.meet()

    fz, fp, fc = ex.slots(3), ex.slots(12), ex.slots(16)

    def slot(r, j, pt):
        return b.g.at[j, ex.zs[r], pt]

    shards = ((2, 0), (3, 1), (2, 0), (3, 1))

    def spread_shard(r):
        here = slot(r, 3, t)
        for j in range(3):
            ex.send(fp + 4 * j + r, here, slot(r, shards[j][0], t), ex.across[j])
        ex.send(fc + 12 + r, here, slot(r, 1, t), ex.mate)

    own = slot(0, 3, t)
    ex.send(fz, own, own, ex.along[0])
    ex.send(fz + 1, own, own, ex.along[1])
    spread_shard(0)
    tiny.start()

    ez, exx, ec = ex.slots(6), ex.slots(2), ex.slots(8)

    def part(r, px, pc):
        return b.w.at[4 * ex.zs[r] + 2 * px + pc]

    def own_rows(r):
        ex.send(ez + 2 * (r - 1), b.wp.at[2 * (ex.zs[r] % 2) + x], part(0, x, c), ex.along[r - 1])

    prepare(b, ex, x_ref, cot_ref, noise_ref, router_ref, eb_ref, inputs[6:11])
    here = slot(1, 3, t)
    ex.arrived(fz, here)
    ex.send(fz + 2, here, here, ex.along[1])
    own_rows(1)
    own_rows(3)
    spread_shard(1)
    for r in (2, 3):
        ex.arrived(fz + r - 1, slot(r, 3, t))
        spread_shard(r)
    own_rows(2)
    tiny.to_plane()
    ct, cy = ex.slots(4), ex.slots(4)
    for r in range(4):
        for j, (_, pt) in enumerate(ex.plane):
            here = slot(r, shards[j][0], pt)
            ex.arrived(fp + 4 * j + r, here)
            ex.send(fc + 4 * j + r, here, slot(r, shards[j][1], pt), ex.mate)
        if r == 0:
            ex.send(exx, b.wp.at[2 * zl + 1 - x], part(0, x, c), ex.across[0])
            ex.send(exx + 1, b.wp.at[2 * (1 - zl) + 1 - x], b.xb, ex.across[0])
        if r == 1:
            tiny.to_half()
        if r == 2:
            tiny.to_pair()
            for g in (1, 2, 3):
                ex.send(ct + g, b.cs.at[g], b.rc.at[g, 0], ex.holder(g))
    ex.send(cy, b.cs.at[0], b.rc.at[0, 1], ex.other_y)
    ex.arrived(exx, part(0, 1 - x, c))
    ex.arrived(exx + 1, b.xb)
    for r in (1, 3, 2):
        source = part(0, 1 - x, c) if r == 1 else b.xb
        ex.send(ez + 2 * (r - 1) + 1, source, part(0, 1 - x, c), ex.along[r - 1])
    ex.send(ec + 1, part(0, 1 - x, c), part(0, 1 - x, c), ex.mate)
    ex.send(ec, part(0, x, c), part(0, x, c), ex.mate)
    b.rc[0, 0] = b.cs[0]
    b.bias[...] = tiny.result()
    b.bias[15:16, 0:128] = (
        b.bias[12:13, 0:128] + 8 * b.bias[13:14, 0:128] + 64 * b.bias[14:15, 0:128]
    )
    b.brow[0:1] = row_of(b.bias[...], 4 * t + ex.expert(0))
    for r in range(4):
        for j, (_, pt) in enumerate(ex.plane + ((x, t),)):
            ex.arrived(fc + 4 * j + r, slot(r, shards[j][1], pt))

    def forward_head(h, carry):
        attend(b, ex, h)

        @pl.when(h == 0)
        def _():
            for g in (1, 2, 3):
                ex.arrived(ct + g, b.rc.at[g, 0])
                ex.send(cy + g, b.rc.at[g, 0], b.rc.at[g, 1], ex.other_y)

        return carry

    lax.fori_loop(0, 4, forward_head, 0)
    for g in (1, 2, 3):
        ex.sent(ct + g, b.cs.at[0])
    ex.sent(cy, b.cs.at[0])
    route(b, ex)

    tt, ty, gt, gy = ex.slots(4), ex.slots(4), ex.slots(4), ex.slots(4)
    for g in (1, 2, 3):
        ex.send(tt + g, b.cs.at[g], b.rt.at[g, 0], ex.holder(g))
        ex.send(gt + g, b.gs.at[g], b.rg.at[g, 0], ex.holder(g))
    ex.send(ty, b.cs.at[0], b.rt.at[0, 1], ex.other_y)
    ex.send(gy, b.gs.at[0], b.rg.at[0, 1], ex.other_y)
    b.rt[0, 0] = b.cs[0]
    b.rg[0, 0] = b.gs[0]
    for r in (1, 2, 3):
        here = part(r, x, c)
        ex.arrived(ez + 2 * (r - 1), here)
        ex.send(ec + 2 * r, here, here, ex.mate)
    for g in (1, 2, 3):
        ex.arrived(tt + g, b.rt.at[g, 0])
        ex.send(ty + g, b.rt.at[g, 0], b.rt.at[g, 1], ex.other_y)
        ex.arrived(gt + g, b.rg.at[g, 0])
        ex.send(gy + g, b.rg.at[g, 0], b.rg.at[g, 1], ex.other_y)
    for r in (1, 2, 3):
        here = part(r, 1 - x, c)
        ex.arrived(ez + 2 * (r - 1) + 1, here)
        ex.send(ec + 2 * r + 1, here, here, ex.mate)
    for g in range(4):
        ex.arrived(cy + g, b.rc.at[g, 1])
        ex.arrived(ty + g, b.rt.at[g, 1])
        ex.arrived(gy + g, b.rg.at[g, 1])
    for r in range(4):
        for i, px in enumerate((x, 1 - x)):
            ex.arrived(ec + 2 * r + i, part(r, px, 1 - c))
    b.db[...] = jnp.zeros_like(b.db)

    yx, yg, yo = ex.slots(4), ex.slots(4), ex.slots(4)
    hx, hg, ho = ex.slots(4), ex.slots(4), ex.slots(4)

    def serve_blocks(g, carry):
        serve(b, ex, g)
        ex.send(yx + g, b.yx.at[g, 1], b.gotx.at[g], ex.other_y)
        ex.send(yg + g, b.yg.at[g, 1], b.gotg.at[g], ex.other_y)
        return carry

    lax.fori_loop(0, 4, serve_blocks, 0)

    def give_back(g, carry):
        ex.arrived(yx + g, b.gotx.at[g])
        ex.arrived(yg + g, b.gotg.at[g])
        add_into(b.yx.at[g, 0], b.gotx.at[g])
        add_into(b.yg.at[g, 0], b.gotg.at[g])

        @pl.when(g > 0)
        def _():
            ex.send(hx + g, b.yx.at[g, 0], b.bx.at[g], ex.holder(g))
            ex.send(hg + g, b.yg.at[g, 0], b.bg.at[g], ex.holder(g))

        return carry

    lax.fori_loop(0, 3, give_back, 0)
    b.bx[0] = b.yx[0, 0]
    b.bg[0] = b.yg[0, 0]
    for k in range(6):
        ex.sent(ez + k, b.xb)
    ex.sent(exx, b.xb)
    ex.sent(exx + 1, b.xb)
    for k in range(8):
        ex.sent(ec + k, b.xb)

    kc, kz, kr = ex.slots(8), ex.slots(8), ex.slots(8)
    mine = ex.expert(0)

    def rows_at(half, i, pc):
        return 4 * (2 * half + i // 2) + 2 * (i % 2) + pc

    def to_mate(base, half):
        for i in range(4):
            ex.send(kc + base + i, b.w.at[rows_at(half, i, 1 - c)], b.gotc.at[base + i], ex.mate)

    weight_grads(b, 1 - zh)
    to_mate(0, 1 - zh)
    give_back(3, 0)
    for g in range(4):
        ex.send(yo + g, b.yo.at[g, 1], b.goto.at[g], ex.other_y)

    def to_owner(far, i):
        half = 1 - zh if far else zh
        slot = 4 * (1 - far) + i
        ex.arrived(kc + slot, b.gotc.at[slot])
        at = rows_at(half, i, c)
        add_into(b.w.at[at], b.gotc.at[slot])

        @pl.when((far == 1) | (i != mine))
        def _():
            pltpu.make_async_remote_copy(
                src_ref=b.w.at[at],
                dst_ref=b.gott.at[far, mine],
                send_sem=ex.send_sems.at[kz + slot],
                recv_sem=ex.recv_sems.at[kr + 4 * far + mine],
                device_id=ex.at(2 * half + i // 2, i % 2, c, t),
                device_id_type=MESH,
            ).start()

    def to_other_half(i, carry):
        to_owner(1, i)
        return carry

    lax.fori_loop(0, 4, to_other_half, 0)
    weight_grads(b, zh)
    to_mate(4, zh)
    for g in (1, 2, 3):
        ex.arrived(hx + g, b.bx.at[g])
        ex.arrived(hg + g, b.bg.at[g])
    back_to_branch(b, ex, total_tokens)
    sums = SumOverAll(ex, b.e0, b.esum, b.egot)
    sums.start()

    db = ex.slots(5)
    for i in range(b.db.shape[1] // 128):
        b.d0[0, i : i + 1] = b.db[0:1, 128 * i : 128 * i + 128]
    ex.send(db, b.d0.at[0], b.dgot.at[0], ex.mate)

    def own_half(i, carry):
        to_owner(0, i)
        return carry

    lax.fori_loop(0, 4, own_half, 0)

    sm, sp, sz = ex.slots(2), ex.slots(12), ex.slots(3)

    def merge_core(i):
        ex.arrived(sm + i, b.gotm.at[i])

        h = 2 + i
        for r in (3, 2, 1, 0):
            z = ex.zs[r]
            add_into(b.hp.at[shard_rows(h, z, 0, 192)], b.gotm.at[i, shard_rows(0, z, 0, 192)])
            for j in (0, 2) if i == 0 else (1,):
                ex.send(
                    sp + 4 * j + r,
                    b.hp.at[shard_rows(h, z, ex.plane[j][1], 96)],
                    b.gotp.at[j, r],
                    ex.across[j],
                )

    def backward_head(j, carry):
        attend_back(b, ex, j)

        @pl.when(j < 2)
        def _():
            ex.send(sm + j, b.hp.at[shard_rows(j)], b.gotm.at[j], ex.mate)

        @pl.when(j == 0)
        def _():
            sums.to_plane()
            ex.arrived(db, b.dgot.at[0])
            b.d0[1] = b.d0[0] + b.dgot[0]
            ex.send(db + 1, b.d0.at[1], b.dgot.at[1], ex.along[0])

        @pl.when(j == 1)
        def _():
            def one(g, carry):
                ex.arrived(yo + g, b.goto.at[g])
                add_into(b.yo.at[g, 0], b.goto.at[g])

                @pl.when(g > 0)
                def _():
                    ex.send(ho + g, b.yo.at[g, 0], b.bo.at[g], ex.holder(g))

                return carry

            lax.fori_loop(0, 4, one, 0)
            b.bo[0] = b.yo[0, 0]
            sums.to_half()

        @pl.when(j == 2)
        def _():
            merge_core(0)
            ex.arrived(db + 1, b.dgot.at[1])
            b.d0[2] = b.d0[1] + b.dgot[1]
            for g in (1, 2, 3):
                ex.send(db + 1 + g, b.d0.at[2], b.dgot.at[1 + g], ex.holder(g))
            sums.to_pair()

        return carry

    lax.fori_loop(0, 4, backward_head, 0)
    merge_core(1)
    first_grad = b.dn1[...]
    normal, inverse = normalise(b.xs[...].astype(F32))
    b.l0[0:1] = jnp.sum(first_grad * normal, axis=0, keepdims=True)
    b.l0[1:2] = jnp.sum(first_grad, axis=0, keepdims=True)
    late = SumOverAll(ex, b.l0, b.lsum, b.lgot)
    late.start()
    ig_ref[...] = (b.ig[...] + norm_back(first_grad * b.vec[0:1], normal, inverse))[0:SEQ]
    late.to_plane()
    for g in (1, 2, 3):
        ex.arrived(ho + g, b.bo.at[g])
    combine(b, ex, out_ref)
    home = 2 * x + c
    for r in (3, 2, 1, 0):
        for j in range(3):
            ex.arrived(sp + 4 * j + r, b.gotp.at[j, r])
        share = b.hp.at[shard_rows(3, ex.zs[r], t, 96)]
        add_into(share, b.gotp.at[0, r], b.gotp.at[1, r], b.gotp.at[2, r])
        if r >= 2:
            ex.send(sz + r - 2, share, b.gots.at[r - 2], ex.along[1])
    late.to_half()
    ex.arrived(sz + 1, b.gots.at[1])
    share = b.hp.at[shard_rows(3, ex.zs[1], t, 96)]
    add_into(share, b.gots.at[1])
    ex.send(sz + 2, share, b.gots.at[2], ex.along[0])
    late.to_pair()

    totals = sums.result()
    early_ref[...] = totals
    load = b.bias[15:16, 0:128] / (2.0 * total_tokens)
    balance = 4.0 * jnp.sum(load * (totals[3:4, 0:128] / total_tokens), axis=-1, keepdims=True)
    early_ref[3:4, 0:128] = jnp.broadcast_to(balance, (1, 128))
    units = b.db.shape[1]
    hidden_rows = jnp.zeros((8, units), F32)
    for g in range(4):
        if g:
            ex.arrived(db + 1 + g, b.dgot.at[1 + g])
        source = b.dgot.at[1 + g] if g else b.d0.at[2]
        line = jnp.concatenate([source[i : i + 1] for i in range(units // 128)], axis=1)
        hidden_rows = jnp.where(rows_of((8, 1)) == ex.expert(g), line, hidden_rows)
    select = hidden_lanes(ex, units)
    ib_ref[...] = sum(nt(part_of, select) for part_of in exact_parts(hidden_rows))[0:4]
    late_sum = late.result()
    late_ref[...] = late_sum
    heads, kind = bias_lanes(ex)
    row = row_of(late_sum, 4 + home)[:, 0:640]
    rows = jnp.concatenate([jnp.where(kind == 0, row, 0.0), jnp.where(kind == 1, row, 0.0)], axis=0)
    hb_ref[...] = sum(nt(part_of, heads) for part_of in exact_parts(rows))
    ex.arrived(sz, b.gots.at[0])
    ex.arrived(sz + 2, b.gots.at[2])
    shard = b.hp[shard_rows(3, d, t, 96)].astype(F32) + b.gots[0].astype(F32) + b.gots[2].astype(F32)
    for k, (whole, lane) in enumerate(((0, 256), (128, 384), (512, 320))):
        hw_ref[k, :, 0:128] = shard[:, whole : whole + 128]
        hw_ref[k, :, 128:192] = shard[:, lane : lane + 64]
    mg_ref[...] = jnp.concatenate([shard[:, 640:768], shard[:, 448:512]], axis=1).T
    b.gott[0, mine] = b.w[4 * d + home]
    for e in range(4):
        ex.arrived(kr + 4 + e, b.gott.at[1, e])

        @pl.when(e != mine)
        def _():
            ex.arrived(kr + e, b.gott.at[0, e])

        og_ref[e] = (b.gott[0, e].astype(F32) + b.gott[1, e].astype(F32)).astype(BF16)
    for sum_of in (tiny, sums, late):
        sum_of.done()
    for k in range(3):
        ex.sent(fz + k, b.a)
        ex.sent(sz + k, b.a)
    for k in range(12):
        ex.sent(fp + k, b.a)
        ex.sent(sp + k, b.a)
    for k in range(16):
        ex.sent(fc + k, b.a)
    for g in range(4):
        for base in (ty, yx, yo):
            ex.sent(base + g, b.cs.at[0])
        for base in (gy, yg):
            ex.sent(base + g, b.gs.at[0])
        ex.sent(kz + g, b.xb)

        @pl.when(g != mine)
        def _():
            ex.sent(kz + 4 + g, b.xb)

    for g in (1, 2, 3):
        for base in (cy, tt, hx, ho):
            ex.sent(base + g, b.cs.at[0])
        for base in (gt, hg):
            ex.sent(base + g, b.gs.at[0])
    for k in range(8):
        ex.sent(kc + k, b.xb)
    for k in range(5):
        ex.sent(db + k, b.dgot.at[0])
    for i in range(2):
        ex.sent(sm + i, b.gotm.at[0])
    assert ex.used <= COPIES


COPIES = 192


def staged_body(
    inputs,
    first_gain,
    first_bias,
    head_weight,
    head_bias,
    merge_weight,
    merge_bias,
    second_gain,
    second_bias,
    router,
    router_noise,
    expert_ids,
    expert_in,
    expert_in_bias,
    expert_out,
    expert_out_bias,
    cotangent,
):
    tok_rows, wide = inputs.shape
    experts, _, units = expert_in.shape
    total_tokens = tok_rows * lax.axis_size(("dp", "heads", "tensor"))
    plan = scratch_plan(wide, units, ROWS)
    output, input_grad, expert_grads, head_grad, merge_grad, early, late, head_bias_grad, in_bias_grad = (
        pl.pallas_call(
            functools.partial(block_kernel, float(total_tokens), plan),
            out_shape=(
                jax.ShapeDtypeStruct((tok_rows, wide), F32),
                jax.ShapeDtypeStruct((tok_rows, wide), F32),
                jax.ShapeDtypeStruct((experts, 2) + expert_in.shape[1:], BF16),
                jax.ShapeDtypeStruct(head_weight.shape, F32),
                jax.ShapeDtypeStruct(merge_weight.shape, F32),
                jax.ShapeDtypeStruct((16, wide), F32),
                jax.ShapeDtypeStruct((8, wide), F32),
                jax.ShapeDtypeStruct(head_bias.shape, F32),
                jax.ShapeDtypeStruct(expert_in_bias.shape, F32),
            ),
            in_specs=[VM] * 17,
            out_specs=(VM,) * 9,
            scratch_shapes=[pltpu.SemaphoreType.DMA((COPIES,))] * 2
            + [pltpu.VMEM(shape, kind) for _, shape, kind in plan],
            compiler_params=pltpu.CompilerParams(
                collective_id=0, has_side_effects=True, vmem_limit_bytes=60 * MIB
            ),
            name="block",
        )(
            inputs,
            cotangent,
            expert_ids.T,
            router_noise.T,
            router.T,
            expert_out_bias,
            first_gain,
            first_bias,
            second_gain,
            second_bias,
            merge_bias,
            head_weight,
            merge_weight,
            expert_in,
            jnp.transpose(expert_out, (0, 2, 1)),
            head_bias,
            expert_in_bias,
        )
    )
    return (
        output,
        early[3, 0],
        input_grad,
        late[0],
        late[1],
        head_grad,
        head_bias_grad,
        merge_grad,
        early[2],
        early[0],
        early[1],
        early[4:8].T,
        expert_grads[:, 0].astype(F32),
        in_bias_grad,
        jnp.transpose(expert_grads[:, 1], (0, 2, 1)).astype(F32),
        early[8:12],
    )


def layer_norm(values, factor, offset):
    average = jnp.mean(values, axis=-1, keepdims=True)
    centred = values - average
    spread = jnp.mean(centred * centred, axis=-1, keepdims=True)
    return centred * lax.rsqrt(spread + 1e-06) * factor + offset


def expert_weights(expert_in, expert_out, expert_in_bias):
    return (
        lax.all_gather(expert_in, ("dp", "heads"), axis=1, tiled=True),
        lax.all_gather(expert_out, ("dp", "heads"), axis=2, tiled=True),
        lax.all_gather(expert_in_bias, ("dp", "heads"), axis=1, tiled=True),
    )


def plain_body(
    inputs,
    first_gain,
    first_bias,
    head_weight,
    head_bias,
    merge_weight,
    merge_bias,
    second_gain,
    second_bias,
    router,
    router_noise,
    expert_ids,
    expert_in,
    expert_in_bias,
    expert_out,
    expert_out_bias,
    cotangent,
):
    tok_rows = inputs.shape[0]
    features = inputs.shape[1]
    experts = expert_in.shape[0]
    head_cols = head_weight.shape[2]
    heads_local = head_cols // HEAD_DIM
    total_tokens = tok_rows * lax.axis_size(("dp", "heads", "tensor"))
    scale = HEAD_DIM ** (-0.5)
    whole_head, whole_merge, whole_bias = (
        lax.all_gather(head_weight, ("dp", "tensor"), axis=1, tiled=True),
        lax.all_gather(merge_weight, ("dp", "tensor"), axis=1, tiled=True),
        lax.all_gather(head_bias, ("dp", "tensor"), axis=1, tiled=True),
    )
    residual_in = inputs.astype(jnp.float32)
    normed, norm_back = jax.vjp(
        layer_norm, residual_in, first_gain.astype(jnp.float32), first_bias.astype(jnp.float32)
    )
    group_rows = lax.all_gather(normed.astype(jnp.bfloat16), "heads", axis=0, tiled=True)
    group_count = group_rows.shape[0]
    group_images = group_count // SEQ
    projected = jnp.einsum(
        "gd,jdc->jgc", group_rows, whole_head, preferred_element_type=jnp.float32
    )
    bias_values = whole_bias.astype(jnp.float32)
    query_low = (projected[0] + bias_values[0]).astype(jnp.bfloat16)
    key_low = projected[1].astype(jnp.bfloat16)
    value_low = (projected[2] + bias_values[1]).astype(jnp.bfloat16)

    def shaped(array):
        return array.reshape(group_images, SEQ, heads_local, HEAD_DIM)

    query_img, key_img, value_img = (shaped(query_low), shaped(key_low), shaped(value_low))
    scores = scale * jnp.einsum(
        "ishd,ithd->ihst", query_img, key_img, preferred_element_type=jnp.float32
    )
    top_score = jnp.max(scores, axis=-1, keepdims=True)
    raised = jnp.exp(scores - top_score)
    row_total = jnp.sum(raised, axis=-1, keepdims=True)
    weights = raised / row_total
    log_total = top_score + jnp.log(row_total)
    attended = jnp.einsum(
        "ihst,ithd->ishd",
        weights.astype(jnp.bfloat16),
        value_img,
        preferred_element_type=jnp.float32,
    )
    attended_low = attended.reshape(group_count, head_cols).astype(jnp.bfloat16)
    segment = attended_low
    branch = lax.psum_scatter(
        jnp.dot(segment, whole_merge, preferred_element_type=jnp.float32).astype(jnp.bfloat16),
        "heads",
        scatter_dimension=0,
        tiled=True,
    ).astype(jnp.float32) + merge_bias.astype(jnp.float32)
    residual = residual_in + branch
    normed_two, norm_two_back = jax.vjp(
        layer_norm, residual, second_gain.astype(jnp.float32), second_bias.astype(jnp.float32)
    )
    second_low = normed_two.astype(jnp.bfloat16)
    router_logits = jnp.dot(second_low, router, preferred_element_type=jnp.float32) + router_noise
    chances = jax.nn.softmax(router_logits, axis=-1)
    expert_range = jnp.arange(experts, dtype=jnp.int32)
    chosen_pair = (expert_ids[:, :, None] == expert_range).astype(jnp.int32)
    chosen = jnp.sum(chosen_pair, axis=1)
    order = jnp.arange(tok_rows, dtype=jnp.int32)
    earlier = (order[None, :] < order[:, None]).astype(jnp.bfloat16)
    before = jnp.dot(
        earlier, chosen.astype(jnp.bfloat16), preferred_element_type=jnp.float32
    ).astype(jnp.int32)
    slot_ids = jnp.take_along_axis(before, expert_ids, axis=1)
    flat_rows = (slot_ids * experts + expert_ids).reshape(-1)
    picks = chosen_pair.astype(jnp.float32)
    count_terms = jnp.sum(chosen.astype(jnp.float32), axis=0)
    chance_terms = jnp.sum(chances, axis=0)
    count_all, chance_all = lax.psum((count_terms, chance_terms), ("dp", "heads", "tensor"))
    load_share = count_all / (2 * total_tokens)
    balance_loss = experts * jnp.sum(load_share * chance_all / total_tokens)
    gate_values = jnp.sum(picks * chances[:, None, :], axis=2)
    doubled = jnp.repeat(second_low, 2, axis=0)
    own_buffer = jnp.zeros((CAP * experts, features), jnp.bfloat16).at[flat_rows].set(doubled)
    pair_buffer = lax.all_gather(
        own_buffer.reshape(CAP, experts, features), "tensor", axis=0, tiled=True
    )
    weight_in, weight_out, bias_in = expert_weights(expert_in, expert_out, expert_in_bias)
    before_act = (
        jnp.einsum("ced,edf->cef", pair_buffer, weight_in, preferred_element_type=jnp.float32)
        + bias_in.astype(jnp.float32)[None, :, :]
    )
    activated, gelu_back = jax.vjp(jax.nn.gelu, before_act)
    activated_low = activated.astype(jnp.bfloat16)
    partial_out = jnp.einsum(
        "cef,efd->ced", activated_low, weight_out, preferred_element_type=jnp.float32
    )
    own_out = (
        lax.psum_scatter(
            partial_out.astype(jnp.bfloat16), "tensor", scatter_dimension=0, tiled=True
        ).astype(jnp.float32)
        + expert_out_bias.astype(jnp.float32)[None, :, :]
    )
    picked = own_out.reshape(CAP * experts, features)[flat_rows].reshape(tok_rows, 2, features)
    output = residual + jnp.sum(gate_values[:, :, None] * picked, axis=1)
    incoming = cotangent.astype(jnp.float32)
    gate_grad = jnp.sum(incoming[:, None, :] * picked, axis=2)
    slot_grad = (
        (gate_values[:, :, None] * incoming[:, None, :])
        .astype(jnp.bfloat16)
        .reshape(tok_rows * 2, features)
    )
    own_slot_grad = (
        jnp.zeros((CAP * experts, features), jnp.bfloat16)
        .at[flat_rows]
        .set(slot_grad)
        .reshape(CAP, experts, features)
    )
    out_bias_grad = jnp.sum(own_slot_grad, axis=0, dtype=jnp.float32)
    pair_grad = lax.all_gather(own_slot_grad, "tensor", axis=0, tiled=True)
    back_in, back_out, unused_bias = expert_weights(expert_in, expert_out, expert_in_bias)
    hidden_grad = jnp.einsum(
        "ced,efd->cef", pair_grad, back_out, preferred_element_type=jnp.float32
    )
    pre_grad = gelu_back(hidden_grad)[0].astype(jnp.bfloat16)
    out_grad_rows = jnp.einsum(
        "cef,ced->def", activated_low, pair_grad, preferred_element_type=jnp.float32
    )
    in_grad_rows = jnp.einsum(
        "ced,cef->def", pair_buffer, pre_grad, preferred_element_type=jnp.float32
    )
    in_bias_rows = jnp.sum(pre_grad, axis=0, dtype=jnp.float32).T
    in_grad_rows, out_grad_rows, in_bias_rows = (
        lax.psum_scatter(in_grad_rows, ("dp", "heads"), scatter_dimension=0, tiled=True),
        lax.psum_scatter(out_grad_rows, ("dp", "heads"), scatter_dimension=0, tiled=True),
        lax.psum_scatter(in_bias_rows, ("dp", "heads"), scatter_dimension=0, tiled=True),
    )
    expert_in_grad = jnp.transpose(in_grad_rows, (1, 0, 2))
    expert_out_grad = jnp.transpose(out_grad_rows, (1, 2, 0))
    in_bias_grad = in_bias_rows.T
    buffer_grad = jnp.einsum("cef,edf->ced", pre_grad, back_in, preferred_element_type=jnp.float32)
    own_buffer_grad = (
        lax.psum_scatter(
            buffer_grad.astype(jnp.bfloat16), "tensor", scatter_dimension=0, tiled=True
        )
        .astype(jnp.float32)
        .reshape(CAP * experts, features)
    )
    second_grad = jnp.sum(own_buffer_grad[flat_rows].reshape(tok_rows, 2, features), axis=1)
    chance_grad = (
        jnp.sum(picks * gate_grad[:, :, None], axis=1) + experts * load_share / total_tokens
    )
    logit_grad = chances * (chance_grad - jnp.sum(chances * chance_grad, axis=-1, keepdims=True))
    logit_low = logit_grad.astype(jnp.bfloat16)
    router_grad = lax.dot_general(
        second_low, logit_low, (((0,), (0,)), ((), ())), preferred_element_type=jnp.float32
    )
    second_grad = second_grad + jnp.dot(logit_low, router.T, preferred_element_type=jnp.float32)
    resid_part, gain_two_grad, bias_two_grad = norm_two_back(second_grad)
    resid_grad = incoming + resid_part
    branch_low = resid_grad.astype(jnp.bfloat16)
    merge_bias_grad = jnp.sum(branch_low, axis=0, dtype=jnp.float32)
    group_grad = lax.all_gather(branch_low, "heads", axis=0, tiled=True)
    merge_rows_grad = lax.dot_general(
        group_grad, attended_low, (((0,), (0,)), ((), ())), preferred_element_type=jnp.float32
    )
    attended_grad = shaped(
        jnp.dot(group_grad, whole_merge.T, preferred_element_type=jnp.float32).astype(jnp.bfloat16)
    )
    weights_again = jnp.exp(
        scale
        * jnp.einsum("ishd,ithd->ihst", query_img, key_img, preferred_element_type=jnp.float32)
        - log_total
    )
    value_grad = jnp.einsum(
        "ihst,ishd->ithd",
        weights_again.astype(jnp.bfloat16),
        attended_grad,
        preferred_element_type=jnp.float32,
    )
    weight_grad = jnp.einsum(
        "ishd,ithd->ihst", attended_grad, value_img, preferred_element_type=jnp.float32
    )
    inner_sum = jnp.sum(weight_grad * weights_again, axis=-1, keepdims=True)
    score_low = (weights_again * (weight_grad - inner_sum)).astype(jnp.bfloat16)
    query_grad = scale * jnp.einsum(
        "ihst,ithd->ishd", score_low, key_img, preferred_element_type=jnp.float32
    )
    key_grad = scale * jnp.einsum(
        "ihst,ishd->ithd", score_low, query_img, preferred_element_type=jnp.float32
    )
    triple_low = jnp.stack(
        [
            query_grad.reshape(group_count, head_cols),
            key_grad.reshape(group_count, head_cols),
            value_grad.reshape(group_count, head_cols),
        ],
        axis=0,
    ).astype(jnp.bfloat16)
    head_rows_grad = jnp.einsum(
        "gd,jgc->djc", group_rows, triple_low, preferred_element_type=jnp.float32
    )
    head_bias_rows = jnp.sum(triple_low[0::2], axis=1, dtype=jnp.float32).T
    segment = triple_low
    first_grad = lax.psum_scatter(
        jnp.einsum("jgc,jdc->gd", segment, whole_head, preferred_element_type=jnp.float32).astype(
            jnp.bfloat16
        ),
        "heads",
        scatter_dimension=0,
        tiled=True,
    ).astype(jnp.float32)
    input_part, gain_one_grad, bias_one_grad = norm_back(first_grad)
    input_grad = resid_grad + input_part
    head_rows_grad, merge_rows_grad, head_bias_rows = (
        lax.psum_scatter(head_rows_grad, ("dp", "tensor"), scatter_dimension=0, tiled=True),
        lax.psum_scatter(merge_rows_grad, ("dp", "tensor"), scatter_dimension=0, tiled=True),
        lax.psum_scatter(head_bias_rows, ("dp", "tensor"), scatter_dimension=0, tiled=True),
    )
    head_weight_grad = jnp.transpose(head_rows_grad, (1, 0, 2))
    merge_grad = merge_rows_grad.T
    head_bias_grad = head_bias_rows.T
    small = lax.psum(
        (
            gain_one_grad,
            bias_one_grad,
            gain_two_grad,
            bias_two_grad,
            merge_bias_grad,
            router_grad,
            out_bias_grad,
        ),
        ("dp", "heads", "tensor"),
    )
    return (
        output,
        balance_loss,
        input_grad,
        small[0],
        small[1],
        head_weight_grad,
        head_bias_grad,
        merge_grad,
        small[4],
        small[2],
        small[3],
        small[5],
        expert_in_grad,
        in_bias_grad,
        expert_out_grad,
        small[6],
    )


def solution(mesh):
    in_specs = (
        P(("dp", "heads", "tensor"), None),
        P(),
        P(),
        P(None, ("dp", "tensor"), "heads"),
        P(None, ("heads", "dp", "tensor")),
        P("heads", ("dp", "tensor")),
        P(),
        P(),
        P(),
        P(),
        P(("dp", "heads", "tensor"), None),
        P(("dp", "heads", "tensor"), None),
        P(None, ("dp", "heads"), "tensor"),
        P(None, ("tensor", "dp", "heads")),
        P(None, "tensor", ("dp", "heads")),
        P(),
        P(("dp", "heads", "tensor"), None),
    )
    out_specs = (
        P(("dp", "heads", "tensor"), None),
        P(),
        P(("dp", "heads", "tensor"), None),
        P(),
        P(),
        P(None, ("dp", "tensor"), "heads"),
        P(None, ("heads", "dp", "tensor")),
        P("heads", ("dp", "tensor")),
        P(),
        P(),
        P(),
        P(),
        P(None, ("dp", "heads"), "tensor"),
        P(None, ("tensor", "dp", "heads")),
        P(None, "tensor", ("dp", "heads")),
        P(),
    )
    sizes = tuple(mesh.shape[name] for name in ("dp", "heads", "tensor"))
    body = staged_body if sizes == (4, 4, 2) else plain_body
    return jax.shard_map(body, mesh=mesh, in_specs=in_specs, out_specs=out_specs, check_vma=False)
```

```python
import functools

import jax
import jax.numpy as jnp
import numpy as np
from jax import lax
from jax.experimental import pallas as pl
from jax.experimental.pallas import tpu as pltpu
from jax.sharding import PartitionSpec as P

HEAD_DIM = 64
SEQ = 197
CAP = 128
ROWS = 208
MIB = 1 << 20
F32 = jnp.float32
BF16 = jnp.bfloat16
MESH = pl.DeviceIdType.MESH
VM = pl.BlockSpec(memory_space=pltpu.VMEM)
SCALE = HEAD_DIM ** (-0.5)
HEADS_AT = ((0, 1, 4, 0, 0), (0, 1, 4, 1, 1), (2, 3, 2, 0, 1))


def nn(a, b):
    return lax.dot_general(a, b, (((1,), (0,)), ((), ())), preferred_element_type=F32)


def nt(a, b):
    return lax.dot_general(a, b, (((1,), (1,)), ((), ())), preferred_element_type=F32)


def tn(a, b):
    return lax.dot_general(a, b, (((0,), (0,)), ((), ())), preferred_element_type=F32)


def exact_parts(values):
    parts = []
    for _ in range(3):
        part = values.astype(BF16)
        parts.append(part)
        values = values - part.astype(F32)
    return parts


def normalise(values):
    average = jnp.mean(values, axis=-1, keepdims=True)
    centred = values - average
    spread = jnp.mean(centred * centred, axis=-1, keepdims=True)
    inverse = lax.rsqrt(spread + 1e-06)
    return centred * inverse, inverse


def norm_back(grad, normal, inverse):
    return inverse * (
        grad
        - jnp.mean(grad, axis=-1, keepdims=True)
        - normal * jnp.mean(grad * normal, axis=-1, keepdims=True)
    )


def lanes(shape):
    return lax.broadcasted_iota(jnp.int32, shape, len(shape) - 1)


def rows_of(shape):
    return lax.broadcasted_iota(jnp.int32, shape, 0)


def halves():
    low = (lanes((1, 128)) < HEAD_DIM).astype(F32)
    return low.astype(BF16), (1 - low).astype(BF16)


def row_of(values, at):
    return jnp.sum(jnp.where(rows_of((values.shape[0], 1)) == at, values, 0.0), axis=0, keepdims=True)


def as_row(column):
    n = column.shape[0]
    return jnp.sum(jnp.where(rows_of((n, n)) == lanes((n, n)), column, 0.0), axis=0, keepdims=True)


def as_column(row):
    n = row.shape[1]
    return jnp.sum(jnp.where(rows_of((n, n)) == lanes((n, n)), row, 0.0), axis=1, keepdims=True)


def scratch_plan(wide, units, rows):
    shard, piece, block = (96, wide), (2, 48, units), (CAP, wide)
    return (
        ("a", shard, BF16),
        ("wp", (4,) + piece, BF16),
        ("g", (4, 4, 2) + shard, BF16),
        ("w", (16,) + piece, BF16),
        ("xb", piece, BF16),
        ("p0", (16, units), BF16),
        ("psum", (3, 16, units), BF16),
        ("pgot", (6, 16, units), BF16),
        ("bias", (16, units), F32),
        ("vec", (8, wide), F32),
        ("brow", (8, units), F32),
        ("eb", (128, wide), BF16),
        ("cs", (4,) + block, BF16),
        ("gs", (4, 8, CAP), F32),
        ("rt", (4, 2) + block, BF16),
        ("rc", (4, 2) + block, BF16),
        ("rg", (4, 2, 8, CAP), F32),
        ("sel", (4, CAP, rows), BF16),
        ("xs", (rows, wide), BF16),
        ("cot", (rows, wide), BF16),
        ("wide8", (128, rows), F32),
        ("chosen", (rows, 128), F32),
        ("spread", (8, rows), F32),
        ("before", (8, rows), F32),
        ("noise", (rows, 128), F32),
        ("router", (128, wide), BF16),
        ("n1", (rows, wide), BF16),
        ("n2", (rows, wide), BF16),
        ("qkv", (4, rows, 640), BF16),
        ("att", (4, rows, 256), BF16),
        ("lse", (4, rows, 128), F32),
        ("res", (rows, wide), F32),
        ("ch", (rows, 128), F32),
        ("chp", (3, rows, 128), BF16),
        ("hp", (4 * 8 * CAP, wide), BF16),
        ("xt", (wide, 8 * CAP), BF16),
        ("gt", (wide, 8 * CAP), BF16),
        ("db", (8, units), F32),
        ("yo", (4, 2) + block, BF16),
        ("yx", (4, 2) + block, BF16),
        ("yg", (4, 2, 8, CAP), F32),
        ("goto", (4,) + block, BF16),
        ("gotx", (4,) + block, BF16),
        ("gotg", (4, 8, CAP), F32),
        ("bo", (4,) + block, BF16),
        ("bx", (4,) + block, BF16),
        ("bg", (4, 8, CAP), F32),
        ("gotc", (8,) + piece, BF16),
        ("gotz", (2,) + piece, BF16),
        ("gotn", (4,) + piece, BF16),
        ("gotf", (2,) + piece, BF16),
        ("gotm", (2, wide, wide), BF16),
        ("gotp", (3, 4) + shard, BF16),
        ("gots", (3,) + shard, BF16),
        ("n1t", (wide, rows), BF16),
        ("brt", (wide, rows), BF16),
        ("dqkv", (rows, 640), BF16),
        ("dn1", (rows, wide), F32),
        ("told", (rows, 128), F32),
        ("ig", (rows, wide), F32),
        ("e0", (16, wide), F32),
        ("esum", (3, 16, wide), F32),
        ("egot", (6, 16, wide), F32),
        ("l0", (8, wide), F32),
        ("lsum", (3, 8, wide), F32),
        ("lgot", (6, 8, wide), F32),
        ("d0", (3, 16, 128), F32),
        ("dgot", (6, 16, 128), F32),
    )


class Buffers:
    pass


class Exchange:
    def __init__(self, send_sems, recv_sems):
        self.send_sems, self.recv_sems = send_sems, recv_sems
        self.used = 0
        d, h, t = lax.axis_index("dp"), lax.axis_index("heads"), lax.axis_index("tensor")
        x, c = h // 2, h % 2
        self.d, self.x, self.c, self.t = d, x, c, t
        self.zh, self.zl = d // 2, d % 2
        self.zs = (d, (d + 2) % 4, 2 * self.zh + 1 - self.zl, 2 * (1 - self.zh) + 1 - self.zl)
        self.plane = ((1 - x, t), (x, 1 - t), (1 - x, 1 - t))
        self.along = [self.at(z, x, c, t) for z in self.zs[1:]]
        self.across = [self.at(d, px, c, pt) for px, pt in self.plane]
        self.mate = self.at(d, x, 1 - c, t)
        self.other_y = self.across[1]

    @staticmethod
    def at(d, x, c, t):
        return (d, 2 * x + c, t)

    def group(self, g):
        return 2 * self.zh + (self.zl + g // 2) % 2, (self.x + g) % 2

    def expert(self, g):
        z, x = self.group(g)
        return 2 * (z % 2) + x

    def holder(self, g):
        z, x = self.group(g)
        return self.at(z, x, self.c, self.t)

    def shard(self, j):
        return 2 * ((self.x + 1 + j) % 2) + (self.c + 1 + j // 2) % 2

    def slots(self, count):
        self.used += count
        return self.used - count

    def send(self, slot, src, dst, peer, lands=None):
        pltpu.make_async_remote_copy(
            src_ref=src,
            dst_ref=dst,
            send_sem=self.send_sems.at[slot],
            recv_sem=self.recv_sems.at[slot if lands is None else lands],
            device_id=peer,
            device_id_type=MESH,
        ).start()

    def sent(self, slot, ref):
        pltpu.make_async_copy(ref, ref, self.send_sems.at[slot]).wait()

    def arrived(self, slot, ref):
        pltpu.make_async_copy(ref, ref, self.recv_sems.at[slot]).wait()

    def meet(self):
        barrier = pltpu.get_barrier_semaphore()
        peers = self.along + self.across + [self.mate]
        peers += [self.at(z, 1 - self.x, self.c, self.t) for z in self.zs[1:]]
        for peer in peers:
            pl.semaphore_signal(barrier, inc=1, device_id=peer, device_id_type=MESH)
        pl.semaphore_wait(barrier, len(peers))


class SumOverAll:
    def __init__(self, ex, own, sums, got, z_first=False):
        self.ex, self.own, self.sums, self.got = ex, own, sums, got
        self.slot = ex.slots(6)
        near, far = [[ex.mate], ex.across], [[ex.along[0]], [ex.along[1]]]
        self.stages = far + near[::-1] if z_first else near + far
        self.at, self.base = 0, 0

    def received(self):
        stage = self.stages[self.at - 1]
        for j in range(len(stage)):
            self.ex.arrived(self.slot + self.base + j, self.got.at[self.base + j])
        before = self.own[...] if self.at == 1 else self.sums[self.at - 2]
        parts = [before] + [self.got[self.base + j] for j in range(len(stage))]
        self.base += len(stage)
        if len(parts) == 2:
            return parts[0].astype(F32) + parts[1].astype(F32)
        return (parts[0].astype(F32) + parts[3].astype(F32)) + (parts[1].astype(F32) + parts[2].astype(F32))

    def advance(self):
        source = self.own
        if self.at:
            self.sums[self.at - 1] = self.received().astype(self.sums.dtype)
            source = self.sums.at[self.at - 1]
        for j, peer in enumerate(self.stages[self.at]):
            self.ex.send(self.slot + self.base + j, source, self.got.at[self.base + j], peer)
        self.at += 1

    def result(self):
        return self.received()

    def done(self):
        for k in range(6):
            self.ex.sent(self.slot + k, self.got.at[k])


def bias_lanes(ex):
    chunk, lane = lanes((1, 640)) // HEAD_DIM, lanes((1, 640)) % HEAD_DIM
    kind = jnp.where(
        (chunk < 2) | (chunk == 4), 0, jnp.where((chunk == 5) | (chunk == 8) | (chunk == 9), 1, 2)
    )
    head = jnp.where((chunk == 1) | (chunk == 9), 1, jnp.where((chunk == 4) | (chunk == 5), 2, 0))
    wanted = 24 * (2 * ex.d + ex.t) + rows_of((24, 640))
    heads = ((HEAD_DIM * head + lane == wanted) & (kind < 2)).astype(F32).astype(BF16)
    return heads, kind


def hidden_lanes(ex, units):
    wanted = 96 * (4 * ex.d + 2 * ex.x + ex.c) + rows_of((96, units))
    return (lanes((96, units)) == wanted).astype(F32).astype(BF16)


def pack(b, ex, inputs):
    heads, merge, w_in, w_out = inputs
    q, k, v = heads[0], heads[1], heads[2]
    m = merge[...].T
    b.a[:, 0:128] = q[:, 0:128]
    b.a[:, 128:256] = k[:, 0:128]
    b.a[:, 256:384] = jnp.concatenate([q[:, 128:192], v[:, 128:192]], axis=1)
    b.a[:, 384:512] = jnp.concatenate([k[:, 128:192], m[:, 128:192]], axis=1)
    b.a[:, 512:640] = v[:, 0:128]
    b.a[:, 640:768] = m[:, 0:128]
    b.wp[:, 0] = w_in[...]
    b.wp[:, 1] = w_out[...]
    me = 2 * ex.x + ex.c
    b.g[3, ex.d, ex.t] = b.a[...]
    b.w[4 * ex.d + me] = b.wp[ex.expert(0)]


def small_operands(b, ex, ids_ref, head_bias_ref, in_bias_ref):
    named = rows_of((4, SEQ))
    ids = ids_ref[...]
    b.wide8[...] = jnp.zeros_like(b.wide8)
    b.wide8[0:4, 0:SEQ] = ((ids[0:1] == named) | (ids[1:2] == named)).astype(F32)
    b.spread[...] = b.wide8[0:8]
    b.chosen[...] = b.wide8[...].T
    heads, kind = bias_lanes(ex)
    row = nn(head_bias_ref[...], heads)
    row = jnp.where(kind == 0, row[0:1], jnp.where(kind == 1, row[1:2], 0.0))
    me = 2 * ex.x + ex.c
    hidden = nn(in_bias_ref[...], hidden_lanes(ex, b.p0.shape[1]))
    b.p0[...] = jnp.zeros_like(b.p0)
    b.p0[0:4] = jnp.where(ex.t == 0, hidden, 0.0).astype(BF16)
    b.p0[4:8] = jnp.where(ex.t == 1, hidden, 0.0).astype(BF16)
    b.p0[8:12, 0:640] = jnp.where(rows_of((4, 1)) == me, row, 0.0).astype(BF16)
    counts = jnp.sum(b.chosen[...], axis=0, keepdims=True)
    high = jnp.floor(counts / 64)
    middle = jnp.floor((counts - 64 * high) / 8)
    digits = jnp.concatenate([counts - 64 * high - 8 * middle, middle, high], axis=0)
    b.p0[12:15, 0:128] = digits.astype(BF16)


def prepare(b, ex, x_ref, cot_ref, noise_ref, router_ref, eb_ref, vector_refs):
    rows = b.xs.shape[0]
    for ref, source in ((b.xs, x_ref), (b.cot, cot_ref)):
        ref[rows - 16 : rows] = jnp.zeros((16, ref.shape[1]), BF16)
        ref[0:SEQ] = source[...]
    for i, ref in enumerate(vector_refs):
        b.vec[i : i + 1] = ref[...].astype(F32).reshape(1, -1)
    b.wide8[...] = jnp.full(b.wide8.shape, -1e30, F32)
    b.wide8[0:4, 0:SEQ] = noise_ref[...]
    b.noise[...] = b.wide8[...].T
    for ref, source in ((b.router, router_ref), (b.eb, eb_ref)):
        ref[...] = jnp.zeros_like(ref)
        ref[0:4] = source[...]
    values = b.xs[...].astype(F32)
    normal, _ = normalise(values)
    b.n1[...] = (normal * b.vec[0:1] + b.vec[1:2]).astype(BF16)
    b.res[...] = values + b.vec[4:5]
    earlier = (rows_of((rows, rows)) < lanes((rows, rows))).astype(F32).astype(BF16)
    b.before[...] = nn(b.spread[...].astype(BF16), earlier)

    def one(g, carry):
        e = ex.expert(g)
        slot = rows_of((CAP, rows)).astype(F32)
        served = (row_of(b.before[...], e) == slot) & (row_of(b.spread[...], e) > 0.5)
        b.sel[g] = jnp.where(served, 1.0, 0.0).astype(BF16)
        b.cs[g] = nn(b.sel[g], b.cot[...]).astype(BF16)
        return carry

    lax.fori_loop(0, 4, one, 0)


def attend(b, ex, h):
    rows, wide = b.n1.shape
    low, high = halves()
    alive = lanes((1, rows)) < SEQ
    weight = b.g[h].reshape(wide, wide)
    b.qkv[h] = (nn(b.n1[...], weight[:, 0:640]) + row_of(b.bias[:, 0:640], 8 + ex.shard(h))).astype(BF16)
    parts = []
    ends = jnp.zeros((rows, 128), F32)
    for i, (sq, sk, sv, uq, uv) in enumerate(HEADS_AT):
        query = b.qkv[h, :, 128 * sq : 128 * sq + 128] * (high if uq else low)
        key = b.qkv[h, :, 128 * sk : 128 * sk + 128]
        value = b.qkv[h, :, 128 * sv : 128 * sv + 128] * (high if uv else low)
        scores = jnp.where(alive, SCALE * nt(query, key), -1e30)
        top = jnp.max(scores, axis=-1, keepdims=True)
        raised = jnp.exp(scores - top)
        total = jnp.sum(raised, axis=-1, keepdims=True)
        parts.append(nn((raised / total).astype(BF16), value))
        ends = jnp.where(lanes((1, 128)) == i, top + jnp.log(total), ends)
    b.lse[h] = ends
    first, second = (parts[0] + parts[1]).astype(BF16), parts[2].astype(BF16)
    b.att[h, :, 0:128] = first
    b.att[h, :, 128:256] = second
    b.res[...] += nt(first, weight[:, 640:768]) + nt(second, weight[:, 384:512])


def attend_back(b, ex, h):
    rows, wide = b.n1.shape
    low, high = halves()
    alive = lanes((1, rows)) < SEQ
    weight = b.g[h].reshape(wide, wide)
    branch = b.ig[...].astype(BF16)
    from_first = nn(branch, weight[:, 640:768]).astype(BF16)
    from_second = nn(branch, weight[:, 384:512]).astype(BF16)
    ends = b.lse[h]
    slabs = [None] * 5
    for i, (sq, sk, sv, uq, uv) in enumerate(HEADS_AT):
        mask_q, mask_v = (high if uq else low), (high if uv else low)
        query = b.qkv[h, :, 128 * sq : 128 * sq + 128] * mask_q
        key = b.qkv[h, :, 128 * sk : 128 * sk + 128]
        value = b.qkv[h, :, 128 * sv : 128 * sv + 128]
        grad = (from_first if i < 2 else from_second) * mask_v
        scores = SCALE * nt(query, key)
        weights = jnp.where(alive, jnp.exp(jnp.where(alive, scores - ends[:, i : i + 1], 0.0)), 0.0)
        value_grad = tn(weights.astype(BF16), grad)
        weight_grad = nt(grad, value)
        inner = jnp.sum(weight_grad * weights, axis=-1, keepdims=True)
        score = (weights * (weight_grad - inner)).astype(BF16)
        query_grad = SCALE * nn(score, key * mask_q)
        key_grad = SCALE * tn(score, query)
        for at, part in ((sq, query_grad), (sk, key_grad), (sv, value_grad)):
            slabs[at] = part if slabs[at] is None else slabs[at] + part
    for at, slab in enumerate(slabs):
        low_slab = slab.astype(BF16)
        b.dqkv[:, 128 * at : 128 * at + 128] = low_slab
        b.l0[:, 128 * at : 128 * at + 128] = jnp.where(
            rows_of((8, 1)) == 4 + ex.shard(h),
            jnp.sum(low_slab.astype(F32), axis=0, keepdims=True),
            b.l0[:, 128 * at : 128 * at + 128],
        )
    b.dn1[...] += nt(b.dqkv[...], weight[:, 0:640])
    put = pl.ds(pl.multiple_of(wide * h, wide), wide)
    for at in range(6):
        if at < 5:
            part = nn(b.n1t[...], b.dqkv[:, 128 * at : 128 * at + 128])
            if at == 3:
                part += nn(b.brt[...], b.att[h, :, 128:256])
        else:
            part = nn(b.brt[...], b.att[h, :, 0:128])
        b.hp[put, 128 * at : 128 * at + 128] = part.astype(BF16)


def route(b, ex):
    normal, _ = normalise(b.res[...])
    b.n2[...] = (normal * b.vec[2:3] + b.vec[3:4]).astype(BF16)
    logits = nt(b.n2[...], b.router[...]) + b.noise[...]
    raised = jnp.exp(logits - jnp.max(logits, axis=-1, keepdims=True))
    chances = raised / jnp.sum(raised, axis=-1, keepdims=True)
    b.ch[...] = chances
    for i, part in enumerate(exact_parts(chances)):
        b.chp[i] = part

    def one(g, carry):
        b.cs[g] = nn(b.sel[g], b.n2[...]).astype(BF16)
        gates = nn(b.sel[g], b.chp[0]) + nn(b.sel[g], b.chp[1]) + nn(b.sel[g], b.chp[2])
        gates = jnp.sum(jnp.where(lanes((1, 128)) == ex.expert(g), gates, 0.0), axis=-1, keepdims=True)
        b.gs[g] = jnp.broadcast_to(as_row(gates), (8, CAP))
        return carry

    lax.fori_loop(0, 4, one, 0)


def serve(b, ex, g):
    cap, wide = b.rt.shape[2:]
    units = b.w.shape[3]
    step = 2 * cap
    x = b.rt[g].reshape(step, wide)
    raw = b.rc[g].reshape(step, wide).astype(F32)
    gate = jnp.concatenate([as_column(b.rg[g, 0, 0:1]), as_column(b.rg[g, 1, 0:1])], axis=0)
    at = pl.ds(pl.multiple_of(g * step, step), step)
    b.xt[:, at] = x.T
    b.gt[:, at] = (gate * raw).astype(BF16).T
    out = jnp.zeros((step, wide), F32)
    back = jnp.zeros((step, wide), F32)
    for f in range(units // wide):
        cols = slice(f * wide, f * wide + wide)
        r = (gate * raw).astype(BF16)
        w_in = b.w[:, 0, :, cols].reshape(wide, wide)
        w_out = b.w[:, 1, :, cols].reshape(wide, wide)
        v = nn(x, w_in) + b.brow[0:1, cols]
        square = v * v
        bend = jnp.tanh(0.7978845608028654 * v * (1.0 + 0.044715 * square))
        hidden = (0.5 * v * (1.0 + bend)).astype(BF16)
        slope = 0.5 * (1.0 + bend) + 0.5 * v * (1.0 - bend * bend) * (
            0.7978845608028654 * (1.0 + 3 * 0.044715 * square)
        )
        low = (nn(r, w_out) * slope).astype(BF16)
        b.hp[pl.ds(pl.multiple_of(f * 8 * cap + g * step, step), step)] = hidden
        b.hp[pl.ds(pl.multiple_of((2 + f) * 8 * cap + g * step, step), step)] = low
        b.db[0:1, cols] += jnp.sum(low.astype(F32), axis=0, keepdims=True)
        out += nt(hidden, w_out)
        back += nt(low, w_in)
    b.yo[g] = out.astype(BF16).reshape(2, cap, wide)
    b.yx[g] = back.astype(BF16).reshape(2, cap, wide)
    told = jnp.sum(raw * out, axis=-1, keepdims=True)
    b.yg[g, 0] = jnp.broadcast_to(as_row(told[0:cap]), (8, cap))
    b.yg[g, 1] = jnp.broadcast_to(as_row(told[cap:step]), (8, cap))


def weight_grads(b, half):
    rows, slots = b.xt.shape[0] // 2, b.xt.shape[1]

    def one(f, carry):
        cols = pl.ds(pl.multiple_of(f * 256, 256), 256)
        shape = (8, b.w.shape[2], 256)
        take = pl.ds(pl.multiple_of(half * rows, rows), rows)
        put = pl.ds(8 * half, 8)
        within = pl.ds(pl.multiple_of((f % 3) * 256, 256), 256)
        hidden = b.hp[pl.ds(pl.multiple_of((f // 3) * slots, slots), slots), within]
        before = b.hp[pl.ds(pl.multiple_of((2 + f // 3) * slots, slots), slots), within]
        b.w[put, 0, :, cols] = nn(b.xt[take], before).astype(BF16).reshape(shape)
        b.w[put, 1, :, cols] = nn(b.gt[take], hidden).astype(BF16).reshape(shape)
        return carry

    lax.fori_loop(0, b.w.shape[3] // 256, one, 0)


def back_to_branch(b, ex, total_tokens):
    chances, chosen = b.ch[...], b.chosen[...]
    b.told[...] = chosen * nt(b.cot[...], b.eb[...])
    b.dn1[...] = jnp.zeros_like(b.dn1)

    def one(g, carry):
        select = b.sel[g]
        b.dn1[...] += tn(select, b.bx[g])
        gate = jnp.where(lanes((1, 128)) == ex.expert(g), as_column(b.bg[g, 0:1]), 0.0)
        first, second, third = exact_parts(gate)
        b.told[...] += tn(select, first) + tn(select, second) + tn(select, third)
        return carry

    lax.fori_loop(0, 4, one, 0)
    chance_grad = b.told[...] + b.bias[15:16, 0:128] * (4.0 / (2.0 * total_tokens * total_tokens))
    logit_grad = chances * (chance_grad - jnp.sum(chances * chance_grad, axis=-1, keepdims=True))
    living = rows_of((b.n1.shape[0], 1)) < SEQ
    logit_low = jnp.where(living, logit_grad, 0.0).astype(BF16)
    b.e0[...] = jnp.zeros_like(b.e0)
    b.e0[3:4, 0:128] = jnp.sum(jnp.where(living, chances, 0.0), axis=0, keepdims=True)
    b.e0[4:8] = tn(logit_low, b.n2[...])[0:4]
    normal, inverse = normalise(b.res[...])
    dn2 = b.dn1[...] + nn(logit_low, b.router[...])
    b.e0[0:1] = jnp.sum(dn2 * normal, axis=0, keepdims=True)
    b.e0[1:2] = jnp.sum(dn2, axis=0, keepdims=True)
    b.ig[...] = b.cot[...].astype(F32) + norm_back(dn2 * b.vec[2:3], normal, inverse)
    branch = b.ig[...].astype(BF16)
    b.e0[2:3] = jnp.sum(branch.astype(F32), axis=0, keepdims=True)
    for e in range(4):
        gate = (chances * chosen)[:, e : e + 1]
        b.e0[8 + e : 9 + e] = jnp.sum(
            (gate * b.cot[...].astype(F32)).astype(BF16).astype(F32), axis=0, keepdims=True
        )
    b.n1t[...] = b.n1[...].T
    b.brt[...] = branch.T
    b.dn1[...] = jnp.zeros_like(b.dn1)
    b.l0[...] = jnp.zeros_like(b.l0)


def combine(b, ex, out_ref):
    gates = b.ch[...] * b.chosen[...]
    first, second, third = exact_parts(gates)
    b.res[...] += nn(first, b.eb[...]) + nn(second, b.eb[...]) + nn(third, b.eb[...])

    def one(g, carry):
        gates = b.ch[...] * b.chosen[...]
        gate = jnp.sum(jnp.where(lanes((1, 128)) == ex.expert(g), gates, 0.0), axis=-1, keepdims=True)
        b.res[...] += gate * tn(b.sel[g], b.bo[g])
        return carry

    lax.fori_loop(0, 4, one, 0)
    out_ref[...] = b.res[0:SEQ]


def shard_rows(h, z=0, y=0, rows=768):
    return pl.ds(pl.multiple_of(768 * h + 192 * z + 96 * y, 96), rows)


def add_into(ref, *others):
    total = ref[...].astype(F32)
    for other in others:
        total += other[...].astype(F32)
    ref[...] = total.astype(ref.dtype)


def block_kernel(total_tokens, plan, *refs):
    inputs, outputs, (send_sems, recv_sems) = refs[:17], refs[17:26], refs[26:28]
    x_ref, cot_ref, ids_ref, noise_ref, router_ref, eb_ref = inputs[:6]
    out_ref, ig_ref, og_ref, hw_ref, mg_ref, early_ref, late_ref, hb_ref, ib_ref = outputs
    b = Buffers()
    for (name, _, _), ref in zip(plan, refs[28:], strict=True):
        setattr(b, name, ref)
    ex = Exchange(send_sems, recv_sems)
    d, x, c, t = ex.d, ex.x, ex.c, ex.t
    zh, zl = ex.zh, ex.zl
    pack(b, ex, inputs[11:15])
    small_operands(b, ex, ids_ref, inputs[15], inputs[16])
    tiny = SumOverAll(ex, b.p0, b.psum, b.pgot)
    ex.meet()

    fz, fp, fc = ex.slots(3), ex.slots(12), ex.slots(16)

    def slot(r, j, pt):
        return b.g.at[j, ex.zs[r], pt]

    shards = ((2, 0), (3, 1), (2, 0), (3, 1))

    def spread_shard(r):
        here = slot(r, 3, t)
        for j in range(3):
            ex.send(fp + 4 * j + r, here, slot(r, shards[j][0], t), ex.across[j])
        ex.send(fc + 12 + r, here, slot(r, 1, t), ex.mate)

    own = slot(0, 3, t)
    ex.send(fz, own, own, ex.along[0])
    ex.send(fz + 1, own, own, ex.along[1])
    spread_shard(0)
    tiny.advance()

    ez, exx, ec = ex.slots(6), ex.slots(2), ex.slots(8)

    def part(r, px, pc):
        return b.w.at[4 * ex.zs[r] + 2 * px + pc]

    def own_rows(r):
        ex.send(ez + 2 * (r - 1), b.wp.at[2 * (ex.zs[r] % 2) + x], part(0, x, c), ex.along[r - 1])

    prepare(b, ex, x_ref, cot_ref, noise_ref, router_ref, eb_ref, inputs[6:11])
    here = slot(1, 3, t)
    ex.arrived(fz, here)
    ex.send(fz + 2, here, here, ex.along[1])
    own_rows(1)
    own_rows(3)
    spread_shard(1)
    for r in (2, 3):
        ex.arrived(fz + r - 1, slot(r, 3, t))
        spread_shard(r)
    own_rows(2)
    tiny.advance()
    ct, cy = ex.slots(4), ex.slots(4)
    for r in range(4):
        for j, (_, pt) in enumerate(ex.plane):
            here = slot(r, shards[j][0], pt)
            ex.arrived(fp + 4 * j + r, here)
            ex.send(fc + 4 * j + r, here, slot(r, shards[j][1], pt), ex.mate)
        if r == 0:
            ex.send(exx, b.wp.at[2 * zl + 1 - x], part(0, x, c), ex.across[0])
            ex.send(exx + 1, b.wp.at[2 * (1 - zl) + 1 - x], b.xb, ex.across[0])
        if r == 1:
            tiny.advance()
        if r == 2:
            tiny.advance()
            for g in (1, 2, 3):
                ex.send(ct + g, b.cs.at[g], b.rc.at[g, 0], ex.holder(g))
    ex.send(cy, b.cs.at[0], b.rc.at[0, 1], ex.other_y)
    ex.arrived(exx, part(0, 1 - x, c))
    ex.arrived(exx + 1, b.xb)
    for r in (1, 3, 2):
        source = part(0, 1 - x, c) if r == 1 else b.xb
        ex.send(ez + 2 * (r - 1) + 1, source, part(0, 1 - x, c), ex.along[r - 1])
    ex.send(ec + 1, part(0, 1 - x, c), part(0, 1 - x, c), ex.mate)
    ex.send(ec, part(0, x, c), part(0, x, c), ex.mate)
    b.rc[0, 0] = b.cs[0]
    b.bias[...] = tiny.result()
    b.bias[15:16, 0:128] = (
        b.bias[12:13, 0:128] + 8 * b.bias[13:14, 0:128] + 64 * b.bias[14:15, 0:128]
    )
    b.brow[0:1] = row_of(b.bias[...], 4 * t + ex.expert(0))
    for r in range(4):
        for j, (_, pt) in enumerate(ex.plane + ((x, t),)):
            ex.arrived(fc + 4 * j + r, slot(r, shards[j][1], pt))

    def forward_head(h, carry):
        attend(b, ex, h)

        @pl.when(h == 0)
        def _():
            for g in (1, 2, 3):
                ex.arrived(ct + g, b.rc.at[g, 0])
                ex.send(cy + g, b.rc.at[g, 0], b.rc.at[g, 1], ex.other_y)

        return carry

    lax.fori_loop(0, 4, forward_head, 0)
    for g in (1, 2, 3):
        ex.sent(ct + g, b.cs.at[0])
    ex.sent(cy, b.cs.at[0])
    route(b, ex)

    tt, ty, gt, gy = ex.slots(4), ex.slots(4), ex.slots(4), ex.slots(4)
    for g in (1, 2, 3):
        ex.send(tt + g, b.cs.at[g], b.rt.at[g, 0], ex.holder(g))
        ex.send(gt + g, b.gs.at[g], b.rg.at[g, 0], ex.holder(g))
    ex.send(ty, b.cs.at[0], b.rt.at[0, 1], ex.other_y)
    ex.send(gy, b.gs.at[0], b.rg.at[0, 1], ex.other_y)
    b.rt[0, 0] = b.cs[0]
    b.rg[0, 0] = b.gs[0]
    for r in (1, 2, 3):
        here = part(r, x, c)
        ex.arrived(ez + 2 * (r - 1), here)
        ex.send(ec + 2 * r, here, here, ex.mate)
    for g in (1, 2, 3):
        ex.arrived(tt + g, b.rt.at[g, 0])
        ex.send(ty + g, b.rt.at[g, 0], b.rt.at[g, 1], ex.other_y)
        ex.arrived(gt + g, b.rg.at[g, 0])
        ex.send(gy + g, b.rg.at[g, 0], b.rg.at[g, 1], ex.other_y)
    for r in (1, 2, 3):
        here = part(r, 1 - x, c)
        ex.arrived(ez + 2 * (r - 1) + 1, here)
        ex.send(ec + 2 * r + 1, here, here, ex.mate)
    for g in range(4):
        ex.arrived(cy + g, b.rc.at[g, 1])
        ex.arrived(ty + g, b.rt.at[g, 1])
        ex.arrived(gy + g, b.rg.at[g, 1])
    for r in range(4):
        for i, px in enumerate((x, 1 - x)):
            ex.arrived(ec + 2 * r + i, part(r, px, 1 - c))
    b.db[...] = jnp.zeros_like(b.db)

    yx, yg, yo = ex.slots(4), ex.slots(4), ex.slots(4)
    hx, hg, ho = ex.slots(4), ex.slots(4), ex.slots(4)

    def serve_blocks(g, carry):
        serve(b, ex, g)
        ex.send(yx + g, b.yx.at[g, 1], b.gotx.at[g], ex.other_y)
        ex.send(yg + g, b.yg.at[g, 1], b.gotg.at[g], ex.other_y)
        return carry

    lax.fori_loop(0, 4, serve_blocks, 0)

    db = ex.slots(5)
    for i in range(b.db.shape[1] // 128):
        b.d0[0, i : i + 1] = b.db[0:1, 128 * i : 128 * i + 128]
    ex.send(db, b.d0.at[0], b.dgot.at[0], ex.mate)

    def give_back(g, carry):
        ex.arrived(yx + g, b.gotx.at[g])
        ex.arrived(yg + g, b.gotg.at[g])
        add_into(b.yx.at[g, 0], b.gotx.at[g])
        add_into(b.yg.at[g, 0], b.gotg.at[g])

        @pl.when(g > 0)
        def _():
            ex.send(hx + g, b.yx.at[g, 0], b.bx.at[g], ex.holder(g))
            ex.send(hg + g, b.yg.at[g, 0], b.bg.at[g], ex.holder(g))

        return carry

    lax.fori_loop(0, 3, give_back, 0)
    ex.arrived(db, b.dgot.at[0])
    b.d0[1] = b.d0[0] + b.dgot[0]
    ex.send(db + 1, b.d0.at[1], b.dgot.at[1], ex.along[0])
    b.bx[0] = b.yx[0, 0]
    b.bg[0] = b.yg[0, 0]
    for k in range(6):
        ex.sent(ez + k, b.xb)
    ex.sent(exx, b.xb)
    ex.sent(exx + 1, b.xb)
    for k in range(8):
        ex.sent(ec + k, b.xb)

    kc, kz, kr = ex.slots(8), ex.slots(8), ex.slots(8)
    mine = ex.expert(0)

    def rows_at(half, i, pc):
        return 4 * (2 * half + i // 2) + 2 * (i % 2) + pc

    def to_mate(base, half):
        for i in range(4):
            ex.send(kc + base + i, b.w.at[rows_at(half, i, 1 - c)], b.gotc.at[base + i], ex.mate)

    weight_grads(b, 1 - zh)
    to_mate(0, 1 - zh)
    give_back(3, 0)
    for g in range(4):
        ex.send(yo + g, b.yo.at[g, 1], b.goto.at[g], ex.other_y)

    def core_sum(far, i):
        ex.arrived(kc + 4 * (1 - far) + i, b.gotc.at[4 * (1 - far) + i])
        at = rows_at(1 - zh if far else zh, i, c)
        add_into(b.w.at[at], b.gotc.at[4 * (1 - far) + i])
        return b.w.at[at]

    def far_rows(k, carry):
        i = 2 * (k % 2) + jnp.where(k < 2, 1 - x, x)
        rows = core_sum(1, i)

        @pl.when(k < 2)
        def _():
            ex.send(kz + k, rows, b.gotz.at[k], ex.along[0], kr + k)

        @pl.when(k >= 2)
        def _():
            owner = ex.at(2 * (1 - zh) + k % 2, x, c, t)
            ex.send(kz + k, rows, b.gotf.at[ex.zl], owner, kr + 2 + ex.zl)

        return carry

    ex.arrived(db + 1, b.dgot.at[1])
    b.d0[2] = b.d0[1] + b.dgot[1]
    for g in (1, 2, 3):
        ex.send(db + 1 + g, b.d0.at[2], b.dgot.at[1 + g], ex.holder(g))
    lax.fori_loop(0, 4, far_rows, 0)
    weight_grads(b, zh)
    to_mate(4, zh)
    for g in (1, 2, 3):
        ex.arrived(hx + g, b.bx.at[g])
        ex.arrived(hg + g, b.bg.at[g])
    back_to_branch(b, ex, total_tokens)
    sums = SumOverAll(ex, b.e0, b.esum, b.egot)
    sums.advance()

    def near_sum(i, carry):
        core_sum(0, i)
        return carry

    lax.fori_loop(0, 4, near_sum, 0)
    beside = b.w.at[4 * ex.zs[2] + 2 * x + c]
    ex.send(kz + 4, beside, b.gotn.at[mine], ex.along[1], kr + 4 + mine)

    def near_rows():
        for k in range(2):
            ex.arrived(kr + k, b.gotz.at[k])
            at = 4 * (2 * zh + k) + 2 * (1 - x) + c
            add_into(b.w.at[at], b.gotz.at[k])
            ex.send(kz + 5 + k, b.w.at[at], b.gotn.at[mine], ex.at(2 * zh + k, 1 - x, c, t), kr + 4 + mine)

    sm, sp, sz = ex.slots(2), ex.slots(12), ex.slots(3)

    def merge_core(i):
        ex.arrived(sm + i, b.gotm.at[i])

        h = 2 + i
        for r in (3, 2, 1, 0):
            z = ex.zs[r]
            add_into(b.hp.at[shard_rows(h, z, 0, 192)], b.gotm.at[i, shard_rows(0, z, 0, 192)])
            for j in (0, 2) if i == 0 else (1,):
                ex.send(
                    sp + 4 * j + r,
                    b.hp.at[shard_rows(h, z, ex.plane[j][1], 96)],
                    b.gotp.at[j, r],
                    ex.across[j],
                )

    def backward_head(j, carry):
        attend_back(b, ex, j)

        @pl.when(j < 2)
        def _():
            ex.send(sm + j, b.hp.at[shard_rows(j)], b.gotm.at[j], ex.mate)

        @pl.when(j == 1)
        def _():
            def one(g, carry):
                ex.arrived(yo + g, b.goto.at[g])
                add_into(b.yo.at[g, 0], b.goto.at[g])

                @pl.when(g > 0)
                def _():
                    ex.send(ho + g, b.yo.at[g, 0], b.bo.at[g], ex.holder(g))

                return carry

            lax.fori_loop(0, 4, one, 0)
            b.bo[0] = b.yo[0, 0]

        @pl.when(j == 2)
        def _():
            merge_core(0)

        return carry

    lax.fori_loop(0, 4, backward_head, 0)
    merge_core(1)
    near_rows()
    sums.advance()
    first_grad = b.dn1[...]
    normal, inverse = normalise(b.xs[...].astype(F32))
    b.l0[0:1] = jnp.sum(first_grad * normal, axis=0, keepdims=True)
    b.l0[1:2] = jnp.sum(first_grad, axis=0, keepdims=True)
    late = SumOverAll(ex, b.l0, b.lsum, b.lgot)
    late.advance()
    ig_ref[...] = (b.ig[...] + norm_back(first_grad * b.vec[0:1], normal, inverse))[0:SEQ]
    sums.advance()
    late.advance()
    for g in (1, 2, 3):
        ex.arrived(ho + g, b.bo.at[g])
    combine(b, ex, out_ref)
    home = 2 * x + c
    for r in (3, 2, 1, 0):
        for j in range(3):
            ex.arrived(sp + 4 * j + r, b.gotp.at[j, r])
        share = b.hp.at[shard_rows(3, ex.zs[r], t, 96)]
        add_into(share, b.gotp.at[0, r], b.gotp.at[1, r], b.gotp.at[2, r])
        if r >= 2:
            ex.send(sz + r - 2, share, b.gots.at[r - 2], ex.along[1])
    sums.advance()
    late.advance()
    ex.arrived(sz + 1, b.gots.at[1])
    share = b.hp.at[shard_rows(3, ex.zs[1], t, 96)]
    add_into(share, b.gots.at[1])
    ex.send(sz + 2, share, b.gots.at[2], ex.along[0])
    late.advance()

    totals = sums.result()
    early_ref[...] = totals
    load = b.bias[15:16, 0:128] / (2.0 * total_tokens)
    balance = 4.0 * jnp.sum(load * (totals[3:4, 0:128] / total_tokens), axis=-1, keepdims=True)
    early_ref[3:4, 0:128] = jnp.broadcast_to(balance, (1, 128))
    units = b.db.shape[1]
    hidden_rows = jnp.zeros((8, units), F32)
    for g in range(4):
        if g:
            ex.arrived(db + 1 + g, b.dgot.at[1 + g])
        source = b.dgot.at[1 + g] if g else b.d0.at[2]
        line = jnp.concatenate([source[i : i + 1] for i in range(units // 128)], axis=1)
        hidden_rows = jnp.where(rows_of((8, 1)) == ex.expert(g), line, hidden_rows)
    select = hidden_lanes(ex, units)
    ib_ref[...] = sum(nt(part_of, select) for part_of in exact_parts(hidden_rows))[0:4]
    late_sum = late.result()
    late_ref[...] = late_sum
    heads, kind = bias_lanes(ex)
    row = row_of(late_sum, 4 + home)[:, 0:640]
    rows = jnp.concatenate([jnp.where(kind == 0, row, 0.0), jnp.where(kind == 1, row, 0.0)], axis=0)
    hb_ref[...] = sum(nt(part_of, heads) for part_of in exact_parts(rows))
    ex.arrived(sz, b.gots.at[0])
    ex.arrived(sz + 2, b.gots.at[2])
    shard = b.hp[shard_rows(3, d, t, 96)].astype(F32) + b.gots[0].astype(F32) + b.gots[2].astype(F32)
    for k, (whole, lane) in enumerate(((0, 256), (128, 384), (512, 320))):
        hw_ref[k, :, 0:128] = shard[:, whole : whole + 128]
        hw_ref[k, :, 128:192] = shard[:, lane : lane + 64]
    mg_ref[...] = jnp.concatenate([shard[:, 640:768], shard[:, 448:512]], axis=1).T
    b.gotn[mine] = b.w[4 * d + home]
    for k in range(2):
        ex.arrived(kr + 2 + k, b.gotf.at[k])
    for e in range(4):

        @pl.when(e != mine)
        def _():
            ex.arrived(kr + 4 + e, b.gotn.at[e])

        far = jnp.where(x == e % 2, b.gotf[e // 2].astype(F32), 0.0)
        og_ref[e] = (b.gotn[e].astype(F32) + far).astype(BF16)
    for sum_of in (tiny, sums, late):
        sum_of.done()
    for k in range(3):
        ex.sent(fz + k, b.a)
        ex.sent(sz + k, b.a)
    for k in range(12):
        ex.sent(fp + k, b.a)
        ex.sent(sp + k, b.a)
    for k in range(16):
        ex.sent(fc + k, b.a)
    for g in range(4):
        for base in (ty, yx, yo):
            ex.sent(base + g, b.cs.at[0])
        for base in (gy, yg):
            ex.sent(base + g, b.gs.at[0])
    for g in (1, 2, 3):
        for base in (cy, tt, hx, ho):
            ex.sent(base + g, b.cs.at[0])
        for base in (gt, hg):
            ex.sent(base + g, b.gs.at[0])
    for k in range(8):
        ex.sent(kc + k, b.xb)
    for k in range(7):
        ex.sent(kz + k, b.xb)
    for k in range(5):
        ex.sent(db + k, b.dgot.at[0])
    for i in range(2):
        ex.sent(sm + i, b.gotm.at[0])
    assert ex.used <= COPIES


COPIES = 192


def staged_body(
    inputs,
    first_gain,
    first_bias,
    head_weight,
    head_bias,
    merge_weight,
    merge_bias,
    second_gain,
    second_bias,
    router,
    router_noise,
    expert_ids,
    expert_in,
    expert_in_bias,
    expert_out,
    expert_out_bias,
    cotangent,
):
    tok_rows, wide = inputs.shape
    experts, _, units = expert_in.shape
    total_tokens = tok_rows * lax.axis_size(("dp", "heads", "tensor"))
    plan = scratch_plan(wide, units, ROWS)
    output, input_grad, expert_grads, head_grad, merge_grad, early, late, head_bias_grad, in_bias_grad = (
        pl.pallas_call(
            functools.partial(block_kernel, float(total_tokens), plan),
            out_shape=(
                jax.ShapeDtypeStruct((tok_rows, wide), F32),
                jax.ShapeDtypeStruct((tok_rows, wide), F32),
                jax.ShapeDtypeStruct((experts, 2) + expert_in.shape[1:], BF16),
                jax.ShapeDtypeStruct(head_weight.shape, F32),
                jax.ShapeDtypeStruct(merge_weight.shape, F32),
                jax.ShapeDtypeStruct((16, wide), F32),
                jax.ShapeDtypeStruct((8, wide), F32),
                jax.ShapeDtypeStruct(head_bias.shape, F32),
                jax.ShapeDtypeStruct(expert_in_bias.shape, F32),
            ),
            in_specs=[VM] * 17,
            out_specs=(VM,) * 9,
            scratch_shapes=[pltpu.SemaphoreType.DMA((COPIES,))] * 2
            + [pltpu.VMEM(shape, kind) for _, shape, kind in plan],
            compiler_params=pltpu.CompilerParams(
                collective_id=0, has_side_effects=True, vmem_limit_bytes=60 * MIB
            ),
            name="block",
        )(
            inputs,
            cotangent,
            expert_ids.T,
            router_noise.T,
            router.T,
            expert_out_bias,
            first_gain,
            first_bias,
            second_gain,
            second_bias,
            merge_bias,
            head_weight,
            merge_weight,
            expert_in,
            jnp.transpose(expert_out, (0, 2, 1)),
            head_bias,
            expert_in_bias,
        )
    )
    return (
        output,
        early[3, 0],
        input_grad,
        late[0],
        late[1],
        head_grad,
        head_bias_grad,
        merge_grad,
        early[2],
        early[0],
        early[1],
        early[4:8].T,
        expert_grads[:, 0].astype(F32),
        in_bias_grad,
        jnp.transpose(expert_grads[:, 1], (0, 2, 1)).astype(F32),
        early[8:12],
    )


def layer_norm(values, factor, offset):
    average = jnp.mean(values, axis=-1, keepdims=True)
    centred = values - average
    spread = jnp.mean(centred * centred, axis=-1, keepdims=True)
    return centred * lax.rsqrt(spread + 1e-06) * factor + offset


def expert_weights(expert_in, expert_out, expert_in_bias):
    return (
        lax.all_gather(expert_in, ("dp", "heads"), axis=1, tiled=True),
        lax.all_gather(expert_out, ("dp", "heads"), axis=2, tiled=True),
        lax.all_gather(expert_in_bias, ("dp", "heads"), axis=1, tiled=True),
    )


def plain_body(
    inputs,
    first_gain,
    first_bias,
    head_weight,
    head_bias,
    merge_weight,
    merge_bias,
    second_gain,
    second_bias,
    router,
    router_noise,
    expert_ids,
    expert_in,
    expert_in_bias,
    expert_out,
    expert_out_bias,
    cotangent,
):
    tok_rows = inputs.shape[0]
    features = inputs.shape[1]
    experts = expert_in.shape[0]
    head_cols = head_weight.shape[2]
    heads_local = head_cols // HEAD_DIM
    total_tokens = tok_rows * lax.axis_size(("dp", "heads", "tensor"))
    scale = HEAD_DIM ** (-0.5)
    whole_head, whole_merge, whole_bias = (
        lax.all_gather(head_weight, ("dp", "tensor"), axis=1, tiled=True),
        lax.all_gather(merge_weight, ("dp", "tensor"), axis=1, tiled=True),
        lax.all_gather(head_bias, ("dp", "tensor"), axis=1, tiled=True),
    )
    residual_in = inputs.astype(jnp.float32)
    normed, norm_back = jax.vjp(
        layer_norm, residual_in, first_gain.astype(jnp.float32), first_bias.astype(jnp.float32)
    )
    group_rows = lax.all_gather(normed.astype(jnp.bfloat16), "heads", axis=0, tiled=True)
    group_count = group_rows.shape[0]
    group_images = group_count // SEQ
    projected = jnp.einsum(
        "gd,jdc->jgc", group_rows, whole_head, preferred_element_type=jnp.float32
    )
    bias_values = whole_bias.astype(jnp.float32)
    query_low = (projected[0] + bias_values[0]).astype(jnp.bfloat16)
    key_low = projected[1].astype(jnp.bfloat16)
    value_low = (projected[2] + bias_values[1]).astype(jnp.bfloat16)

    def shaped(array):
        return array.reshape(group_images, SEQ, heads_local, HEAD_DIM)

    query_img, key_img, value_img = (shaped(query_low), shaped(key_low), shaped(value_low))
    scores = scale * jnp.einsum(
        "ishd,ithd->ihst", query_img, key_img, preferred_element_type=jnp.float32
    )
    top_score = jnp.max(scores, axis=-1, keepdims=True)
    raised = jnp.exp(scores - top_score)
    row_total = jnp.sum(raised, axis=-1, keepdims=True)
    weights = raised / row_total
    log_total = top_score + jnp.log(row_total)
    attended = jnp.einsum(
        "ihst,ithd->ishd",
        weights.astype(jnp.bfloat16),
        value_img,
        preferred_element_type=jnp.float32,
    )
    attended_low = attended.reshape(group_count, head_cols).astype(jnp.bfloat16)
    segment = attended_low
    branch = lax.psum_scatter(
        jnp.dot(segment, whole_merge, preferred_element_type=jnp.float32).astype(jnp.bfloat16),
        "heads",
        scatter_dimension=0,
        tiled=True,
    ).astype(jnp.float32) + merge_bias.astype(jnp.float32)
    residual = residual_in + branch
    normed_two, norm_two_back = jax.vjp(
        layer_norm, residual, second_gain.astype(jnp.float32), second_bias.astype(jnp.float32)
    )
    second_low = normed_two.astype(jnp.bfloat16)
    router_logits = jnp.dot(second_low, router, preferred_element_type=jnp.float32) + router_noise
    chances = jax.nn.softmax(router_logits, axis=-1)
    expert_range = jnp.arange(experts, dtype=jnp.int32)
    chosen_pair = (expert_ids[:, :, None] == expert_range).astype(jnp.int32)
    chosen = jnp.sum(chosen_pair, axis=1)
    order = jnp.arange(tok_rows, dtype=jnp.int32)
    earlier = (order[None, :] < order[:, None]).astype(jnp.bfloat16)
    before = jnp.dot(
        earlier, chosen.astype(jnp.bfloat16), preferred_element_type=jnp.float32
    ).astype(jnp.int32)
    slot_ids = jnp.take_along_axis(before, expert_ids, axis=1)
    flat_rows = (slot_ids * experts + expert_ids).reshape(-1)
    picks = chosen_pair.astype(jnp.float32)
    count_terms = jnp.sum(chosen.astype(jnp.float32), axis=0)
    chance_terms = jnp.sum(chances, axis=0)
    count_all, chance_all = lax.psum((count_terms, chance_terms), ("dp", "heads", "tensor"))
    load_share = count_all / (2 * total_tokens)
    balance_loss = experts * jnp.sum(load_share * chance_all / total_tokens)
    gate_values = jnp.sum(picks * chances[:, None, :], axis=2)
    doubled = jnp.repeat(second_low, 2, axis=0)
    own_buffer = jnp.zeros((CAP * experts, features), jnp.bfloat16).at[flat_rows].set(doubled)
    pair_buffer = lax.all_gather(
        own_buffer.reshape(CAP, experts, features), "tensor", axis=0, tiled=True
    )
    weight_in, weight_out, bias_in = expert_weights(expert_in, expert_out, expert_in_bias)
    before_act = (
        jnp.einsum("ced,edf->cef", pair_buffer, weight_in, preferred_element_type=jnp.float32)
        + bias_in.astype(jnp.float32)[None, :, :]
    )
    activated, gelu_back = jax.vjp(jax.nn.gelu, before_act)
    activated_low = activated.astype(jnp.bfloat16)
    partial_out = jnp.einsum(
        "cef,efd->ced", activated_low, weight_out, preferred_element_type=jnp.float32
    )
    own_out = (
        lax.psum_scatter(
            partial_out.astype(jnp.bfloat16), "tensor", scatter_dimension=0, tiled=True
        ).astype(jnp.float32)
        + expert_out_bias.astype(jnp.float32)[None, :, :]
    )
    picked = own_out.reshape(CAP * experts, features)[flat_rows].reshape(tok_rows, 2, features)
    output = residual + jnp.sum(gate_values[:, :, None] * picked, axis=1)
    incoming = cotangent.astype(jnp.float32)
    gate_grad = jnp.sum(incoming[:, None, :] * picked, axis=2)
    slot_grad = (
        (gate_values[:, :, None] * incoming[:, None, :])
        .astype(jnp.bfloat16)
        .reshape(tok_rows * 2, features)
    )
    own_slot_grad = (
        jnp.zeros((CAP * experts, features), jnp.bfloat16)
        .at[flat_rows]
        .set(slot_grad)
        .reshape(CAP, experts, features)
    )
    out_bias_grad = jnp.sum(own_slot_grad, axis=0, dtype=jnp.float32)
    pair_grad = lax.all_gather(own_slot_grad, "tensor", axis=0, tiled=True)
    back_in, back_out, unused_bias = expert_weights(expert_in, expert_out, expert_in_bias)
    hidden_grad = jnp.einsum(
        "ced,efd->cef", pair_grad, back_out, preferred_element_type=jnp.float32
    )
    pre_grad = gelu_back(hidden_grad)[0].astype(jnp.bfloat16)
    out_grad_rows = jnp.einsum(
        "cef,ced->def", activated_low, pair_grad, preferred_element_type=jnp.float32
    )
    in_grad_rows = jnp.einsum(
        "ced,cef->def", pair_buffer, pre_grad, preferred_element_type=jnp.float32
    )
    in_bias_rows = jnp.sum(pre_grad, axis=0, dtype=jnp.float32).T
    in_grad_rows, out_grad_rows, in_bias_rows = (
        lax.psum_scatter(in_grad_rows, ("dp", "heads"), scatter_dimension=0, tiled=True),
        lax.psum_scatter(out_grad_rows, ("dp", "heads"), scatter_dimension=0, tiled=True),
        lax.psum_scatter(in_bias_rows, ("dp", "heads"), scatter_dimension=0, tiled=True),
    )
    expert_in_grad = jnp.transpose(in_grad_rows, (1, 0, 2))
    expert_out_grad = jnp.transpose(out_grad_rows, (1, 2, 0))
    in_bias_grad = in_bias_rows.T
    buffer_grad = jnp.einsum("cef,edf->ced", pre_grad, back_in, preferred_element_type=jnp.float32)
    own_buffer_grad = (
        lax.psum_scatter(
            buffer_grad.astype(jnp.bfloat16), "tensor", scatter_dimension=0, tiled=True
        )
        .astype(jnp.float32)
        .reshape(CAP * experts, features)
    )
    second_grad = jnp.sum(own_buffer_grad[flat_rows].reshape(tok_rows, 2, features), axis=1)
    chance_grad = (
        jnp.sum(picks * gate_grad[:, :, None], axis=1) + experts * load_share / total_tokens
    )
    logit_grad = chances * (chance_grad - jnp.sum(chances * chance_grad, axis=-1, keepdims=True))
    logit_low = logit_grad.astype(jnp.bfloat16)
    router_grad = lax.dot_general(
        second_low, logit_low, (((0,), (0,)), ((), ())), preferred_element_type=jnp.float32
    )
    second_grad = second_grad + jnp.dot(logit_low, router.T, preferred_element_type=jnp.float32)
    resid_part, gain_two_grad, bias_two_grad = norm_two_back(second_grad)
    resid_grad = incoming + resid_part
    branch_low = resid_grad.astype(jnp.bfloat16)
    merge_bias_grad = jnp.sum(branch_low, axis=0, dtype=jnp.float32)
    group_grad = lax.all_gather(branch_low, "heads", axis=0, tiled=True)
    merge_rows_grad = lax.dot_general(
        group_grad, attended_low, (((0,), (0,)), ((), ())), preferred_element_type=jnp.float32
    )
    attended_grad = shaped(
        jnp.dot(group_grad, whole_merge.T, preferred_element_type=jnp.float32).astype(jnp.bfloat16)
    )
    weights_again = jnp.exp(
        scale
        * jnp.einsum("ishd,ithd->ihst", query_img, key_img, preferred_element_type=jnp.float32)
        - log_total
    )
    value_grad = jnp.einsum(
        "ihst,ishd->ithd",
        weights_again.astype(jnp.bfloat16),
        attended_grad,
        preferred_element_type=jnp.float32,
    )
    weight_grad = jnp.einsum(
        "ishd,ithd->ihst", attended_grad, value_img, preferred_element_type=jnp.float32
    )
    inner_sum = jnp.sum(weight_grad * weights_again, axis=-1, keepdims=True)
    score_low = (weights_again * (weight_grad - inner_sum)).astype(jnp.bfloat16)
    query_grad = scale * jnp.einsum(
        "ihst,ithd->ishd", score_low, key_img, preferred_element_type=jnp.float32
    )
    key_grad = scale * jnp.einsum(
        "ihst,ishd->ithd", score_low, query_img, preferred_element_type=jnp.float32
    )
    triple_low = jnp.stack(
        [
            query_grad.reshape(group_count, head_cols),
            key_grad.reshape(group_count, head_cols),
            value_grad.reshape(group_count, head_cols),
        ],
        axis=0,
    ).astype(jnp.bfloat16)
    head_rows_grad = jnp.einsum(
        "gd,jgc->djc", group_rows, triple_low, preferred_element_type=jnp.float32
    )
    head_bias_rows = jnp.sum(triple_low[0::2], axis=1, dtype=jnp.float32).T
    segment = triple_low
    first_grad = lax.psum_scatter(
        jnp.einsum("jgc,jdc->gd", segment, whole_head, preferred_element_type=jnp.float32).astype(
            jnp.bfloat16
        ),
        "heads",
        scatter_dimension=0,
        tiled=True,
    ).astype(jnp.float32)
    input_part, gain_one_grad, bias_one_grad = norm_back(first_grad)
    input_grad = resid_grad + input_part
    head_rows_grad, merge_rows_grad, head_bias_rows = (
        lax.psum_scatter(head_rows_grad, ("dp", "tensor"), scatter_dimension=0, tiled=True),
        lax.psum_scatter(merge_rows_grad, ("dp", "tensor"), scatter_dimension=0, tiled=True),
        lax.psum_scatter(head_bias_rows, ("dp", "tensor"), scatter_dimension=0, tiled=True),
    )
    head_weight_grad = jnp.transpose(head_rows_grad, (1, 0, 2))
    merge_grad = merge_rows_grad.T
    head_bias_grad = head_bias_rows.T
    small = lax.psum(
        (
            gain_one_grad,
            bias_one_grad,
            gain_two_grad,
            bias_two_grad,
            merge_bias_grad,
            router_grad,
            out_bias_grad,
        ),
        ("dp", "heads", "tensor"),
    )
    return (
        output,
        balance_loss,
        input_grad,
        small[0],
        small[1],
        head_weight_grad,
        head_bias_grad,
        merge_grad,
        small[4],
        small[2],
        small[3],
        small[5],
        expert_in_grad,
        in_bias_grad,
        expert_out_grad,
        small[6],
    )


def solution(mesh):
    in_specs = (
        P(("dp", "heads", "tensor"), None),
        P(),
        P(),
        P(None, ("dp", "tensor"), "heads"),
        P(None, ("heads", "dp", "tensor")),
        P("heads", ("dp", "tensor")),
        P(),
        P(),
        P(),
        P(),
        P(("dp", "heads", "tensor"), None),
        P(("dp", "heads", "tensor"), None),
        P(None, ("dp", "heads"), "tensor"),
        P(None, ("tensor", "dp", "heads")),
        P(None, "tensor", ("dp", "heads")),
        P(),
        P(("dp", "heads", "tensor"), None),
    )
    out_specs = (
        P(("dp", "heads", "tensor"), None),
        P(),
        P(("dp", "heads", "tensor"), None),
        P(),
        P(),
        P(None, ("dp", "tensor"), "heads"),
        P(None, ("heads", "dp", "tensor")),
        P("heads", ("dp", "tensor")),
        P(),
        P(),
        P(),
        P(),
        P(None, ("dp", "heads"), "tensor"),
        P(None, ("tensor", "dp", "heads")),
        P(None, "tensor", ("dp", "heads")),
        P(),
    )
    sizes = tuple(mesh.shape[name] for name in ("dp", "heads", "tensor"))
    body = staged_body if sizes == (4, 4, 2) else plain_body
    return jax.shard_map(body, mesh=mesh, in_specs=in_specs, out_specs=out_specs, check_vma=False)
```

```python
import functools

import jax
import jax.numpy as jnp
import numpy as np
from jax import lax
from jax.experimental import pallas as pl
from jax.experimental.pallas import tpu as pltpu
from jax.sharding import PartitionSpec as P

HEAD_DIM = 64
SEQ = 197
CAP = 128
ROWS = 208
MIB = 1 << 20
F32 = jnp.float32
BF16 = jnp.bfloat16
MESH = pl.DeviceIdType.MESH
VM = pl.BlockSpec(memory_space=pltpu.VMEM)
SCALE = HEAD_DIM ** (-0.5)
HEADS_AT = ((0, 1, 4, 0, 0), (0, 1, 4, 1, 1), (2, 3, 2, 0, 1))


def nn(a, b):
    return lax.dot_general(a, b, (((1,), (0,)), ((), ())), preferred_element_type=F32)


def nt(a, b):
    return lax.dot_general(a, b, (((1,), (1,)), ((), ())), preferred_element_type=F32)


def tn(a, b):
    return lax.dot_general(a, b, (((0,), (0,)), ((), ())), preferred_element_type=F32)


def exact_parts(values):
    parts = []
    for _ in range(3):
        part = values.astype(BF16)
        parts.append(part)
        values = values - part.astype(F32)
    return parts


def normalise(values):
    average = jnp.mean(values, axis=-1, keepdims=True)
    centred = values - average
    spread = jnp.mean(centred * centred, axis=-1, keepdims=True)
    inverse = lax.rsqrt(spread + 1e-06)
    return centred * inverse, inverse


def norm_back(grad, normal, inverse):
    return inverse * (
        grad
        - jnp.mean(grad, axis=-1, keepdims=True)
        - normal * jnp.mean(grad * normal, axis=-1, keepdims=True)
    )


def lanes(shape):
    return lax.broadcasted_iota(jnp.int32, shape, len(shape) - 1)


def rows_of(shape):
    return lax.broadcasted_iota(jnp.int32, shape, 0)


def halves():
    low = (lanes((1, 128)) < HEAD_DIM).astype(F32)
    return low.astype(BF16), (1 - low).astype(BF16)


def row_of(values, at):
    return jnp.sum(jnp.where(rows_of((values.shape[0], 1)) == at, values, 0.0), axis=0, keepdims=True)


def as_row(column):
    n = column.shape[0]
    return jnp.sum(jnp.where(rows_of((n, n)) == lanes((n, n)), column, 0.0), axis=0, keepdims=True)


def as_column(row):
    n = row.shape[1]
    return jnp.sum(jnp.where(rows_of((n, n)) == lanes((n, n)), row, 0.0), axis=1, keepdims=True)


def scratch_plan(wide, units, rows):
    shard, piece, block = (96, wide), (2, 48, units), (CAP, wide)
    return (
        ("a", shard, BF16),
        ("wp", (4,) + piece, BF16),
        ("g", (4, 4, 2) + shard, BF16),
        ("w", (16,) + piece, BF16),
        ("xb", piece, BF16),
        ("p0", (16, units), BF16),
        ("psum", (3, 16, units), BF16),
        ("pgot", (6, 16, units), BF16),
        ("bias", (16, units), F32),
        ("vec", (8, wide), F32),
        ("brow", (8, units), F32),
        ("eb", (128, wide), BF16),
        ("cs", (4,) + block, BF16),
        ("gs", (4, 8, CAP), F32),
        ("rt", (4, 2) + block, BF16),
        ("rc", (4, 2) + block, BF16),
        ("rg", (4, 2, 8, CAP), F32),
        ("sel", (4, CAP, rows), BF16),
        ("xs", (rows, wide), BF16),
        ("cot", (rows, wide), BF16),
        ("wide8", (128, rows), F32),
        ("chosen", (rows, 128), F32),
        ("spread", (8, rows), F32),
        ("before", (8, rows), F32),
        ("noise", (rows, 128), F32),
        ("router", (128, wide), BF16),
        ("n1", (rows, wide), BF16),
        ("n2", (rows, wide), BF16),
        ("qkv", (4, rows, 640), BF16),
        ("att", (4, rows, 256), BF16),
        ("lse", (4, rows, 128), F32),
        ("res", (rows, wide), F32),
        ("ch", (rows, 128), F32),
        ("chp", (3, rows, 128), BF16),
        ("hp", (4 * 8 * CAP, wide), BF16),
        ("xt", (wide, 8 * CAP), BF16),
        ("gt", (wide, 8 * CAP), BF16),
        ("db", (8, units), F32),
        ("yo", (4, 2) + block, BF16),
        ("yx", (4, 2) + block, BF16),
        ("yg", (4, 2, 8, CAP), F32),
        ("goto", (4,) + block, BF16),
        ("gotx", (4,) + block, BF16),
        ("gotg", (4, 8, CAP), F32),
        ("bo", (4,) + block, BF16),
        ("bx", (4,) + block, BF16),
        ("bg", (4, 8, CAP), F32),
        ("gotc", (8,) + piece, BF16),
        ("gotz", (2,) + piece, BF16),
        ("gotn", (4,) + piece, BF16),
        ("gotf", (2,) + piece, BF16),
        ("gotm", (2, wide, wide), BF16),
        ("gotp", (3, 4) + shard, BF16),
        ("gots", (3,) + shard, BF16),
        ("n1t", (wide, rows), BF16),
        ("brt", (wide, rows), BF16),
        ("dqkv", (rows, 640), BF16),
        ("dn1", (rows, wide), F32),
        ("told", (rows, 128), F32),
        ("ig", (rows, wide), F32),
        ("e0", (16, wide), F32),
        ("esum", (3, 16, wide), F32),
        ("egot", (6, 16, wide), F32),
        ("l0", (8, wide), F32),
        ("lsum", (3, 8, wide), F32),
        ("lgot", (6, 8, wide), F32),
        ("d0", (3, 16, 128), F32),
        ("dgot", (6, 16, 128), F32),
    )


class Buffers:
    pass


class Exchange:
    def __init__(self, send_sems, recv_sems):
        self.send_sems, self.recv_sems = send_sems, recv_sems
        self.used = 0
        d, h, t = lax.axis_index("dp"), lax.axis_index("heads"), lax.axis_index("tensor")
        x, c = h // 2, h % 2
        self.d, self.x, self.c, self.t = d, x, c, t
        self.zh, self.zl = d // 2, d % 2
        self.zs = (d, (d + 2) % 4, 2 * self.zh + 1 - self.zl, 2 * (1 - self.zh) + 1 - self.zl)
        self.plane = ((1 - x, t), (x, 1 - t), (1 - x, 1 - t))
        self.along = [self.at(z, x, c, t) for z in self.zs[1:]]
        self.across = [self.at(d, px, c, pt) for px, pt in self.plane]
        self.mate = self.at(d, x, 1 - c, t)
        self.other_y = self.across[1]

    @staticmethod
    def at(d, x, c, t):
        return (d, 2 * x + c, t)

    def group(self, g):
        return 2 * self.zh + (self.zl + g // 2) % 2, (self.x + g) % 2

    def expert(self, g):
        z, x = self.group(g)
        return 2 * (z % 2) + x

    def holder(self, g):
        z, x = self.group(g)
        return self.at(z, x, self.c, self.t)

    def shard(self, j):
        return 2 * ((self.x + 1 + j) % 2) + (self.c + 1 + j // 2) % 2

    def slots(self, count):
        self.used += count
        return self.used - count

    def send(self, slot, src, dst, peer, lands=None):
        pltpu.make_async_remote_copy(
            src_ref=src,
            dst_ref=dst,
            send_sem=self.send_sems.at[slot],
            recv_sem=self.recv_sems.at[slot if lands is None else lands],
            device_id=peer,
            device_id_type=MESH,
        ).start()

    def sent(self, slot, ref):
        pltpu.make_async_copy(ref, ref, self.send_sems.at[slot]).wait()

    def arrived(self, slot, ref):
        pltpu.make_async_copy(ref, ref, self.recv_sems.at[slot]).wait()

    def meet(self):
        barrier = pltpu.get_barrier_semaphore()
        peers = self.along + self.across + [self.mate]
        peers += [self.at(z, 1 - self.x, self.c, self.t) for z in self.zs[1:]]
        for peer in peers:
            pl.semaphore_signal(barrier, inc=1, device_id=peer, device_id_type=MESH)
        pl.semaphore_wait(barrier, len(peers))


class SumOverAll:
    def __init__(self, ex, own, sums, got, z_first=False):
        self.ex, self.own, self.sums, self.got = ex, own, sums, got
        self.slot = ex.slots(6)
        near, far = [[ex.mate], ex.across], [[ex.along[0]], [ex.along[1]]]
        self.stages = far + near[::-1] if z_first else near + far
        self.at, self.base = 0, 0

    def received(self):
        stage = self.stages[self.at - 1]
        for j in range(len(stage)):
            self.ex.arrived(self.slot + self.base + j, self.got.at[self.base + j])
        before = self.own[...] if self.at == 1 else self.sums[self.at - 2]
        parts = [before] + [self.got[self.base + j] for j in range(len(stage))]
        self.base += len(stage)
        if len(parts) == 2:
            return parts[0].astype(F32) + parts[1].astype(F32)
        return (parts[0].astype(F32) + parts[3].astype(F32)) + (parts[1].astype(F32) + parts[2].astype(F32))

    def advance(self):
        source = self.own
        if self.at:
            self.sums[self.at - 1] = self.received().astype(self.sums.dtype)
            source = self.sums.at[self.at - 1]
        for j, peer in enumerate(self.stages[self.at]):
            self.ex.send(self.slot + self.base + j, source, self.got.at[self.base + j], peer)
        self.at += 1

    def result(self):
        return self.received()

    def done(self):
        for k in range(6):
            self.ex.sent(self.slot + k, self.got.at[k])


def bias_lanes(ex):
    chunk, lane = lanes((1, 640)) // HEAD_DIM, lanes((1, 640)) % HEAD_DIM
    kind = jnp.where(
        (chunk < 2) | (chunk == 4), 0, jnp.where((chunk == 5) | (chunk == 8) | (chunk == 9), 1, 2)
    )
    head = jnp.where((chunk == 1) | (chunk == 9), 1, jnp.where((chunk == 4) | (chunk == 5), 2, 0))
    wanted = 24 * (2 * ex.d + ex.t) + rows_of((24, 640))
    heads = ((HEAD_DIM * head + lane == wanted) & (kind < 2)).astype(F32).astype(BF16)
    return heads, kind


def hidden_lanes(ex, units):
    wanted = 96 * (4 * ex.d + 2 * ex.x + ex.c) + rows_of((96, units))
    return (lanes((96, units)) == wanted).astype(F32).astype(BF16)


def pack(b, ex, inputs):
    heads, merge, w_in, w_out = inputs
    q, k, v = heads[0], heads[1], heads[2]
    m = merge[...].T
    b.a[:, 0:128] = q[:, 0:128]
    b.a[:, 128:256] = k[:, 0:128]
    b.a[:, 256:384] = jnp.concatenate([q[:, 128:192], v[:, 128:192]], axis=1)
    b.a[:, 384:512] = jnp.concatenate([k[:, 128:192], m[:, 128:192]], axis=1)
    b.a[:, 512:640] = v[:, 0:128]
    b.a[:, 640:768] = m[:, 0:128]
    b.wp[:, 0] = w_in[...]
    b.wp[:, 1] = w_out[...]
    me = 2 * ex.x + ex.c
    b.g[3, ex.d, ex.t] = b.a[...]
    b.w[4 * ex.d + me] = b.wp[ex.expert(0)]


def small_operands(b, ex, ids_ref, head_bias_ref, in_bias_ref):
    named = rows_of((4, SEQ))
    ids = ids_ref[...]
    b.wide8[...] = jnp.zeros_like(b.wide8)
    b.wide8[0:4, 0:SEQ] = ((ids[0:1] == named) | (ids[1:2] == named)).astype(F32)
    b.spread[...] = b.wide8[0:8]
    b.chosen[...] = b.wide8[...].T
    heads, kind = bias_lanes(ex)
    row = nn(head_bias_ref[...], heads)
    row = jnp.where(kind == 0, row[0:1], jnp.where(kind == 1, row[1:2], 0.0))
    me = 2 * ex.x + ex.c
    hidden = nn(in_bias_ref[...], hidden_lanes(ex, b.p0.shape[1]))
    b.p0[...] = jnp.zeros_like(b.p0)
    b.p0[0:4] = jnp.where(ex.t == 0, hidden, 0.0).astype(BF16)
    b.p0[4:8] = jnp.where(ex.t == 1, hidden, 0.0).astype(BF16)
    b.p0[8:12, 0:640] = jnp.where(rows_of((4, 1)) == me, row, 0.0).astype(BF16)
    counts = jnp.sum(b.chosen[...], axis=0, keepdims=True)
    high = jnp.floor(counts / 64)
    middle = jnp.floor((counts - 64 * high) / 8)
    digits = jnp.concatenate([counts - 64 * high - 8 * middle, middle, high], axis=0)
    b.p0[12:15, 0:128] = digits.astype(BF16)


def prepare(b, ex, x_ref, cot_ref, noise_ref, router_ref, eb_ref, vector_refs):
    rows = b.xs.shape[0]
    for ref, source in ((b.xs, x_ref), (b.cot, cot_ref)):
        ref[rows - 16 : rows] = jnp.zeros((16, ref.shape[1]), BF16)
        ref[0:SEQ] = source[...]
    for i, ref in enumerate(vector_refs):
        b.vec[i : i + 1] = ref[...].astype(F32).reshape(1, -1)
    b.wide8[...] = jnp.full(b.wide8.shape, -1e30, F32)
    b.wide8[0:4, 0:SEQ] = noise_ref[...]
    b.noise[...] = b.wide8[...].T
    for ref, source in ((b.router, router_ref), (b.eb, eb_ref)):
        ref[...] = jnp.zeros_like(ref)
        ref[0:4] = source[...]
    values = b.xs[...].astype(F32)
    normal, _ = normalise(values)
    b.n1[...] = (normal * b.vec[0:1] + b.vec[1:2]).astype(BF16)
    b.res[...] = values + b.vec[4:5]
    earlier = (rows_of((rows, rows)) < lanes((rows, rows))).astype(F32).astype(BF16)
    b.before[...] = nn(b.spread[...].astype(BF16), earlier)

    def one(g, carry):
        e = ex.expert(g)
        slot = rows_of((CAP, rows)).astype(F32)
        served = (row_of(b.before[...], e) == slot) & (row_of(b.spread[...], e) > 0.5)
        b.sel[g] = jnp.where(served, 1.0, 0.0).astype(BF16)
        b.cs[g] = nn(b.sel[g], b.cot[...]).astype(BF16)
        return carry

    lax.fori_loop(0, 4, one, 0)


def attend(b, ex, h):
    rows, wide = b.n1.shape
    low, high = halves()
    alive = lanes((1, rows)) < SEQ
    weight = b.g[h].reshape(wide, wide)
    b.qkv[h] = (nn(b.n1[...], weight[:, 0:640]) + row_of(b.bias[:, 0:640], 8 + ex.shard(h))).astype(BF16)
    parts = []
    ends = jnp.zeros((rows, 128), F32)
    for i, (sq, sk, sv, uq, uv) in enumerate(HEADS_AT):
        query = b.qkv[h, :, 128 * sq : 128 * sq + 128] * (high if uq else low)
        key = b.qkv[h, :, 128 * sk : 128 * sk + 128]
        value = b.qkv[h, :, 128 * sv : 128 * sv + 128] * (high if uv else low)
        scores = jnp.where(alive, SCALE * nt(query, key), -1e30)
        top = jnp.max(scores, axis=-1, keepdims=True)
        raised = jnp.exp(scores - top)
        total = jnp.sum(raised, axis=-1, keepdims=True)
        parts.append(nn((raised / total).astype(BF16), value))
        ends = jnp.where(lanes((1, 128)) == i, top + jnp.log(total), ends)
    b.lse[h] = ends
    first, second = (parts[0] + parts[1]).astype(BF16), parts[2].astype(BF16)
    b.att[h, :, 0:128] = first
    b.att[h, :, 128:256] = second
    b.res[...] += nt(first, weight[:, 640:768]) + nt(second, weight[:, 384:512])


def attend_back(b, ex, h):
    rows, wide = b.n1.shape
    low, high = halves()
    alive = lanes((1, rows)) < SEQ
    weight = b.g[h].reshape(wide, wide)
    branch = b.ig[...].astype(BF16)
    from_first = nn(branch, weight[:, 640:768]).astype(BF16)
    from_second = nn(branch, weight[:, 384:512]).astype(BF16)
    ends = b.lse[h]
    slabs = [None] * 5
    for i, (sq, sk, sv, uq, uv) in enumerate(HEADS_AT):
        mask_q, mask_v = (high if uq else low), (high if uv else low)
        query = b.qkv[h, :, 128 * sq : 128 * sq + 128] * mask_q
        key = b.qkv[h, :, 128 * sk : 128 * sk + 128]
        value = b.qkv[h, :, 128 * sv : 128 * sv + 128]
        grad = (from_first if i < 2 else from_second) * mask_v
        scores = SCALE * nt(query, key)
        weights = jnp.where(alive, jnp.exp(jnp.where(alive, scores - ends[:, i : i + 1], 0.0)), 0.0)
        value_grad = tn(weights.astype(BF16), grad)
        weight_grad = nt(grad, value)
        inner = jnp.sum(weight_grad * weights, axis=-1, keepdims=True)
        score = (weights * (weight_grad - inner)).astype(BF16)
        query_grad = SCALE * nn(score, key * mask_q)
        key_grad = SCALE * tn(score, query)
        for at, part in ((sq, query_grad), (sk, key_grad), (sv, value_grad)):
            slabs[at] = part if slabs[at] is None else slabs[at] + part
    for at, slab in enumerate(slabs):
        low_slab = slab.astype(BF16)
        b.dqkv[:, 128 * at : 128 * at + 128] = low_slab
        b.l0[:, 128 * at : 128 * at + 128] = jnp.where(
            rows_of((8, 1)) == 4 + ex.shard(h),
            jnp.sum(low_slab.astype(F32), axis=0, keepdims=True),
            b.l0[:, 128 * at : 128 * at + 128],
        )
    b.dn1[...] += nt(b.dqkv[...], weight[:, 0:640])
    put = pl.ds(pl.multiple_of(wide * h, wide), wide)
    for at in range(6):
        if at < 5:
            part = nn(b.n1t[...], b.dqkv[:, 128 * at : 128 * at + 128])
            if at == 3:
                part += nn(b.brt[...], b.att[h, :, 128:256])
        else:
            part = nn(b.brt[...], b.att[h, :, 0:128])
        b.hp[put, 128 * at : 128 * at + 128] = part.astype(BF16)


def route(b, ex):
    normal, _ = normalise(b.res[...])
    b.n2[...] = (normal * b.vec[2:3] + b.vec[3:4]).astype(BF16)
    logits = nt(b.n2[...], b.router[...]) + b.noise[...]
    raised = jnp.exp(logits - jnp.max(logits, axis=-1, keepdims=True))
    chances = raised / jnp.sum(raised, axis=-1, keepdims=True)
    b.ch[...] = chances
    for i, part in enumerate(exact_parts(chances)):
        b.chp[i] = part

    def one(g, carry):
        b.cs[g] = nn(b.sel[g], b.n2[...]).astype(BF16)
        gates = nn(b.sel[g], b.chp[0]) + nn(b.sel[g], b.chp[1]) + nn(b.sel[g], b.chp[2])
        gates = jnp.sum(jnp.where(lanes((1, 128)) == ex.expert(g), gates, 0.0), axis=-1, keepdims=True)
        b.gs[g] = jnp.broadcast_to(as_row(gates), (8, CAP))
        return carry

    lax.fori_loop(0, 4, one, 0)


def serve(b, ex, g):
    cap, wide = b.rt.shape[2:]
    units = b.w.shape[3]
    step = 2 * cap
    x = b.rt[g].reshape(step, wide)
    raw = b.rc[g].reshape(step, wide).astype(F32)
    gate = jnp.concatenate([as_column(b.rg[g, 0, 0:1]), as_column(b.rg[g, 1, 0:1])], axis=0)
    at = pl.ds(pl.multiple_of(g * step, step), step)
    b.xt[:, at] = x.T
    b.gt[:, at] = (gate * raw).astype(BF16).T
    out = jnp.zeros((step, wide), F32)
    back = jnp.zeros((step, wide), F32)
    for f in range(units // wide):
        cols = slice(f * wide, f * wide + wide)
        r = (gate * raw).astype(BF16)
        w_in = b.w[:, 0, :, cols].reshape(wide, wide)
        w_out = b.w[:, 1, :, cols].reshape(wide, wide)
        v = nn(x, w_in) + b.brow[0:1, cols]
        square = v * v
        bend = jnp.tanh(0.7978845608028654 * v * (1.0 + 0.044715 * square))
        hidden = (0.5 * v * (1.0 + bend)).astype(BF16)
        slope = 0.5 * (1.0 + bend) + 0.5 * v * (1.0 - bend * bend) * (
            0.7978845608028654 * (1.0 + 3 * 0.044715 * square)
        )
        low = (nn(r, w_out) * slope).astype(BF16)
        b.hp[pl.ds(pl.multiple_of(f * 8 * cap + g * step, step), step)] = hidden
        b.hp[pl.ds(pl.multiple_of((2 + f) * 8 * cap + g * step, step), step)] = low
        b.db[0:1, cols] += jnp.sum(low.astype(F32), axis=0, keepdims=True)
        out += nt(hidden, w_out)
        back += nt(low, w_in)
    b.yo[g] = out.astype(BF16).reshape(2, cap, wide)
    b.yx[g] = back.astype(BF16).reshape(2, cap, wide)
    told = jnp.sum(raw * out, axis=-1, keepdims=True)
    b.yg[g, 0] = jnp.broadcast_to(as_row(told[0:cap]), (8, cap))
    b.yg[g, 1] = jnp.broadcast_to(as_row(told[cap:step]), (8, cap))


def weight_grads(b, half):
    rows, slots = b.xt.shape[0] // 2, b.xt.shape[1]

    def one(f, carry):
        cols = pl.ds(pl.multiple_of(f * 256, 256), 256)
        shape = (8, b.w.shape[2], 256)
        take = pl.ds(pl.multiple_of(half * rows, rows), rows)
        put = pl.ds(8 * half, 8)
        within = pl.ds(pl.multiple_of((f % 3) * 256, 256), 256)
        hidden = b.hp[pl.ds(pl.multiple_of((f // 3) * slots, slots), slots), within]
        before = b.hp[pl.ds(pl.multiple_of((2 + f // 3) * slots, slots), slots), within]
        b.w[put, 0, :, cols] = nn(b.xt[take], before).astype(BF16).reshape(shape)
        b.w[put, 1, :, cols] = nn(b.gt[take], hidden).astype(BF16).reshape(shape)
        return carry

    lax.fori_loop(0, b.w.shape[3] // 256, one, 0)


def back_to_branch(b, ex, total_tokens):
    chances, chosen = b.ch[...], b.chosen[...]
    b.told[...] = chosen * nt(b.cot[...], b.eb[...])
    b.dn1[...] = jnp.zeros_like(b.dn1)

    def one(g, carry):
        select = b.sel[g]
        b.dn1[...] += tn(select, b.bx[g])
        gate = jnp.where(lanes((1, 128)) == ex.expert(g), as_column(b.bg[g, 0:1]), 0.0)
        first, second, third = exact_parts(gate)
        b.told[...] += tn(select, first) + tn(select, second) + tn(select, third)
        return carry

    lax.fori_loop(0, 4, one, 0)
    chance_grad = b.told[...] + b.bias[15:16, 0:128] * (4.0 / (2.0 * total_tokens * total_tokens))
    logit_grad = chances * (chance_grad - jnp.sum(chances * chance_grad, axis=-1, keepdims=True))
    living = rows_of((b.n1.shape[0], 1)) < SEQ
    logit_low = jnp.where(living, logit_grad, 0.0).astype(BF16)
    b.e0[...] = jnp.zeros_like(b.e0)
    b.e0[3:4, 0:128] = jnp.sum(jnp.where(living, chances, 0.0), axis=0, keepdims=True)
    b.e0[4:8] = tn(logit_low, b.n2[...])[0:4]
    normal, inverse = normalise(b.res[...])
    dn2 = b.dn1[...] + nn(logit_low, b.router[...])
    b.e0[0:1] = jnp.sum(dn2 * normal, axis=0, keepdims=True)
    b.e0[1:2] = jnp.sum(dn2, axis=0, keepdims=True)
    b.ig[...] = b.cot[...].astype(F32) + norm_back(dn2 * b.vec[2:3], normal, inverse)
    branch = b.ig[...].astype(BF16)
    b.e0[2:3] = jnp.sum(branch.astype(F32), axis=0, keepdims=True)
    for e in range(4):
        gate = (chances * chosen)[:, e : e + 1]
        b.e0[8 + e : 9 + e] = jnp.sum(
            (gate * b.cot[...].astype(F32)).astype(BF16).astype(F32), axis=0, keepdims=True
        )
    b.n1t[...] = b.n1[...].T
    b.brt[...] = branch.T
    b.dn1[...] = jnp.zeros_like(b.dn1)
    b.l0[...] = jnp.zeros_like(b.l0)


def combine(b, ex, out_ref):
    gates = b.ch[...] * b.chosen[...]
    first, second, third = exact_parts(gates)
    b.res[...] += nn(first, b.eb[...]) + nn(second, b.eb[...]) + nn(third, b.eb[...])

    def one(g, carry):
        gates = b.ch[...] * b.chosen[...]
        gate = jnp.sum(jnp.where(lanes((1, 128)) == ex.expert(g), gates, 0.0), axis=-1, keepdims=True)
        b.res[...] += gate * tn(b.sel[g], b.bo[g])
        return carry

    lax.fori_loop(0, 4, one, 0)
    out_ref[...] = b.res[0:SEQ]


def shard_rows(h, z=0, y=0, rows=768):
    return pl.ds(pl.multiple_of(768 * h + 192 * z + 96 * y, 96), rows)


def add_into(ref, *others):
    total = ref[...].astype(F32)
    for other in others:
        total += other[...].astype(F32)
    ref[...] = total.astype(ref.dtype)


def block_kernel(total_tokens, plan, *refs):
    inputs, outputs, (send_sems, recv_sems) = refs[:17], refs[17:26], refs[26:28]
    x_ref, cot_ref, ids_ref, noise_ref, router_ref, eb_ref = inputs[:6]
    out_ref, ig_ref, og_ref, hw_ref, mg_ref, early_ref, late_ref, hb_ref, ib_ref = outputs
    b = Buffers()
    for (name, _, _), ref in zip(plan, refs[28:], strict=True):
        setattr(b, name, ref)
    ex = Exchange(send_sems, recv_sems)
    d, x, c, t = ex.d, ex.x, ex.c, ex.t
    zh, zl = ex.zh, ex.zl
    pack(b, ex, inputs[11:15])
    small_operands(b, ex, ids_ref, inputs[15], inputs[16])
    tiny = SumOverAll(ex, b.p0, b.psum, b.pgot)
    ex.meet()

    fz, fp, fc = ex.slots(3), ex.slots(12), ex.slots(16)

    def slot(r, j, pt):
        return b.g.at[j, ex.zs[r], pt]

    shards = ((2, 0), (3, 1), (2, 0), (3, 1))

    def spread_shard(r):
        here = slot(r, 3, t)
        for j in range(3):
            ex.send(fp + 4 * j + r, here, slot(r, shards[j][0], t), ex.across[j])
        ex.send(fc + 12 + r, here, slot(r, 1, t), ex.mate)

    own = slot(0, 3, t)
    ex.send(fz, own, own, ex.along[0])
    ex.send(fz + 1, own, own, ex.along[1])
    spread_shard(0)
    tiny.advance()

    ez, exx, ec = ex.slots(6), ex.slots(2), ex.slots(8)

    def part(r, px, pc):
        return b.w.at[4 * ex.zs[r] + 2 * px + pc]

    def own_rows(r):
        ex.send(ez + 2 * (r - 1), b.wp.at[2 * (ex.zs[r] % 2) + x], part(0, x, c), ex.along[r - 1])

    prepare(b, ex, x_ref, cot_ref, noise_ref, router_ref, eb_ref, inputs[6:11])
    here = slot(1, 3, t)
    ex.arrived(fz, here)
    ex.send(fz + 2, here, here, ex.along[1])
    own_rows(1)
    own_rows(3)
    spread_shard(1)
    for r in (2, 3):
        ex.arrived(fz + r - 1, slot(r, 3, t))
        spread_shard(r)
    own_rows(2)
    tiny.advance()
    ct, cy = ex.slots(4), ex.slots(4)
    for r in range(4):
        for j, (_, pt) in enumerate(ex.plane):
            here = slot(r, shards[j][0], pt)
            ex.arrived(fp + 4 * j + r, here)
            ex.send(fc + 4 * j + r, here, slot(r, shards[j][1], pt), ex.mate)
        if r == 0:
            ex.send(exx, b.wp.at[2 * zl + 1 - x], part(0, x, c), ex.across[0])
            ex.send(exx + 1, b.wp.at[2 * (1 - zl) + 1 - x], b.xb, ex.across[0])
        if r == 1:
            tiny.advance()
        if r == 2:
            tiny.advance()
            for g in (1, 2, 3):
                ex.send(ct + g, b.cs.at[g], b.rc.at[g, 0], ex.holder(g))
    ex.send(cy, b.cs.at[0], b.rc.at[0, 1], ex.other_y)
    ex.arrived(exx, part(0, 1 - x, c))
    ex.arrived(exx + 1, b.xb)
    for r in (1, 3, 2):
        source = part(0, 1 - x, c) if r == 1 else b.xb
        ex.send(ez + 2 * (r - 1) + 1, source, part(0, 1 - x, c), ex.along[r - 1])
    ex.send(ec + 1, part(0, 1 - x, c), part(0, 1 - x, c), ex.mate)
    ex.send(ec, part(0, x, c), part(0, x, c), ex.mate)
    b.rc[0, 0] = b.cs[0]
    b.bias[...] = tiny.result()
    b.bias[15:16, 0:128] = (
        b.bias[12:13, 0:128] + 8 * b.bias[13:14, 0:128] + 64 * b.bias[14:15, 0:128]
    )
    b.brow[0:1] = row_of(b.bias[...], 4 * t + ex.expert(0))
    for r in range(4):
        for j, (_, pt) in enumerate(ex.plane + ((x, t),)):
            ex.arrived(fc + 4 * j + r, slot(r, shards[j][1], pt))

    def forward_head(h, carry):
        attend(b, ex, h)

        @pl.when(h == 0)
        def _():
            for g in (1, 2, 3):
                ex.arrived(ct + g, b.rc.at[g, 0])
                ex.send(cy + g, b.rc.at[g, 0], b.rc.at[g, 1], ex.other_y)

        return carry

    lax.fori_loop(0, 4, forward_head, 0)
    for g in (1, 2, 3):
        ex.sent(ct + g, b.cs.at[0])
    ex.sent(cy, b.cs.at[0])
    route(b, ex)

    tt, ty, gt, gy = ex.slots(4), ex.slots(4), ex.slots(4), ex.slots(4)
    for g in (1, 2, 3):
        ex.send(tt + g, b.cs.at[g], b.rt.at[g, 0], ex.holder(g))
        ex.send(gt + g, b.gs.at[g], b.rg.at[g, 0], ex.holder(g))
    ex.send(ty, b.cs.at[0], b.rt.at[0, 1], ex.other_y)
    ex.send(gy, b.gs.at[0], b.rg.at[0, 1], ex.other_y)
    b.rt[0, 0] = b.cs[0]
    b.rg[0, 0] = b.gs[0]
    for r in (1, 2, 3):
        here = part(r, x, c)
        ex.arrived(ez + 2 * (r - 1), here)
        ex.send(ec + 2 * r, here, here, ex.mate)
    for g in (1, 2, 3):
        ex.arrived(tt + g, b.rt.at[g, 0])
        ex.send(ty + g, b.rt.at[g, 0], b.rt.at[g, 1], ex.other_y)
        ex.arrived(gt + g, b.rg.at[g, 0])
        ex.send(gy + g, b.rg.at[g, 0], b.rg.at[g, 1], ex.other_y)
    for r in (1, 2, 3):
        here = part(r, 1 - x, c)
        ex.arrived(ez + 2 * (r - 1) + 1, here)
        ex.send(ec + 2 * r + 1, here, here, ex.mate)
    for g in range(4):
        ex.arrived(cy + g, b.rc.at[g, 1])
        ex.arrived(ty + g, b.rt.at[g, 1])
        ex.arrived(gy + g, b.rg.at[g, 1])
    for r in range(4):
        for i, px in enumerate((x, 1 - x)):
            ex.arrived(ec + 2 * r + i, part(r, px, 1 - c))
    b.db[...] = jnp.zeros_like(b.db)

    yx, yg, yo = ex.slots(4), ex.slots(4), ex.slots(4)
    hx, hg, ho = ex.slots(4), ex.slots(4), ex.slots(4)

    def serve_blocks(g, carry):
        serve(b, ex, g)
        ex.send(yx + g, b.yx.at[g, 1], b.gotx.at[g], ex.other_y)
        ex.send(yg + g, b.yg.at[g, 1], b.gotg.at[g], ex.other_y)
        return carry

    lax.fori_loop(0, 4, serve_blocks, 0)

    db = ex.slots(5)
    for i in range(b.db.shape[1] // 128):
        b.d0[0, i : i + 1] = b.db[0:1, 128 * i : 128 * i + 128]
    ex.send(db, b.d0.at[0], b.dgot.at[0], ex.mate)

    def give_back(g, carry):
        ex.arrived(yx + g, b.gotx.at[g])
        ex.arrived(yg + g, b.gotg.at[g])
        add_into(b.yx.at[g, 0], b.gotx.at[g])
        add_into(b.yg.at[g, 0], b.gotg.at[g])

        @pl.when(g > 0)
        def _():
            ex.send(hx + g, b.yx.at[g, 0], b.bx.at[g], ex.holder(g))
            ex.send(hg + g, b.yg.at[g, 0], b.bg.at[g], ex.holder(g))

        return carry

    lax.fori_loop(0, 3, give_back, 0)
    ex.arrived(db, b.dgot.at[0])
    b.d0[1] = b.d0[0] + b.dgot[0]
    ex.send(db + 1, b.d0.at[1], b.dgot.at[1], ex.along[0])
    b.bx[0] = b.yx[0, 0]
    b.bg[0] = b.yg[0, 0]
    for k in range(6):
        ex.sent(ez + k, b.xb)
    ex.sent(exx, b.xb)
    ex.sent(exx + 1, b.xb)
    for k in range(8):
        ex.sent(ec + k, b.xb)

    kc, kz, kr = ex.slots(8), ex.slots(8), ex.slots(8)
    mine = ex.expert(0)

    def rows_at(half, i, pc):
        return 4 * (2 * half + i // 2) + 2 * (i % 2) + pc

    def to_mate(base, half):
        for i in range(4):
            ex.send(kc + base + i, b.w.at[rows_at(half, i, 1 - c)], b.gotc.at[base + i], ex.mate)

    weight_grads(b, 1 - zh)
    to_mate(0, 1 - zh)
    give_back(3, 0)
    for g in range(4):
        ex.send(yo + g, b.yo.at[g, 1], b.goto.at[g], ex.other_y)

    def core_sum(far, i):
        ex.arrived(kc + 4 * (1 - far) + i, b.gotc.at[4 * (1 - far) + i])
        at = rows_at(1 - zh if far else zh, i, c)
        add_into(b.w.at[at], b.gotc.at[4 * (1 - far) + i])
        return b.w.at[at]

    def far_rows(k, carry):
        i = 2 * (k % 2) + jnp.where(k < 2, 1 - x, x)
        rows = core_sum(1, i)

        @pl.when(k < 2)
        def _():
            ex.send(kz + k, rows, b.gotz.at[k], ex.along[0], kr + k)

        @pl.when(k >= 2)
        def _():
            owner = ex.at(2 * (1 - zh) + k % 2, x, c, t)
            ex.send(kz + k, rows, b.gotf.at[ex.zl], owner, kr + 2 + ex.zl)

        return carry

    ex.arrived(db + 1, b.dgot.at[1])
    b.d0[2] = b.d0[1] + b.dgot[1]
    for g in (1, 2, 3):
        ex.send(db + 1 + g, b.d0.at[2], b.dgot.at[1 + g], ex.holder(g))
    lax.fori_loop(0, 4, far_rows, 0)
    weight_grads(b, zh)
    to_mate(4, zh)
    for g in (1, 2, 3):
        ex.arrived(hx + g, b.bx.at[g])
        ex.arrived(hg + g, b.bg.at[g])
    back_to_branch(b, ex, total_tokens)
    sums = SumOverAll(ex, b.e0, b.esum, b.egot)
    sums.advance()

    def near_sum(i, carry):
        core_sum(0, i)
        return carry

    lax.fori_loop(0, 4, near_sum, 0)
    beside = b.w.at[4 * ex.zs[2] + 2 * x + c]
    ex.send(kz + 4, beside, b.gotn.at[mine], ex.along[1], kr + 4 + mine)

    def near_rows():
        for k in range(2):
            ex.arrived(kr + k, b.gotz.at[k])
            at = 4 * (2 * zh + k) + 2 * (1 - x) + c
            add_into(b.w.at[at], b.gotz.at[k])
            ex.send(kz + 5 + k, b.w.at[at], b.gotn.at[mine], ex.at(2 * zh + k, 1 - x, c, t), kr + 4 + mine)

    sm, sp, sz = ex.slots(2), ex.slots(12), ex.slots(3)

    def merge_core(i):
        ex.arrived(sm + i, b.gotm.at[i])

        h = 2 + i
        for r in (3, 2, 1, 0):
            z = ex.zs[r]
            add_into(b.hp.at[shard_rows(h, z, 0, 192)], b.gotm.at[i, shard_rows(0, z, 0, 192)])
            for j in (0, 2) if i == 0 else (1,):
                ex.send(
                    sp + 4 * j + r,
                    b.hp.at[shard_rows(h, z, ex.plane[j][1], 96)],
                    b.gotp.at[j, r],
                    ex.across[j],
                )

    def backward_head(j, carry):
        attend_back(b, ex, j)

        @pl.when(j < 2)
        def _():
            ex.send(sm + j, b.hp.at[shard_rows(j)], b.gotm.at[j], ex.mate)

        @pl.when(j == 1)
        def _():
            def one(g, carry):
                ex.arrived(yo + g, b.goto.at[g])
                add_into(b.yo.at[g, 0], b.goto.at[g])

                @pl.when(g > 0)
                def _():
                    ex.send(ho + g, b.yo.at[g, 0], b.bo.at[g], ex.holder(g))

                return carry

            lax.fori_loop(0, 4, one, 0)
            b.bo[0] = b.yo[0, 0]

        @pl.when(j == 2)
        def _():
            merge_core(0)

        return carry

    lax.fori_loop(0, 4, backward_head, 0)
    merge_core(1)
    sums.advance()
    first_grad = b.dn1[...]
    normal, inverse = normalise(b.xs[...].astype(F32))
    b.l0[0:1] = jnp.sum(first_grad * normal, axis=0, keepdims=True)
    b.l0[1:2] = jnp.sum(first_grad, axis=0, keepdims=True)
    late = SumOverAll(ex, b.l0, b.lsum, b.lgot)
    late.advance()
    ig_ref[...] = (b.ig[...] + norm_back(first_grad * b.vec[0:1], normal, inverse))[0:SEQ]
    sums.advance()
    late.advance()
    home = 2 * x + c
    for r in (3, 2, 1, 0):
        for j in range(3):
            ex.arrived(sp + 4 * j + r, b.gotp.at[j, r])
        share = b.hp.at[shard_rows(3, ex.zs[r], t, 96)]
        add_into(share, b.gotp.at[0, r], b.gotp.at[1, r], b.gotp.at[2, r])
        if r >= 2:
            ex.send(sz + r - 2, share, b.gots.at[r - 2], ex.along[1])
    near_rows()
    sums.advance()
    late.advance()
    ex.arrived(sz + 1, b.gots.at[1])
    share = b.hp.at[shard_rows(3, ex.zs[1], t, 96)]
    add_into(share, b.gots.at[1])
    ex.send(sz + 2, share, b.gots.at[2], ex.along[0])
    for g in (1, 2, 3):
        ex.arrived(ho + g, b.bo.at[g])
    combine(b, ex, out_ref)
    late.advance()

    totals = sums.result()
    early_ref[...] = totals
    load = b.bias[15:16, 0:128] / (2.0 * total_tokens)
    balance = 4.0 * jnp.sum(load * (totals[3:4, 0:128] / total_tokens), axis=-1, keepdims=True)
    early_ref[3:4, 0:128] = jnp.broadcast_to(balance, (1, 128))
    units = b.db.shape[1]
    hidden_rows = jnp.zeros((8, units), F32)
    for g in range(4):
        if g:
            ex.arrived(db + 1 + g, b.dgot.at[1 + g])
        source = b.dgot.at[1 + g] if g else b.d0.at[2]
        line = jnp.concatenate([source[i : i + 1] for i in range(units // 128)], axis=1)
        hidden_rows = jnp.where(rows_of((8, 1)) == ex.expert(g), line, hidden_rows)
    select = hidden_lanes(ex, units)
    ib_ref[...] = sum(nt(part_of, select) for part_of in exact_parts(hidden_rows))[0:4]
    late_sum = late.result()
    late_ref[...] = late_sum
    heads, kind = bias_lanes(ex)
    row = row_of(late_sum, 4 + home)[:, 0:640]
    rows = jnp.concatenate([jnp.where(kind == 0, row, 0.0), jnp.where(kind == 1, row, 0.0)], axis=0)
    hb_ref[...] = sum(nt(part_of, heads) for part_of in exact_parts(rows))
    ex.arrived(sz, b.gots.at[0])
    ex.arrived(sz + 2, b.gots.at[2])
    shard = b.hp[shard_rows(3, d, t, 96)].astype(F32) + b.gots[0].astype(F32) + b.gots[2].astype(F32)
    for k, (whole, lane) in enumerate(((0, 256), (128, 384), (512, 320))):
        hw_ref[k, :, 0:128] = shard[:, whole : whole + 128]
        hw_ref[k, :, 128:192] = shard[:, lane : lane + 64]
    mg_ref[...] = jnp.concatenate([shard[:, 640:768], shard[:, 448:512]], axis=1).T
    b.gotn[mine] = b.w[4 * d + home]
    for k in range(2):
        ex.arrived(kr + 2 + k, b.gotf.at[k])
    for e in range(4):

        @pl.when(e != mine)
        def _():
            ex.arrived(kr + 4 + e, b.gotn.at[e])

        far = jnp.where(x == e % 2, b.gotf[e // 2].astype(F32), 0.0)
        og_ref[e] = (b.gotn[e].astype(F32) + far).astype(BF16)
    for sum_of in (tiny, sums, late):
        sum_of.done()
    for k in range(3):
        ex.sent(fz + k, b.a)
        ex.sent(sz + k, b.a)
    for k in range(12):
        ex.sent(fp + k, b.a)
        ex.sent(sp + k, b.a)
    for k in range(16):
        ex.sent(fc + k, b.a)
    for g in range(4):
        for base in (ty, yx, yo):
            ex.sent(base + g, b.cs.at[0])
        for base in (gy, yg):
            ex.sent(base + g, b.gs.at[0])
    for g in (1, 2, 3):
        for base in (cy, tt, hx, ho):
            ex.sent(base + g, b.cs.at[0])
        for base in (gt, hg):
            ex.sent(base + g, b.gs.at[0])
    for k in range(8):
        ex.sent(kc + k, b.xb)
    for k in range(7):
        ex.sent(kz + k, b.xb)
    for k in range(5):
        ex.sent(db + k, b.dgot.at[0])
    for i in range(2):
        ex.sent(sm + i, b.gotm.at[0])
    assert ex.used <= COPIES


COPIES = 192


def staged_body(
    inputs,
    first_gain,
    first_bias,
    head_weight,
    head_bias,
    merge_weight,
    merge_bias,
    second_gain,
    second_bias,
    router,
    router_noise,
    expert_ids,
    expert_in,
    expert_in_bias,
    expert_out,
    expert_out_bias,
    cotangent,
):
    tok_rows, wide = inputs.shape
    experts, _, units = expert_in.shape
    total_tokens = tok_rows * lax.axis_size(("dp", "heads", "tensor"))
    plan = scratch_plan(wide, units, ROWS)
    output, input_grad, expert_grads, head_grad, merge_grad, early, late, head_bias_grad, in_bias_grad = (
        pl.pallas_call(
            functools.partial(block_kernel, float(total_tokens), plan),
            out_shape=(
                jax.ShapeDtypeStruct((tok_rows, wide), F32),
                jax.ShapeDtypeStruct((tok_rows, wide), F32),
                jax.ShapeDtypeStruct((experts, 2) + expert_in.shape[1:], BF16),
                jax.ShapeDtypeStruct(head_weight.shape, F32),
                jax.ShapeDtypeStruct(merge_weight.shape, F32),
                jax.ShapeDtypeStruct((16, wide), F32),
                jax.ShapeDtypeStruct((8, wide), F32),
                jax.ShapeDtypeStruct(head_bias.shape, F32),
                jax.ShapeDtypeStruct(expert_in_bias.shape, F32),
            ),
            in_specs=[VM] * 17,
            out_specs=(VM,) * 9,
            scratch_shapes=[pltpu.SemaphoreType.DMA((COPIES,))] * 2
            + [pltpu.VMEM(shape, kind) for _, shape, kind in plan],
            compiler_params=pltpu.CompilerParams(
                collective_id=0, has_side_effects=True, vmem_limit_bytes=60 * MIB
            ),
            name="block",
        )(
            inputs,
            cotangent,
            expert_ids.T,
            router_noise.T,
            router.T,
            expert_out_bias,
            first_gain,
            first_bias,
            second_gain,
            second_bias,
            merge_bias,
            head_weight,
            merge_weight,
            expert_in,
            jnp.transpose(expert_out, (0, 2, 1)),
            head_bias,
            expert_in_bias,
        )
    )
    return (
        output,
        early[3, 0],
        input_grad,
        late[0],
        late[1],
        head_grad,
        head_bias_grad,
        merge_grad,
        early[2],
        early[0],
        early[1],
        early[4:8].T,
        expert_grads[:, 0].astype(F32),
        in_bias_grad,
        jnp.transpose(expert_grads[:, 1], (0, 2, 1)).astype(F32),
        early[8:12],
    )


def layer_norm(values, factor, offset):
    average = jnp.mean(values, axis=-1, keepdims=True)
    centred = values - average
    spread = jnp.mean(centred * centred, axis=-1, keepdims=True)
    return centred * lax.rsqrt(spread + 1e-06) * factor + offset


def expert_weights(expert_in, expert_out, expert_in_bias):
    return (
        lax.all_gather(expert_in, ("dp", "heads"), axis=1, tiled=True),
        lax.all_gather(expert_out, ("dp", "heads"), axis=2, tiled=True),
        lax.all_gather(expert_in_bias, ("dp", "heads"), axis=1, tiled=True),
    )


def plain_body(
    inputs,
    first_gain,
    first_bias,
    head_weight,
    head_bias,
    merge_weight,
    merge_bias,
    second_gain,
    second_bias,
    router,
    router_noise,
    expert_ids,
    expert_in,
    expert_in_bias,
    expert_out,
    expert_out_bias,
    cotangent,
):
    tok_rows = inputs.shape[0]
    features = inputs.shape[1]
    experts = expert_in.shape[0]
    head_cols = head_weight.shape[2]
    heads_local = head_cols // HEAD_DIM
    total_tokens = tok_rows * lax.axis_size(("dp", "heads", "tensor"))
    scale = HEAD_DIM ** (-0.5)
    whole_head, whole_merge, whole_bias = (
        lax.all_gather(head_weight, ("dp", "tensor"), axis=1, tiled=True),
        lax.all_gather(merge_weight, ("dp", "tensor"), axis=1, tiled=True),
        lax.all_gather(head_bias, ("dp", "tensor"), axis=1, tiled=True),
    )
    residual_in = inputs.astype(jnp.float32)
    normed, norm_back = jax.vjp(
        layer_norm, residual_in, first_gain.astype(jnp.float32), first_bias.astype(jnp.float32)
    )
    group_rows = lax.all_gather(normed.astype(jnp.bfloat16), "heads", axis=0, tiled=True)
    group_count = group_rows.shape[0]
    group_images = group_count // SEQ
    projected = jnp.einsum(
        "gd,jdc->jgc", group_rows, whole_head, preferred_element_type=jnp.float32
    )
    bias_values = whole_bias.astype(jnp.float32)
    query_low = (projected[0] + bias_values[0]).astype(jnp.bfloat16)
    key_low = projected[1].astype(jnp.bfloat16)
    value_low = (projected[2] + bias_values[1]).astype(jnp.bfloat16)

    def shaped(array):
        return array.reshape(group_images, SEQ, heads_local, HEAD_DIM)

    query_img, key_img, value_img = (shaped(query_low), shaped(key_low), shaped(value_low))
    scores = scale * jnp.einsum(
        "ishd,ithd->ihst", query_img, key_img, preferred_element_type=jnp.float32
    )
    top_score = jnp.max(scores, axis=-1, keepdims=True)
    raised = jnp.exp(scores - top_score)
    row_total = jnp.sum(raised, axis=-1, keepdims=True)
    weights = raised / row_total
    log_total = top_score + jnp.log(row_total)
    attended = jnp.einsum(
        "ihst,ithd->ishd",
        weights.astype(jnp.bfloat16),
        value_img,
        preferred_element_type=jnp.float32,
    )
    attended_low = attended.reshape(group_count, head_cols).astype(jnp.bfloat16)
    segment = attended_low
    branch = lax.psum_scatter(
        jnp.dot(segment, whole_merge, preferred_element_type=jnp.float32).astype(jnp.bfloat16),
        "heads",
        scatter_dimension=0,
        tiled=True,
    ).astype(jnp.float32) + merge_bias.astype(jnp.float32)
    residual = residual_in + branch
    normed_two, norm_two_back = jax.vjp(
        layer_norm, residual, second_gain.astype(jnp.float32), second_bias.astype(jnp.float32)
    )
    second_low = normed_two.astype(jnp.bfloat16)
    router_logits = jnp.dot(second_low, router, preferred_element_type=jnp.float32) + router_noise
    chances = jax.nn.softmax(router_logits, axis=-1)
    expert_range = jnp.arange(experts, dtype=jnp.int32)
    chosen_pair = (expert_ids[:, :, None] == expert_range).astype(jnp.int32)
    chosen = jnp.sum(chosen_pair, axis=1)
    order = jnp.arange(tok_rows, dtype=jnp.int32)
    earlier = (order[None, :] < order[:, None]).astype(jnp.bfloat16)
    before = jnp.dot(
        earlier, chosen.astype(jnp.bfloat16), preferred_element_type=jnp.float32
    ).astype(jnp.int32)
    slot_ids = jnp.take_along_axis(before, expert_ids, axis=1)
    flat_rows = (slot_ids * experts + expert_ids).reshape(-1)
    picks = chosen_pair.astype(jnp.float32)
    count_terms = jnp.sum(chosen.astype(jnp.float32), axis=0)
    chance_terms = jnp.sum(chances, axis=0)
    count_all, chance_all = lax.psum((count_terms, chance_terms), ("dp", "heads", "tensor"))
    load_share = count_all / (2 * total_tokens)
    balance_loss = experts * jnp.sum(load_share * chance_all / total_tokens)
    gate_values = jnp.sum(picks * chances[:, None, :], axis=2)
    doubled = jnp.repeat(second_low, 2, axis=0)
    own_buffer = jnp.zeros((CAP * experts, features), jnp.bfloat16).at[flat_rows].set(doubled)
    pair_buffer = lax.all_gather(
        own_buffer.reshape(CAP, experts, features), "tensor", axis=0, tiled=True
    )
    weight_in, weight_out, bias_in = expert_weights(expert_in, expert_out, expert_in_bias)
    before_act = (
        jnp.einsum("ced,edf->cef", pair_buffer, weight_in, preferred_element_type=jnp.float32)
        + bias_in.astype(jnp.float32)[None, :, :]
    )
    activated, gelu_back = jax.vjp(jax.nn.gelu, before_act)
    activated_low = activated.astype(jnp.bfloat16)
    partial_out = jnp.einsum(
        "cef,efd->ced", activated_low, weight_out, preferred_element_type=jnp.float32
    )
    own_out = (
        lax.psum_scatter(
            partial_out.astype(jnp.bfloat16), "tensor", scatter_dimension=0, tiled=True
        ).astype(jnp.float32)
        + expert_out_bias.astype(jnp.float32)[None, :, :]
    )
    picked = own_out.reshape(CAP * experts, features)[flat_rows].reshape(tok_rows, 2, features)
    output = residual + jnp.sum(gate_values[:, :, None] * picked, axis=1)
    incoming = cotangent.astype(jnp.float32)
    gate_grad = jnp.sum(incoming[:, None, :] * picked, axis=2)
    slot_grad = (
        (gate_values[:, :, None] * incoming[:, None, :])
        .astype(jnp.bfloat16)
        .reshape(tok_rows * 2, features)
    )
    own_slot_grad = (
        jnp.zeros((CAP * experts, features), jnp.bfloat16)
        .at[flat_rows]
        .set(slot_grad)
        .reshape(CAP, experts, features)
    )
    out_bias_grad = jnp.sum(own_slot_grad, axis=0, dtype=jnp.float32)
    pair_grad = lax.all_gather(own_slot_grad, "tensor", axis=0, tiled=True)
    back_in, back_out, unused_bias = expert_weights(expert_in, expert_out, expert_in_bias)
    hidden_grad = jnp.einsum(
        "ced,efd->cef", pair_grad, back_out, preferred_element_type=jnp.float32
    )
    pre_grad = gelu_back(hidden_grad)[0].astype(jnp.bfloat16)
    out_grad_rows = jnp.einsum(
        "cef,ced->def", activated_low, pair_grad, preferred_element_type=jnp.float32
    )
    in_grad_rows = jnp.einsum(
        "ced,cef->def", pair_buffer, pre_grad, preferred_element_type=jnp.float32
    )
    in_bias_rows = jnp.sum(pre_grad, axis=0, dtype=jnp.float32).T
    in_grad_rows, out_grad_rows, in_bias_rows = (
        lax.psum_scatter(in_grad_rows, ("dp", "heads"), scatter_dimension=0, tiled=True),
        lax.psum_scatter(out_grad_rows, ("dp", "heads"), scatter_dimension=0, tiled=True),
        lax.psum_scatter(in_bias_rows, ("dp", "heads"), scatter_dimension=0, tiled=True),
    )
    expert_in_grad = jnp.transpose(in_grad_rows, (1, 0, 2))
    expert_out_grad = jnp.transpose(out_grad_rows, (1, 2, 0))
    in_bias_grad = in_bias_rows.T
    buffer_grad = jnp.einsum("cef,edf->ced", pre_grad, back_in, preferred_element_type=jnp.float32)
    own_buffer_grad = (
        lax.psum_scatter(
            buffer_grad.astype(jnp.bfloat16), "tensor", scatter_dimension=0, tiled=True
        )
        .astype(jnp.float32)
        .reshape(CAP * experts, features)
    )
    second_grad = jnp.sum(own_buffer_grad[flat_rows].reshape(tok_rows, 2, features), axis=1)
    chance_grad = (
        jnp.sum(picks * gate_grad[:, :, None], axis=1) + experts * load_share / total_tokens
    )
    logit_grad = chances * (chance_grad - jnp.sum(chances * chance_grad, axis=-1, keepdims=True))
    logit_low = logit_grad.astype(jnp.bfloat16)
    router_grad = lax.dot_general(
        second_low, logit_low, (((0,), (0,)), ((), ())), preferred_element_type=jnp.float32
    )
    second_grad = second_grad + jnp.dot(logit_low, router.T, preferred_element_type=jnp.float32)
    resid_part, gain_two_grad, bias_two_grad = norm_two_back(second_grad)
    resid_grad = incoming + resid_part
    branch_low = resid_grad.astype(jnp.bfloat16)
    merge_bias_grad = jnp.sum(branch_low, axis=0, dtype=jnp.float32)
    group_grad = lax.all_gather(branch_low, "heads", axis=0, tiled=True)
    merge_rows_grad = lax.dot_general(
        group_grad, attended_low, (((0,), (0,)), ((), ())), preferred_element_type=jnp.float32
    )
    attended_grad = shaped(
        jnp.dot(group_grad, whole_merge.T, preferred_element_type=jnp.float32).astype(jnp.bfloat16)
    )
    weights_again = jnp.exp(
        scale
        * jnp.einsum("ishd,ithd->ihst", query_img, key_img, preferred_element_type=jnp.float32)
        - log_total
    )
    value_grad = jnp.einsum(
        "ihst,ishd->ithd",
        weights_again.astype(jnp.bfloat16),
        attended_grad,
        preferred_element_type=jnp.float32,
    )
    weight_grad = jnp.einsum(
        "ishd,ithd->ihst", attended_grad, value_img, preferred_element_type=jnp.float32
    )
    inner_sum = jnp.sum(weight_grad * weights_again, axis=-1, keepdims=True)
    score_low = (weights_again * (weight_grad - inner_sum)).astype(jnp.bfloat16)
    query_grad = scale * jnp.einsum(
        "ihst,ithd->ishd", score_low, key_img, preferred_element_type=jnp.float32
    )
    key_grad = scale * jnp.einsum(
        "ihst,ishd->ithd", score_low, query_img, preferred_element_type=jnp.float32
    )
    triple_low = jnp.stack(
        [
            query_grad.reshape(group_count, head_cols),
            key_grad.reshape(group_count, head_cols),
            value_grad.reshape(group_count, head_cols),
        ],
        axis=0,
    ).astype(jnp.bfloat16)
    head_rows_grad = jnp.einsum(
        "gd,jgc->djc", group_rows, triple_low, preferred_element_type=jnp.float32
    )
    head_bias_rows = jnp.sum(triple_low[0::2], axis=1, dtype=jnp.float32).T
    segment = triple_low
    first_grad = lax.psum_scatter(
        jnp.einsum("jgc,jdc->gd", segment, whole_head, preferred_element_type=jnp.float32).astype(
            jnp.bfloat16
        ),
        "heads",
        scatter_dimension=0,
        tiled=True,
    ).astype(jnp.float32)
    input_part, gain_one_grad, bias_one_grad = norm_back(first_grad)
    input_grad = resid_grad + input_part
    head_rows_grad, merge_rows_grad, head_bias_rows = (
        lax.psum_scatter(head_rows_grad, ("dp", "tensor"), scatter_dimension=0, tiled=True),
        lax.psum_scatter(merge_rows_grad, ("dp", "tensor"), scatter_dimension=0, tiled=True),
        lax.psum_scatter(head_bias_rows, ("dp", "tensor"), scatter_dimension=0, tiled=True),
    )
    head_weight_grad = jnp.transpose(head_rows_grad, (1, 0, 2))
    merge_grad = merge_rows_grad.T
    head_bias_grad = head_bias_rows.T
    small = lax.psum(
        (
            gain_one_grad,
            bias_one_grad,
            gain_two_grad,
            bias_two_grad,
            merge_bias_grad,
            router_grad,
            out_bias_grad,
        ),
        ("dp", "heads", "tensor"),
    )
    return (
        output,
        balance_loss,
        input_grad,
        small[0],
        small[1],
        head_weight_grad,
        head_bias_grad,
        merge_grad,
        small[4],
        small[2],
        small[3],
        small[5],
        expert_in_grad,
        in_bias_grad,
        expert_out_grad,
        small[6],
    )


def solution(mesh):
    in_specs = (
        P(("dp", "heads", "tensor"), None),
        P(),
        P(),
        P(None, ("dp", "tensor"), "heads"),
        P(None, ("heads", "dp", "tensor")),
        P("heads", ("dp", "tensor")),
        P(),
        P(),
        P(),
        P(),
        P(("dp", "heads", "tensor"), None),
        P(("dp", "heads", "tensor"), None),
        P(None, ("dp", "heads"), "tensor"),
        P(None, ("tensor", "dp", "heads")),
        P(None, "tensor", ("dp", "heads")),
        P(),
        P(("dp", "heads", "tensor"), None),
    )
    out_specs = (
        P(("dp", "heads", "tensor"), None),
        P(),
        P(("dp", "heads", "tensor"), None),
        P(),
        P(),
        P(None, ("dp", "tensor"), "heads"),
        P(None, ("heads", "dp", "tensor")),
        P("heads", ("dp", "tensor")),
        P(),
        P(),
        P(),
        P(),
        P(None, ("dp", "heads"), "tensor"),
        P(None, ("tensor", "dp", "heads")),
        P(None, "tensor", ("dp", "heads")),
        P(),
    )
    sizes = tuple(mesh.shape[name] for name in ("dp", "heads", "tensor"))
    body = staged_body if sizes == (4, 4, 2) else plain_body
    return jax.shard_map(body, mesh=mesh, in_specs=in_specs, out_specs=out_specs, check_vma=False)
```
